32 devices in a mesh: gx: 4 (over y, x), gy: 8 (over z, core).
Axes of the slice: x: 2, y: 2, z: 4, core: 2. Of those that a mesh axis runs over, the one named last changes fastest.
Arguments:
- state: float32 [8, 8, 64, 1024], P(None, None, 'gx', 'gy'), may hold values from -3 to 3
- residual: float32 [64], replicated, may hold values from -2.5 to 2.5
- shift_rows: int32 [64], P('gx'), may hold values from 0 to 1023
- shear_offset: int32 [1], replicated, may hold values from 0 to 1023
Outputs:
- evolved: float32 [8, 8, 64, 1024], P(None, None, 'gx', 'gy')
The draws below stay inside these ranges and needn't reach their ends.
Inputs may be any that keep to these rules, and one draw needn't show every extreme that they name: `shift_rows`: each row's whole-cell displacement; it wraps around the 1024 azimuthal cells. `shear_offset`: whole-cell offset of the sheared radial boundary.
All inputs are finite; a program needn't handle non-finite values.
Results may differ from the reference program's by a relative error of at most 0.00002.
Values sent between devices are 32-bit elements; how exact they have to be, the bound alone decides.
A program may use at most 128 MiB of HBM per device.

```python
import jax
import jax.numpy as jnp

NZ = 8
NX = 64
NY = 1024


def plant(result, own_key, least, high):
    spot = [jax.random.randint(jax.random.fold_in(own_key, axis), (), 0, length) for axis, length in enumerate(result.shape)]
    widest = result.shape.index(max(result.shape))
    neighbour = spot[:widest] + [(spot[widest] + 1) % result.shape[widest]] + spot[widest + 1:]
    return result.at[tuple(spot)].set(least).at[tuple(neighbour)].set(high)


def steps_of(key, extent, shards, low, high):
    level, own = 1.0, jax.random.fold_in(key, 6)
    for position, shards_of in shards:
        heights = jnp.exp(jax.random.uniform(jax.random.fold_in(own, position), (shards_of,), jnp.float32, low / len(shards), high / len(shards)))
        level = level * jnp.repeat(heights, extent[position] // shards_of).reshape([-1 if axis == position else 1 for axis in range(len(extent))])
    return level


def noise(rng, extent, spread, reach, cuts=(), held_as=jnp.bfloat16):
    result = spread * jax.random.normal(rng, extent, jnp.float32)
    if cuts:
        result = result * steps_of(rng, extent, cuts, -0.22, 0.18)
    return jnp.clip(result, -reach, reach).astype(held_as)


def setup_inputs(seed: int = 0) -> dict:
    key_of = jax.random.split(jax.random.key(seed), 5)
    return {
        "state": noise(key_of[0], (8, NZ, NX, NY), 0.5, 3.0, ((2, 4), (3, 8)), jnp.float32),
        "residual": jnp.clip(jax.random.uniform(key_of[1], (NX,), jnp.float32, -2.5, 2.5), -2.5, 2.5),
        "shift_rows": plant(jax.random.randint(key_of[2], (NX,), 0, NY), jax.random.fold_in(key_of[2], 1), 0, NY - 1).astype(jnp.int32),
        "shear_offset": jax.random.randint(key_of[3], (1,), 0, NY).astype(jnp.int32),
    }


time_step = 0.2
viscous = 0.1
resist = 0.1
sound_sq = 1.0
rotation = 0.5
shear_rate = 1.5


def ahead(field, dimension):
    return jnp.roll(field, -1, dimension)


def behind(field, dimension):
    return jnp.roll(field, 1, dimension)


def deriv(field, dimension):
    return 0.5 * (ahead(field, dimension) - behind(field, dimension))


def laplace(field):
    total = -6.0 * field
    for dimension in range(3):
        total = total + ahead(field, dimension) + behind(field, dimension)
    return total


def pair_mean(field, first_dim, second_dim):
    back_one = behind(field, first_dim)
    return 0.25 * (field + back_one + behind(field, second_dim) + behind(back_one, second_dim))


def rates(state, residual):
    log_rho, vel_x, vel_y, vel_z, entropy, mag_x, mag_y, mag_z = state
    drift = vel_y + residual[None, :, None]

    def advect(field):
        return vel_x * deriv(field, 1) + drift * deriv(field, 2) + vel_z * deriv(field, 0)

    cell_x = 0.5 * (mag_x + ahead(mag_x, 1))
    cell_y = 0.5 * (mag_y + ahead(mag_y, 2))
    cell_z = 0.5 * (mag_z + ahead(mag_z, 0))
    cur_x = deriv(cell_z, 2) - deriv(cell_y, 0)
    cur_y = deriv(cell_x, 0) - deriv(cell_z, 1)
    cur_z = deriv(cell_y, 1) - deriv(cell_x, 2)
    inverse = jnp.exp(-log_rho)
    force_x = inverse * (cur_y * cell_z - cur_z * cell_y)
    force_y = inverse * (cur_z * cell_x - cur_x * cell_z)
    force_z = inverse * (cur_x * cell_y - cur_y * cell_x)
    rate_rho = -advect(log_rho) - (deriv(vel_x, 1) + deriv(vel_y, 2) + deriv(vel_z, 0)) + viscous * laplace(log_rho)
    rate_vx = -advect(vel_x) - sound_sq * (deriv(log_rho, 1) + deriv(entropy, 1)) + force_x + viscous * laplace(vel_x) + 2.0 * rotation * vel_y
    rate_vy = -advect(vel_y) - sound_sq * (deriv(log_rho, 2) + deriv(entropy, 2)) + force_y + viscous * laplace(vel_y) - (2.0 - shear_rate) * rotation * vel_x
    rate_vz = -advect(vel_z) - sound_sq * (deriv(log_rho, 0) + deriv(entropy, 0)) + force_z + viscous * laplace(vel_z)
    rate_ent = -advect(entropy) + viscous * laplace(entropy) + resist * inverse * (cur_x * cur_x + cur_y * cur_y + cur_z * cur_z)
    emf_z = -(pair_mean(vel_x, 1, 2) * 0.5 * (mag_y + behind(mag_y, 1)) - pair_mean(drift, 1, 2) * 0.5 * (mag_x + behind(mag_x, 2))) + resist * ((mag_y - behind(mag_y, 1)) - (mag_x - behind(mag_x, 2)))
    emf_x = -(pair_mean(drift, 2, 0) * 0.5 * (mag_z + behind(mag_z, 2)) - pair_mean(vel_z, 2, 0) * 0.5 * (mag_y + behind(mag_y, 0))) + resist * ((mag_z - behind(mag_z, 2)) - (mag_y - behind(mag_y, 0)))
    emf_y = -(pair_mean(vel_z, 1, 0) * 0.5 * (mag_x + behind(mag_x, 0)) - pair_mean(vel_x, 1, 0) * 0.5 * (mag_z + behind(mag_z, 1))) + resist * ((mag_x - behind(mag_x, 0)) - (mag_z - behind(mag_z, 1)))
    back_y = behind(mag_x, 2)
    stretch = 0.25 * (mag_x + ahead(mag_x, 1) + back_y + ahead(back_y, 1))
    rate_bx = -(ahead(emf_z, 2) - emf_z) + (ahead(emf_y, 0) - emf_y)
    rate_by = -(ahead(emf_x, 0) - emf_x) + (ahead(emf_z, 1) - emf_z) - shear_rate * rotation * stretch
    rate_bz = -(ahead(emf_y, 1) - emf_y) + (ahead(emf_x, 2) - emf_x)
    return jnp.stack([rate_rho, rate_vx, rate_vy, rate_vz, rate_ent, rate_bx, rate_by, rate_bz])


def crop(field, depth):
    return field[..., depth:-depth, depth:-depth]


def reference(state, residual, shift_rows, shear_offset):
    cells_y = state.shape[3]
    columns = jnp.arange(cells_y, dtype=jnp.int32)
    source = (columns[None, :] - shift_rows[:, None]) % cells_y
    moved = jnp.take_along_axis(state, source[None, None], axis=3)
    offset = shear_offset[0]

    def extend(field):
        lower = jnp.roll(field[:, :, -2:, :], -offset, 3)
        upper = jnp.roll(field[:, :, :2, :], offset, 3)
        wide = jnp.concatenate([lower, field, upper], 2)
        return jnp.concatenate([wide[..., -2:], wide, wide[..., :2]], 3)

    drift_rows = jnp.concatenate([residual[-2:], residual, residual[:2]])
    first = moved + time_step * crop(rates(extend(moved), drift_rows), 2)
    second = first + time_step * crop(rates(extend(first), drift_rows), 2)
    return 0.5 * (moved + second)
```

```python
import functools

import jax
import jax.numpy as jnp
from jax import lax
from jax.experimental import pallas as pl
from jax.experimental.pallas import tpu as pltpu
from jax.sharding import PartitionSpec as P

time_step = 0.2
viscous = 0.1
resist = 0.1
sound_sq = 1.0
rotation = 0.5
shear_rate = 1.5

MESH = pl.DeviceIdType.MESH
DEPTH = 2


class Copies:
    def __init__(self, send, recv):
        self.send, self.recv, self.made = send, recv, []

    def start(self, source, target, device):
        k = len(self.made)
        copy = pltpu.make_async_remote_copy(
            src_ref=source,
            dst_ref=target,
            send_sem=self.send.at[k],
            recv_sem=self.recv.at[k],
            device_id=device,
            device_id_type=MESH,
        )
        copy.start()
        self.made.append(copy)
        return copy


def copy_count(chips):
    return 8 + sum(10 if 2 * s < chips else 6 for s in range(1, chips // 2 + 1)) + 8 * (chips // 2 + 1)


def gather(state_ref, grid_ref, copies, local_sem, groups, radial):
    rows = state_ref.shape[0]
    chips = groups // 2
    half = rows // 2
    gx, gy = lax.axis_index("gx"), lax.axis_index("gy")
    chip, core = gy // 2, gy % 2

    def at_chip(offset):
        return lax.rem(chip + offset + chips, chips) * 2 + core

    right, left = (gx, at_chip(1)), (gx, at_chip(-1))
    twin = (gx, chip * 2 + (1 - core))
    x_next = (lax.rem(gx + 1, radial), gy)
    x_prev = (lax.rem(gx + radial - 1, radial), gy)

    barrier = pltpu.get_barrier_semaphore()
    for other in (right, left, twin, x_next, x_prev):
        pl.semaphore_signal(barrier, inc=1, device_id=other, device_id_type=MESH)
    pl.semaphore_wait(barrier, 5)

    def piece(block, part):
        return grid_ref.at[block, pl.ds(DEPTH + part * half, half)]

    def low_rows(block):
        return grid_ref.at[block, pl.ds(0, DEPTH)]

    def high_rows(block):
        return grid_ref.at[block, pl.ds(DEPTH + rows, DEPTH)]

    def send_rows(block, part, source):
        if part == 0:
            edge = source.at[pl.ds(0, DEPTH)]
            return block, 0, copies.start(edge, high_rows(block), x_prev)
        edge = source.at[pl.ds(half - DEPTH, DEPTH)]
        return block, 1, copies.start(edge, low_rows(block), x_next)

    to_twin = []

    def pass_rows(sent):
        for block, part, copy in sent:
            copy.wait_recv()
            strip = high_rows(block) if part == 0 else low_rows(block)
            to_twin.append(copies.start(strip, strip, twin))

    own = [state_ref.at[pl.ds(0, half)], state_ref.at[pl.ds(half, half)]]
    keep = pltpu.make_async_copy(state_ref, grid_ref.at[gy, pl.ds(DEPTH, rows)], local_sem)

    flights = []
    order = [(0, 0), (1, 1), (0, 1), (1, 0)] if chips > 2 else [(0, 0), (1, 1)]
    for way, part in order:
        flights.append(
            (way, part, copies.start(own[part], piece(gy, part), right if way == 0 else left))
        )
    sent = [send_rows(gy, part, own[part]) for part in (0, 1)]
    for part in (0, 1):
        to_twin.append(copies.start(own[part], piece(gy, part), twin))
    keep.start()
    pass_rows(sent)
    for step in range(1, chips // 2 + 1):
        later, sent = [], []
        for way, part, copy in flights:
            block = at_chip(-step if way == 0 else step)
            copy.wait_recv()
            ref = piece(block, part)
            if 2 * (step + 1) < chips or (2 * (step + 1) == chips and part == way):
                later.append((way, part, copies.start(ref, ref, right if way == 0 else left)))
            to_twin.append(copies.start(ref, ref, twin))
            sent.append(send_rows(block, part, ref))
        pass_rows(sent)
        flights = later
    keep.wait()
    for copy in to_twin:
        copy.wait_recv()
    for copy in copies.made:
        copy.wait_send()


def row_sweep(load, first_row, last_row, drift_of, emit):
    def y_ahead(a):
        return pltpu.roll(a, a.shape[1] - 1, 1)

    def y_behind(a):
        return pltpu.roll(a, 1, 1)

    def z_ahead(a):
        return pltpu.roll(a, a.shape[0] - 1, 0)

    def z_behind(a):
        return pltpu.roll(a, 1, 0)

    def cells(by, bz):
        return 0.5 * (by + y_ahead(by)), 0.5 * (bz + z_ahead(bz))

    def radial_edges(prev, cur, prev_drift, cur_drift):
        sum_x = prev[1] + cur[1]
        sum_w = (prev[2] + prev_drift) + (cur[2] + cur_drift)
        sum_z = prev[3] + cur[3]
        bx, by, bz = cur[5], cur[6], cur[7]
        bx_y, bx_z = y_behind(bx), z_behind(bx)
        emf_z = 0.125 * (
            (sum_w + y_behind(sum_w)) * (bx + bx_y) - (sum_x + y_behind(sum_x)) * (by + prev[6])
        ) + resist * ((by - prev[6]) - (bx - bx_y))
        emf_y = 0.125 * (
            (sum_x + z_behind(sum_x)) * (bz + prev[7]) - (sum_z + z_behind(sum_z)) * (bx + bx_z)
        ) + resist * ((bx - bx_z) - (bz - prev[7]))
        return emf_z, emf_y

    start_prev, start_cur = load(first_row - 1), load(first_row)
    carry = (
        *cells(start_prev[6], start_prev[7]),
        *cells(start_cur[6], start_cur[7]),
        *radial_edges(start_prev, start_cur, drift_of(first_row - 1), drift_of(first_row)),
    )

    def one(row, carry):
        cy_prev, cz_prev, cy, cz, emf_z, emf_y = carry
        prev, cur, nxt = load(row - 1), load(row), load(row + 1)
        drift = drift_of(row)
        log_rho, vx, vy, vz, ent, bx, by, bz = cur
        w = vy + drift
        cy_next, cz_next = cells(nxt[6], nxt[7])
        emf_z_next, emf_y_next = radial_edges(cur, nxt, drift, drift_of(row + 1))

        half_x, half_w, half_z = 0.5 * vx, 0.5 * w, 0.5 * vz
        diffs, advs = [], []
        for f in range(5):
            a = cur[f]
            ya, yb, za, zb = y_ahead(a), y_behind(a), z_ahead(a), z_behind(a)
            dx, dy, dz = nxt[f] - prev[f], ya - yb, za - zb
            lap = ((nxt[f] + prev[f]) + (ya + yb) + (za + zb)) - 6.0 * a
            diffs.append((dx, dy, dz))
            advs.append(viscous * lap - (half_x * dx + half_w * dy + half_z * dz))

        sum_bx = bx + nxt[5]
        cx = 0.5 * sum_bx
        cur_x = 0.5 * ((y_ahead(cz) - y_behind(cz)) - (z_ahead(cy) - z_behind(cy)))
        cur_y = 0.5 * ((z_ahead(cx) - z_behind(cx)) - (cz_next - cz_prev))
        cur_z = 0.5 * ((cy_next - cy_prev) - (y_ahead(cx) - y_behind(cx)))
        inverse = jnp.exp(-log_rho)
        force_x = inverse * (cur_y * cz - cur_z * cy)
        force_y = inverse * (cur_z * cx - cur_x * cz)
        force_z = inverse * (cur_x * cy - cur_y * cx)

        pairs = [diffs[0][d] + diffs[4][d] for d in range(3)]
        rates = [
            advs[0] - 0.5 * (diffs[1][0] + diffs[2][1] + diffs[3][2]),
            advs[1] - (0.5 * sound_sq) * pairs[0] + force_x + (2.0 * rotation) * vy,
            advs[2] - (0.5 * sound_sq) * pairs[1] + force_y - ((2.0 - shear_rate) * rotation) * vx,
            advs[3] - (0.5 * sound_sq) * pairs[2] + force_z,
            advs[4] + resist * inverse * (cur_x * cur_x + cur_y * cur_y + cur_z * cur_z),
        ]

        w_y, z_y = w + y_behind(w), vz + y_behind(vz)
        bz_y, by_z = y_behind(bz), z_behind(by)
        emf_x = 0.125 * (
            (z_y + z_behind(z_y)) * (by + by_z) - (w_y + z_behind(w_y)) * (bz + bz_y)
        ) + resist * ((bz - bz_y) - (by - by_z))
        stretch = 0.25 * (sum_bx + y_behind(sum_bx))
        rates.append((z_ahead(emf_y) - emf_y) - (y_ahead(emf_z) - emf_z))
        rates.append(
            (emf_z_next - emf_z) - (z_ahead(emf_x) - emf_x) - (shear_rate * rotation) * stretch
        )
        rates.append((y_ahead(emf_x) - emf_x) - (emf_y_next - emf_y))
        emit(row, cur, rates)
        return cy, cz, cy_next, cz_next, emf_z_next, emf_y_next

    if last_row - first_row < 3:
        for row in range(first_row, last_row + 1):
            carry = one(row, carry)
        return
    lax.fori_loop(first_row, last_row + 1, one, carry, unroll=2)


def step_kernel(
    groups, radial, state_ref, table_ref, drift_ref, out_ref,
    grid_ref, moved_ref, first_ref, send, recv, local_sem,
):
    rows, fields, _, cols = state_ref.shape
    gather(state_ref, grid_ref, Copies(send, recv), local_sem, groups, radial)

    lane = lax.broadcasted_iota(jnp.int32, state_ref.shape[2:], 1)

    def turn(row, _):
        amount = table_ref[4, row]
        inside = lane < cols - amount
        low_side = lane < cols // 2
        blocks = [table_ref[k, row] for k in range(4)]
        for f in range(fields):
            before, here, after, beyond = [
                pltpu.roll(grid_ref[b, row, f], cols - amount, 1) for b in blocks
            ]
            moved_ref[row, f, :, :cols] = jnp.where(inside, here, after)
            moved_ref[row, f, :, cols:] = jnp.where(
                low_side, jnp.where(inside, after, beyond), jnp.where(inside, before, here)
            )
        return 0

    lax.fori_loop(0, rows + 2 * DEPTH, turn, 0)

    def drift_of(row):
        return drift_ref[row]

    def emit_first(row, cur, rates):
        for f in range(fields):
            first_ref[row, f] = cur[f] + time_step * rates[f]

    def emit_out(row, cur, rates):
        for f in range(fields):
            second = cur[f][:, :cols] + time_step * rates[f][:, :cols]
            out_ref[row - DEPTH, f] = 0.5 * (moved_ref[row, f, :, :cols] + second)

    def load_from(ref):
        return lambda row: [ref[row, f] for f in range(fields)]

    row_sweep(load_from(moved_ref), 1, rows + 2, drift_of, emit_first)
    row_sweep(load_from(first_ref), 2, rows + 1, drift_of, emit_out)


def gathered(state, residual, shift_rows, shear_offset):
    fields, vertical, rows, cols = state.shape
    groups, radial = lax.axis_size("gy"), lax.axis_size("gx")
    gx, gy = lax.axis_index("gx"), lax.axis_index("gy")
    cells_y = cols * groups
    wide = rows + 2 * DEPTH

    up = [(i, (i + 1) % radial) for i in range(radial)]
    down = [(target, source) for source, target in up]
    low = lax.ppermute(shift_rows[-DEPTH:], "gx", up)
    high = lax.ppermute(shift_rows[:DEPTH], "gx", down)
    offset = shear_offset[0]
    low = low - jnp.where(gx == 0, offset, 0)
    high = high + jnp.where(gx == radial - 1, offset, 0)
    amounts = jnp.concatenate([low, shift_rows, high])
    origin = (cols * gy - amounts) % cells_y
    block, part = origin // cols, origin % cols
    table = jnp.stack(
        [(block + groups - 1) % groups, block, (block + 1) % groups, (block + 2) % groups, part]
    )
    padded = jnp.concatenate([residual[-DEPTH:], residual, residual[:DEPTH]])
    drift = lax.dynamic_slice_in_dim(padded, gx * rows, wide)

    count = copy_count(groups // 2)
    out = pl.pallas_call(
        functools.partial(step_kernel, groups, radial),
        out_shape=jax.ShapeDtypeStruct((rows, fields, vertical, cols), jnp.float32),
        in_specs=[
            pl.BlockSpec(memory_space=pltpu.VMEM),
            pl.BlockSpec(memory_space=pltpu.SMEM),
            pl.BlockSpec(memory_space=pltpu.SMEM),
        ],
        out_specs=pl.BlockSpec(memory_space=pltpu.VMEM),
        scratch_shapes=[
            pltpu.VMEM((groups, wide, fields, vertical, cols), jnp.float32),
            pltpu.VMEM((wide, fields, vertical, 2 * cols), jnp.float32),
            pltpu.VMEM((wide, fields, vertical, 2 * cols), jnp.float32),
            pltpu.SemaphoreType.DMA((count,)),
            pltpu.SemaphoreType.DMA((count,)),
            pltpu.SemaphoreType.DMA,
        ],
        compiler_params=pltpu.CompilerParams(collective_id=0, has_side_effects=True),
    )(jnp.transpose(state, (2, 0, 1, 3)), table, drift)
    return jnp.transpose(out, (1, 2, 0, 3))


def spread_kernel(
    groups, radial, state_ref, shift_hbm, offset_hbm, residual_hbm, out_ref,
    shift_ref, offset_ref, residual_ref, taken_a, taken_b, turned_ref, low_ref, high_ref, back_ref, moved_ref, first_ref,
    send, recv, local_sems,
):
    fields, vertical, rows, cols = state_ref.shape
    half = rows // 2
    gx, gy = lax.axis_index("gx"), lax.axis_index("gy")
    copies = Copies(send, recv)
    x_next = (lax.rem(gx + 1, radial), gy)
    x_prev = (lax.rem(gx + radial - 1, radial), gy)
    others = [(gx, lax.rem(gy + k, groups)) for k in range(1, groups)]

    small = [
        pltpu.make_async_copy(source, target, local_sems.at[5 + k])
        for k, (source, target) in enumerate(
            ((shift_hbm, shift_ref), (offset_hbm, offset_ref), (residual_hbm, residual_ref))
        )
    ]
    for copy in small:
        copy.start()
    barrier = pltpu.get_barrier_semaphore()
    for other in (*others, x_prev, x_next):
        pl.semaphore_signal(barrier, inc=1, device_id=other, device_id_type=MESH)
    pl.semaphore_wait(barrier, groups + 1)

    def part_rows(part):
        return pl.ds(part * half, half)

    taken = (taken_a, taken_b)
    out_flights, keep = [], []
    for part in (0, 1):
        out_flights.append([
            copies.start(
                state_ref.at[other[1], :, part_rows(part)],
                taken[part].at[gy],
                other,
            )
            for other in others
        ])
        keep.append(
            pltpu.make_async_copy(
                state_ref.at[gy, :, part_rows(part)], taken[part].at[gy], local_sems.at[part]
            )
        )
        keep[part].start()

    lane = lax.broadcasted_iota(jnp.int32, (vertical, cols), 1)

    def displace(block_of, amount, place, slot, packed):
        whole, part = amount // cols, amount % cols
        rolled = [
            pltpu.roll(block_of(lax.rem(k - whole + groups, groups)), part, 1)
            for k in range(groups)
        ]
        row = [jnp.where(lane < part, rolled[d - 1], rolled[d]) for d in range(groups)]
        mine = (lane >= 4 * place) & (lane < 4 * place + 4)
        result = []
        for d in range(groups):
            turned_ref[d, slot] = row[d]
            edges = jnp.where(lane < cols // 2, row[(d + 1) % groups], row[d - 1])
            result.append(jnp.where(mine, pltpu.roll(edges, 4 * place + 2, 1), packed[d]))
        return result

    empty = [jnp.zeros((vertical, cols), jnp.float32)] * groups

    def store_packed(slot, packed):
        for d in range(groups):
            turned_ref[d, slot] = packed[d]

    back_flights, kept = [], []

    def send_back(index, first_slot, count):
        span = pl.ds(first_slot, count)
        back_flights.append([
            copies.start(turned_ref.at[other[1], span], back_ref.at[gy, span], other)
            for other in others
        ])
        stay = pltpu.make_async_copy(
            turned_ref.at[gy, span], back_ref.at[gy, span], local_sems.at[2 + index]
        )
        stay.start()
        kept.append(stay)

    ghosts, packed = [], empty
    for copy in small:
        copy.wait()
    for part in (0, 1):
        for copy in out_flights[part]:
            copy.wait_recv()
        keep[part].wait()
        for place in range(half):
            row = part * half + place
            packed = displace(
                lambda b: taken[part][b, :, place, :], shift_ref[row], row, row, packed
            )
        if part == 0:
            ghosts.append(copies.start(turned_ref.at[:, pl.ds(0, DEPTH)], high_ref, x_prev))
        else:
            store_packed(rows, packed)
            edge = pl.ds(rows - DEPTH, DEPTH)
            ghosts.append(copies.start(turned_ref.at[:, edge], low_ref, x_next))
        send_back(part, part * half, half + part)

    for copy in ghosts:
        copy.wait_recv()
    cells_y = cols * groups
    offset = offset_ref[0]
    turn_low = jnp.where(gx == 0, lax.rem(cells_y - offset, cells_y), 0)
    turn_high = jnp.where(gx == radial - 1, offset, 0)
    packed = empty
    for place in range(2 * DEPTH):
        ref, amount = (low_ref, turn_low) if place < DEPTH else (high_ref, turn_high)
        packed = displace(
            lambda b: ref[b, place % DEPTH], amount, place, rows + 1 + place, packed
        )
    store_packed(rows + 1 + 2 * DEPTH, packed)
    send_back(2, rows + 1, 2 * DEPTH + 1)

    def arrive(indices, first_slot, count, row_of):
        for index in indices:
            for copy in back_flights[index]:
                copy.wait_recv()
            kept[index].wait()
        for f in range(fields):
            packed = back_ref[f, first_slot + count]
            for place in range(count):
                moved_ref[row_of(place), f, :, :cols] = back_ref[f, first_slot + place]
                moved_ref[row_of(place), f, :, cols:] = pltpu.roll(
                    packed, (cols - 2 - 4 * place) % cols, 1
                )

    start = gx * rows - DEPTH + residual_ref.shape[0]

    def drift_of(row):
        return residual_ref[lax.rem(start + row, residual_ref.shape[0])]

    def emit_first(row, cur, rates):
        for f in range(fields):
            first_ref[row, f] = cur[f] + time_step * rates[f]

    def emit_out(row, cur, rates):
        for f in range(fields):
            second = cur[f][:, :cols] + time_step * rates[f][:, :cols]
            out_ref[f, :, row - DEPTH, :] = moved_ref[row, f, :, :cols] + second

    def load_from(ref):
        return lambda row: [ref[row, f] for f in range(fields)]

    def stage_one(low, high):
        row_sweep(load_from(moved_ref), low, high, drift_of, emit_first)

    def stage_two(low, high):
        row_sweep(load_from(first_ref), low, high, drift_of, emit_out)

    arrive((0, 1), 0, rows, lambda place: DEPTH + place)
    stage_one(3, rows)
    stage_two(4, rows - 1)
    arrive(
        (2,), rows + 1, 2 * DEPTH, lambda place: place if place < DEPTH else rows + place
    )
    stage_one(1, 2)
    stage_one(rows + 1, rows + 2)
    stage_two(2, 3)
    stage_two(rows, rows + 1)
    for copy in copies.made:
        copy.wait_send()


def spread(state, residual, shift_rows, shear_offset):
    fields, vertical, rows, cols = state.shape
    groups, radial = lax.axis_size("gy"), lax.axis_size("gx")
    wide = rows + 2 * DEPTH
    slots = rows + 2 * DEPTH + 2
    count = 5 * (groups - 1) + 2
    anywhere = pl.BlockSpec(memory_space=pl.ANY)
    vmem = pl.BlockSpec(memory_space=pltpu.VMEM)
    out = pl.pallas_call(
        functools.partial(spread_kernel, groups, radial),
        out_shape=pltpu.VMEM(state.shape, jnp.float32),
        in_specs=[anywhere] * 4,
        out_specs=vmem,
        scratch_shapes=[
            pltpu.SMEM(shift_rows.shape, jnp.int32),
            pltpu.SMEM(shear_offset.shape, jnp.int32),
            pltpu.SMEM(residual.shape, jnp.float32),
            pltpu.VMEM((groups, vertical, rows // 2, cols), jnp.float32),
            pltpu.VMEM((groups, vertical, rows // 2, cols), jnp.float32),
            pltpu.VMEM((groups, slots, vertical, cols), jnp.float32),
            pltpu.VMEM((groups, DEPTH, vertical, cols), jnp.float32),
            pltpu.VMEM((groups, DEPTH, vertical, cols), jnp.float32),
            pltpu.VMEM((fields, slots, vertical, cols), jnp.float32),
            pltpu.VMEM((wide, fields, vertical, 2 * cols), jnp.float32),
            pltpu.VMEM((wide, fields, vertical, 2 * cols), jnp.float32),
            pltpu.SemaphoreType.DMA((count,)),
            pltpu.SemaphoreType.DMA((count,)),
            pltpu.SemaphoreType.DMA((8,)),
        ],
        compiler_params=pltpu.CompilerParams(collective_id=1, has_side_effects=True),
    )(state, shift_rows, shear_offset, residual)
    return 0.5 * out


def local(state, residual, shift_rows, shear_offset):
    if lax.axis_size("gy") == state.shape[0] and state.shape[2] % 16 == 0:
        return spread(state, residual, shift_rows, shear_offset)
    return gathered(state, residual, shift_rows, shear_offset)


def solution(mesh):
    return jax.shard_map(
        local,
        mesh=mesh,
        in_specs=(P(None, None, "gx", "gy"), P(), P("gx"), P()),
        out_specs=P(None, None, "gx", "gy"),
        check_vma=False,
    )
```

```python
import functools

import jax
import jax.numpy as jnp
from jax import lax
from jax.experimental import pallas as pl
from jax.experimental.pallas import tpu as pltpu
from jax.sharding import PartitionSpec as P

time_step = 0.2
viscous = 0.1
resist = 0.1
sound_sq = 1.0
rotation = 0.5
shear_rate = 1.5

MESH = pl.DeviceIdType.MESH
DEPTH = 2


class Copies:
    def __init__(self, send, recv):
        self.send, self.recv, self.made = send, recv, []

    def start(self, source, target, device):
        k = len(self.made)
        copy = pltpu.make_async_remote_copy(
            src_ref=source,
            dst_ref=target,
            send_sem=self.send.at[k],
            recv_sem=self.recv.at[k],
            device_id=device,
            device_id_type=MESH,
        )
        copy.start()
        self.made.append(copy)
        return copy


def copy_count(chips):
    return 8 + sum(10 if 2 * s < chips else 6 for s in range(1, chips // 2 + 1)) + 8 * (chips // 2 + 1)


def gather(state_ref, grid_ref, copies, local_sem, groups, radial):
    rows = state_ref.shape[0]
    chips = groups // 2
    half = rows // 2
    gx, gy = lax.axis_index("gx"), lax.axis_index("gy")
    chip, core = gy // 2, gy % 2

    def at_chip(offset):
        return lax.rem(chip + offset + chips, chips) * 2 + core

    right, left = (gx, at_chip(1)), (gx, at_chip(-1))
    twin = (gx, chip * 2 + (1 - core))
    x_next = (lax.rem(gx + 1, radial), gy)
    x_prev = (lax.rem(gx + radial - 1, radial), gy)

    barrier = pltpu.get_barrier_semaphore()
    for other in (right, left, twin, x_next, x_prev):
        pl.semaphore_signal(barrier, inc=1, device_id=other, device_id_type=MESH)
    pl.semaphore_wait(barrier, 5)

    def piece(block, part):
        return grid_ref.at[block, pl.ds(DEPTH + part * half, half)]

    def low_rows(block):
        return grid_ref.at[block, pl.ds(0, DEPTH)]

    def high_rows(block):
        return grid_ref.at[block, pl.ds(DEPTH + rows, DEPTH)]

    def send_rows(block, part, source):
        if part == 0:
            edge = source.at[pl.ds(0, DEPTH)]
            return block, 0, copies.start(edge, high_rows(block), x_prev)
        edge = source.at[pl.ds(half - DEPTH, DEPTH)]
        return block, 1, copies.start(edge, low_rows(block), x_next)

    to_twin = []

    def pass_rows(sent):
        for block, part, copy in sent:
            copy.wait_recv()
            strip = high_rows(block) if part == 0 else low_rows(block)
            to_twin.append(copies.start(strip, strip, twin))

    own = [state_ref.at[pl.ds(0, half)], state_ref.at[pl.ds(half, half)]]
    keep = pltpu.make_async_copy(state_ref, grid_ref.at[gy, pl.ds(DEPTH, rows)], local_sem)

    flights = []
    order = [(0, 0), (1, 1), (0, 1), (1, 0)] if chips > 2 else [(0, 0), (1, 1)]
    for way, part in order:
        flights.append(
            (way, part, copies.start(own[part], piece(gy, part), right if way == 0 else left))
        )
    sent = [send_rows(gy, part, own[part]) for part in (0, 1)]
    for part in (0, 1):
        to_twin.append(copies.start(own[part], piece(gy, part), twin))
    keep.start()
    pass_rows(sent)
    for step in range(1, chips // 2 + 1):
        later, sent = [], []
        for way, part, copy in flights:
            block = at_chip(-step if way == 0 else step)
            copy.wait_recv()
            ref = piece(block, part)
            if 2 * (step + 1) < chips or (2 * (step + 1) == chips and part == way):
                later.append((way, part, copies.start(ref, ref, right if way == 0 else left)))
            to_twin.append(copies.start(ref, ref, twin))
            sent.append(send_rows(block, part, ref))
        pass_rows(sent)
        flights = later
    keep.wait()
    for copy in to_twin:
        copy.wait_recv()
    for copy in copies.made:
        copy.wait_send()


def row_sweep(load, first_row, last_row, drift_of, emit):
    def y_ahead(a):
        return pltpu.roll(a, a.shape[1] - 1, 1)

    def y_behind(a):
        return pltpu.roll(a, 1, 1)

    def z_ahead(a):
        return pltpu.roll(a, a.shape[0] - 1, 0)

    def z_behind(a):
        return pltpu.roll(a, 1, 0)

    def cells(by, bz):
        return 0.5 * (by + y_ahead(by)), 0.5 * (bz + z_ahead(bz))

    def radial_edges(prev, cur, prev_drift, cur_drift):
        sum_x = prev[1] + cur[1]
        sum_w = (prev[2] + prev_drift) + (cur[2] + cur_drift)
        sum_z = prev[3] + cur[3]
        bx, by, bz = cur[5], cur[6], cur[7]
        bx_y, bx_z = y_behind(bx), z_behind(bx)
        emf_z = 0.125 * (
            (sum_w + y_behind(sum_w)) * (bx + bx_y) - (sum_x + y_behind(sum_x)) * (by + prev[6])
        ) + resist * ((by - prev[6]) - (bx - bx_y))
        emf_y = 0.125 * (
            (sum_x + z_behind(sum_x)) * (bz + prev[7]) - (sum_z + z_behind(sum_z)) * (bx + bx_z)
        ) + resist * ((bx - bx_z) - (bz - prev[7]))
        return emf_z, emf_y

    start_prev, start_cur = load(first_row - 1), load(first_row)
    carry = (
        *cells(start_prev[6], start_prev[7]),
        *cells(start_cur[6], start_cur[7]),
        *radial_edges(start_prev, start_cur, drift_of(first_row - 1), drift_of(first_row)),
    )

    def one(row, carry):
        cy_prev, cz_prev, cy, cz, emf_z, emf_y = carry
        prev, cur, nxt = load(row - 1), load(row), load(row + 1)
        drift = drift_of(row)
        log_rho, vx, vy, vz, ent, bx, by, bz = cur
        w = vy + drift
        cy_next, cz_next = cells(nxt[6], nxt[7])
        emf_z_next, emf_y_next = radial_edges(cur, nxt, drift, drift_of(row + 1))

        half_x, half_w, half_z = 0.5 * vx, 0.5 * w, 0.5 * vz
        diffs, advs = [], []
        for f in range(5):
            a = cur[f]
            ya, yb, za, zb = y_ahead(a), y_behind(a), z_ahead(a), z_behind(a)
            dx, dy, dz = nxt[f] - prev[f], ya - yb, za - zb
            lap = ((nxt[f] + prev[f]) + (ya + yb) + (za + zb)) - 6.0 * a
            diffs.append((dx, dy, dz))
            advs.append(viscous * lap - (half_x * dx + half_w * dy + half_z * dz))

        sum_bx = bx + nxt[5]
        cx = 0.5 * sum_bx
        cur_x = 0.5 * ((y_ahead(cz) - y_behind(cz)) - (z_ahead(cy) - z_behind(cy)))
        cur_y = 0.5 * ((z_ahead(cx) - z_behind(cx)) - (cz_next - cz_prev))
        cur_z = 0.5 * ((cy_next - cy_prev) - (y_ahead(cx) - y_behind(cx)))
        inverse = jnp.exp(-log_rho)
        force_x = inverse * (cur_y * cz - cur_z * cy)
        force_y = inverse * (cur_z * cx - cur_x * cz)
        force_z = inverse * (cur_x * cy - cur_y * cx)

        pairs = [diffs[0][d] + diffs[4][d] for d in range(3)]
        rates = [
            advs[0] - 0.5 * (diffs[1][0] + diffs[2][1] + diffs[3][2]),
            advs[1] - (0.5 * sound_sq) * pairs[0] + force_x + (2.0 * rotation) * vy,
            advs[2] - (0.5 * sound_sq) * pairs[1] + force_y - ((2.0 - shear_rate) * rotation) * vx,
            advs[3] - (0.5 * sound_sq) * pairs[2] + force_z,
            advs[4] + resist * inverse * (cur_x * cur_x + cur_y * cur_y + cur_z * cur_z),
        ]

        w_y, z_y = w + y_behind(w), vz + y_behind(vz)
        bz_y, by_z = y_behind(bz), z_behind(by)
        emf_x = 0.125 * (
            (z_y + z_behind(z_y)) * (by + by_z) - (w_y + z_behind(w_y)) * (bz + bz_y)
        ) + resist * ((bz - bz_y) - (by - by_z))
        stretch = 0.25 * (sum_bx + y_behind(sum_bx))
        rates.append((z_ahead(emf_y) - emf_y) - (y_ahead(emf_z) - emf_z))
        rates.append(
            (emf_z_next - emf_z) - (z_ahead(emf_x) - emf_x) - (shear_rate * rotation) * stretch
        )
        rates.append((y_ahead(emf_x) - emf_x) - (emf_y_next - emf_y))
        emit(row, cur, rates)
        return cy, cz, cy_next, cz_next, emf_z_next, emf_y_next

    if last_row - first_row < 3:
        for row in range(first_row, last_row + 1):
            carry = one(row, carry)
        return
    lax.fori_loop(first_row, last_row + 1, one, carry, unroll=2)


def step_kernel(
    groups, radial, state_ref, table_ref, drift_ref, out_ref,
    grid_ref, moved_ref, first_ref, send, recv, local_sem,
):
    rows, fields, _, cols = state_ref.shape
    gather(state_ref, grid_ref, Copies(send, recv), local_sem, groups, radial)

    lane = lax.broadcasted_iota(jnp.int32, state_ref.shape[2:], 1)

    def turn(row, _):
        amount = table_ref[4, row]
        inside = lane < cols - amount
        low_side = lane < cols // 2
        blocks = [table_ref[k, row] for k in range(4)]
        for f in range(fields):
            before, here, after, beyond = [
                pltpu.roll(grid_ref[b, row, f], cols - amount, 1) for b in blocks
            ]
            moved_ref[row, f, :, :cols] = jnp.where(inside, here, after)
            moved_ref[row, f, :, cols:] = jnp.where(
                low_side, jnp.where(inside, after, beyond), jnp.where(inside, before, here)
            )
        return 0

    lax.fori_loop(0, rows + 2 * DEPTH, turn, 0)

    def drift_of(row):
        return drift_ref[row]

    def emit_first(row, cur, rates):
        for f in range(fields):
            first_ref[row, f] = cur[f] + time_step * rates[f]

    def emit_out(row, cur, rates):
        for f in range(fields):
            second = cur[f][:, :cols] + time_step * rates[f][:, :cols]
            out_ref[row - DEPTH, f] = 0.5 * (moved_ref[row, f, :, :cols] + second)

    def load_from(ref):
        return lambda row: [ref[row, f] for f in range(fields)]

    row_sweep(load_from(moved_ref), 1, rows + 2, drift_of, emit_first)
    row_sweep(load_from(first_ref), 2, rows + 1, drift_of, emit_out)


def gathered(state, residual, shift_rows, shear_offset):
    fields, vertical, rows, cols = state.shape
    groups, radial = lax.axis_size("gy"), lax.axis_size("gx")
    gx, gy = lax.axis_index("gx"), lax.axis_index("gy")
    cells_y = cols * groups
    wide = rows + 2 * DEPTH

    up = [(i, (i + 1) % radial) for i in range(radial)]
    down = [(target, source) for source, target in up]
    low = lax.ppermute(shift_rows[-DEPTH:], "gx", up)
    high = lax.ppermute(shift_rows[:DEPTH], "gx", down)
    offset = shear_offset[0]
    low = low - jnp.where(gx == 0, offset, 0)
    high = high + jnp.where(gx == radial - 1, offset, 0)
    amounts = jnp.concatenate([low, shift_rows, high])
    origin = (cols * gy - amounts) % cells_y
    block, part = origin // cols, origin % cols
    table = jnp.stack(
        [(block + groups - 1) % groups, block, (block + 1) % groups, (block + 2) % groups, part]
    )
    padded = jnp.concatenate([residual[-DEPTH:], residual, residual[:DEPTH]])
    drift = lax.dynamic_slice_in_dim(padded, gx * rows, wide)

    count = copy_count(groups // 2)
    out = pl.pallas_call(
        functools.partial(step_kernel, groups, radial),
        out_shape=jax.ShapeDtypeStruct((rows, fields, vertical, cols), jnp.float32),
        in_specs=[
            pl.BlockSpec(memory_space=pltpu.VMEM),
            pl.BlockSpec(memory_space=pltpu.SMEM),
            pl.BlockSpec(memory_space=pltpu.SMEM),
        ],
        out_specs=pl.BlockSpec(memory_space=pltpu.VMEM),
        scratch_shapes=[
            pltpu.VMEM((groups, wide, fields, vertical, cols), jnp.float32),
            pltpu.VMEM((wide, fields, vertical, 2 * cols), jnp.float32),
            pltpu.VMEM((wide, fields, vertical, 2 * cols), jnp.float32),
            pltpu.SemaphoreType.DMA((count,)),
            pltpu.SemaphoreType.DMA((count,)),
            pltpu.SemaphoreType.DMA,
        ],
        compiler_params=pltpu.CompilerParams(collective_id=0, has_side_effects=True),
    )(jnp.transpose(state, (2, 0, 1, 3)), table, drift)
    return jnp.transpose(out, (1, 2, 0, 3))


def spread_kernel(
    groups, radial, state_ref, shift_hbm, offset_hbm, residual_hbm, out_ref,
    shift_ref, offset_ref, residual_ref, taken_0, taken_1, taken_2, taken_3, turned_ref, edge_ref,
    shear_ref, moved_ref, own_edges, low_edges, high_edges, first_ref, send, recv, local_sems,
):
    fields, vertical, rows, cols = state_ref.shape
    quarter = rows // 4
    taken = (taken_0, taken_1, taken_2, taken_3)
    cells_y = cols * groups
    gx, gy = lax.axis_index("gx"), lax.axis_index("gy")
    copies = Copies(send, recv)
    x_next = (lax.rem(gx + 1, radial), gy)
    x_prev = (lax.rem(gx + radial - 1, radial), gy)
    others = [(gx, lax.rem(gy + k, groups)) for k in range(1, groups)]
    first_x, last_x = gx == 0, gx == radial - 1
    stays = []

    def stay(source, target):
        copy = pltpu.make_async_copy(source, target, local_sems.at[len(stays)])
        copy.start()
        stays.append(copy)
        return copy

    small = [
        stay(source, target)
        for source, target in (
            (shift_hbm, shift_ref), (offset_hbm, offset_ref), (residual_hbm, residual_ref)
        )
    ]
    barrier = pltpu.get_barrier_semaphore()
    for other in (*others, x_prev, x_next):
        pl.semaphore_signal(barrier, inc=1, device_id=other, device_id_type=MESH)
    pl.semaphore_wait(barrier, groups + 1)

    def quarter_rows(q):
        return pl.ds(q * quarter, quarter)

    out_flights = {}
    for q in (0, 3, 1, 2):
        out_flights[q] = [
            copies.start(
                state_ref.at[other[1], :, quarter_rows(q)], taken[q].at[gy], other
            )
            for other in others
        ]
        out_flights[q].append(stay(state_ref.at[gy, :, quarter_rows(q)], taken[q].at[gy]))

    def wait_all(flights):
        for copy in flights:
            copy.wait() if any(copy is s for s in stays) else copy.wait_recv()

    lane = lax.broadcasted_iota(jnp.int32, (vertical, cols), 1)
    empty = [jnp.zeros((vertical, cols), jnp.float32)] * groups

    def displace(block_of, amount, place, slot, packed):
        whole, part = amount // cols, amount % cols
        rolled = [
            pltpu.roll(block_of(lax.rem(k - whole + groups, groups)), part, 1)
            for k in range(groups)
        ]
        row = [jnp.where(lane < part, rolled[d - 1], rolled[d]) for d in range(groups)]
        mine = (lane >= 4 * place) & (lane < 4 * place + 4)
        result = []
        for d in range(groups):
            turned_ref[d, slot] = row[d]
            edges = jnp.where(lane < cols // 2, row[(d + 1) % groups], row[d - 1])
            result.append(jnp.where(mine, pltpu.roll(edges, 4 * place + 2, 1), packed[d]))
        return result

    def displace_quarter(q, packed):
        wait_all(out_flights[q])
        for place in range(quarter):
            row = q * quarter + place
            packed = displace(
                lambda b: taken[q][b, :, place, :], shift_ref[row], row, row, packed
            )
        return packed

    def main_lanes(block, first_row, count):
        return moved_ref.at[block, pl.ds(first_row, count), :, pl.ds(0, cols)]

    def send_back(slot, first_row, count):
        span = pl.ds(slot, count)
        flights = [
            copies.start(turned_ref.at[other[1], span], main_lanes(gy, first_row, count), other)
            for other in others
        ]
        flights.append(stay(turned_ref.at[gy, span], main_lanes(gy, first_row, count)))
        return flights

    def make(source, target, device):
        k = len(copies.made)
        copy = pltpu.make_async_remote_copy(
            src_ref=source,
            dst_ref=target,
            send_sem=send.at[k],
            recv_sem=recv.at[k],
            device_id=device,
            device_id_type=MESH,
        )
        copies.made.append(copy)
        optional.append(copy)
        return copy

    optional = []
    for copy in small:
        copy.wait()
    packed = displace_quarter(0, empty)
    back = {0: send_back(0, DEPTH, quarter)}
    packed = displace_quarter(3, packed)
    to_last = make(turned_ref.at[:, pl.ds(0, DEPTH)], shear_ref, x_prev)
    to_first = make(turned_ref.at[:, pl.ds(rows - DEPTH, DEPTH)], shear_ref, x_next)
    pl.when(first_x)(to_last.start)
    pl.when(last_x)(to_first.start)
    back[3] = send_back(3 * quarter, DEPTH + 3 * quarter, quarter)

    def sheared(first_row, flight, amount):
        flight.wait_recv()
        edges = empty
        for place in range(DEPTH):
            edges = displace(
                lambda b: shear_ref[b, place], amount, rows + place, rows + place, edges
            )
        for d in range(groups):
            edge_ref[d] = edges[d]
        for copy in shear_back[first_row]:
            copy.start()

    span = pl.ds(rows, DEPTH)
    low_row, high_row = 0, DEPTH + rows
    shear_back = {}
    for first_row in (low_row, high_row):
        shear_back[first_row] = [
            make(turned_ref.at[other[1], span], main_lanes(gy, first_row, DEPTH), other)
            for other in others
        ]
        copy = pltpu.make_async_copy(
            turned_ref.at[gy, span], main_lanes(gy, first_row, DEPTH), local_sems.at[len(stays)]
        )
        stays.append(copy)
        shear_back[first_row].append(copy)
    offset = offset_ref[0]
    for d in range(groups):
        edge_ref[d] = empty[0]

    @pl.when(first_x)
    def _():
        sheared(low_row, to_first, lax.rem(cells_y - offset, cells_y))

    @pl.when(last_x)
    def _():
        sheared(high_row, to_last, offset)

    packed = displace_quarter(1, packed)
    packed = displace_quarter(2, packed)
    for d in range(groups):
        edge_ref[d] = jnp.where(lane < 4 * rows, packed[d], edge_ref[d])
    edge_flights = [
        copies.start(edge_ref.at[other[1]], own_edges.at[gy], other) for other in others
    ]
    edge_flights.append(stay(edge_ref.at[gy], own_edges.at[gy]))
    for q in (1, 2):
        back[q] = send_back(q * quarter, DEPTH + q * quarter, quarter)

    for q in (0, 3):
        wait_all(back[q])
    rows_down = make(
        main_lanes(slice(None), DEPTH, DEPTH), main_lanes(slice(None), high_row, DEPTH), x_prev
    )
    rows_up = make(
        main_lanes(slice(None), rows, DEPTH), main_lanes(slice(None), low_row, DEPTH), x_next
    )
    edges_down = make(own_edges, high_edges, x_prev)
    edges_up = make(own_edges, low_edges, x_next)
    not_first, not_last = gx > 0, gx < radial - 1
    pl.when(not_first)(rows_down.start)
    pl.when(not_last)(rows_up.start)
    wait_all(edge_flights)
    pl.when(not_first)(edges_down.start)
    pl.when(not_last)(edges_up.start)

    def unpack(edges_ref, first_place, first_row, count):
        for f in range(fields):
            packed = edges_ref[f]
            for k in range(count):
                moved_ref[f, first_row + k, :, cols:] = pltpu.roll(
                    packed, (cols - 2 - 4 * (first_place + k)) % cols, 1
                )

    start = gx * rows - DEPTH + residual_ref.shape[0]

    def drift_of(row):
        return residual_ref[lax.rem(start + row, residual_ref.shape[0])]

    def emit_first(row, cur, rates):
        for f in range(fields):
            first_ref[row, f] = cur[f] + time_step * rates[f]

    def emit_out(row, cur, rates):
        for f in range(fields):
            second = cur[f][:, :cols] + time_step * rates[f][:, :cols]
            out_ref[f, :, row - DEPTH, :] = moved_ref[f, row, :, :cols] + second

    def stage_one(low, high):
        row_sweep(
            lambda row: [moved_ref[f, row] for f in range(fields)],
            DEPTH + low, DEPTH + high, drift_of, emit_first,
        )

    def stage_two(low, high):
        row_sweep(
            lambda row: [first_ref[row, f] for f in range(fields)],
            DEPTH + low, DEPTH + high, drift_of, emit_out,
        )

    unpack(own_edges, 0, DEPTH, rows)
    stage_one(1, quarter - 2)
    stage_one(3 * quarter + 1, rows - 2)

    @pl.when(first_x)
    def _():
        wait_all(shear_back[low_row])
        unpack(own_edges, rows, low_row, DEPTH)

    @pl.when(not_first)
    def _():
        rows_up.wait_recv()
        edges_up.wait_recv()
        unpack(low_edges, rows - DEPTH, low_row, DEPTH)

    @pl.when(last_x)
    def _():
        wait_all(shear_back[high_row])
        unpack(own_edges, rows, high_row, DEPTH)

    @pl.when(not_last)
    def _():
        rows_down.wait_recv()
        edges_down.wait_recv()
        unpack(high_edges, 0, high_row, DEPTH)

    stage_one(-1, 0)
    stage_one(rows - 1, rows)
    stage_two(0, quarter - 3)
    stage_two(3 * quarter + 2, rows - 1)
    wait_all(back[1])
    stage_one(quarter - 1, 2 * quarter - 2)
    stage_two(quarter - 2, 2 * quarter - 3)
    wait_all(back[2])
    stage_one(2 * quarter - 1, 3 * quarter)
    stage_two(2 * quarter - 2, 3 * quarter + 1)

    for copy in copies.made:
        if not any(copy is o for o in optional):
            copy.wait_send()

    @pl.when(first_x)
    def _():
        to_last.wait_send()
        for copy in shear_back[low_row][:-1]:
            copy.wait_send()

    @pl.when(last_x)
    def _():
        to_first.wait_send()
        for copy in shear_back[high_row][:-1]:
            copy.wait_send()

    @pl.when(not_first)
    def _():
        rows_down.wait_send()
        edges_down.wait_send()

    @pl.when(not_last)
    def _():
        rows_up.wait_send()
        edges_up.wait_send()


def spread(state, residual, shift_rows, shear_offset):
    fields, vertical, rows, cols = state.shape
    groups, radial = lax.axis_size("gy"), lax.axis_size("gx")
    wide = rows + 2 * DEPTH
    count = 11 * (groups - 1) + 6
    anywhere = pl.BlockSpec(memory_space=pl.ANY)
    vmem = pl.BlockSpec(memory_space=pltpu.VMEM)
    edges = pltpu.VMEM((groups, vertical, cols), jnp.float32)
    out = pl.pallas_call(
        functools.partial(spread_kernel, groups, radial),
        out_shape=pltpu.VMEM(state.shape, jnp.float32),
        in_specs=[anywhere] * 4,
        out_specs=vmem,
        scratch_shapes=[
            pltpu.SMEM(shift_rows.shape, jnp.int32),
            pltpu.SMEM(shear_offset.shape, jnp.int32),
            pltpu.SMEM(residual.shape, jnp.float32),
            *[pltpu.VMEM((groups, vertical, rows // 4, cols), jnp.float32)] * 4,
            pltpu.VMEM((groups, rows + DEPTH, vertical, cols), jnp.float32),
            edges,
            pltpu.VMEM((groups, DEPTH, vertical, cols), jnp.float32),
            pltpu.VMEM((fields, wide, vertical, 2 * cols), jnp.float32),
            edges,
            edges,
            edges,
            pltpu.VMEM((wide, fields, vertical, 2 * cols), jnp.float32),
            pltpu.SemaphoreType.DMA((count,)),
            pltpu.SemaphoreType.DMA((count,)),
            pltpu.SemaphoreType.DMA((14,)),
        ],
        compiler_params=pltpu.CompilerParams(collective_id=1, has_side_effects=True),
    )(state, shift_rows, shear_offset, residual)
    return 0.5 * out


def local(state, residual, shift_rows, shear_offset):
    fields, _, rows, cols = state.shape
    paired = lax.axis_size("gy") == fields and lax.axis_size("gx") > 2
    if paired and rows % 16 == 0 and 4 * (rows + DEPTH) <= cols:
        return spread(state, residual, shift_rows, shear_offset)
    return gathered(state, residual, shift_rows, shear_offset)


def solution(mesh):
    return jax.shard_map(
        local,
        mesh=mesh,
        in_specs=(P(None, None, "gx", "gy"), P(), P("gx"), P()),
        out_specs=P(None, None, "gx", "gy"),
        check_vma=False,
    )
```

```python
import functools

import jax
import jax.numpy as jnp
from jax import lax
from jax.experimental import pallas as pl
from jax.experimental.pallas import tpu as pltpu
from jax.sharding import PartitionSpec as P

time_step = 0.2
viscous = 0.1
resist = 0.1
sound_sq = 1.0
rotation = 0.5
shear_rate = 1.5

MESH = pl.DeviceIdType.MESH
DEPTH = 2


class Copies:
    def __init__(self, send, recv):
        self.send, self.recv, self.made = send, recv, []

    def start(self, source, target, device):
        k = len(self.made)
        copy = pltpu.make_async_remote_copy(
            src_ref=source,
            dst_ref=target,
            send_sem=self.send.at[k],
            recv_sem=self.recv.at[k],
            device_id=device,
            device_id_type=MESH,
        )
        copy.start()
        self.made.append(copy)
        return copy


def copy_count(chips):
    return 8 + sum(10 if 2 * s < chips else 6 for s in range(1, chips // 2 + 1)) + 8 * (chips // 2 + 1)


def gather(state_ref, grid_ref, copies, local_sem, groups, radial):
    rows = state_ref.shape[0]
    chips = groups // 2
    half = rows // 2
    gx, gy = lax.axis_index("gx"), lax.axis_index("gy")
    chip, core = gy // 2, gy % 2

    def at_chip(offset):
        return lax.rem(chip + offset + chips, chips) * 2 + core

    right, left = (gx, at_chip(1)), (gx, at_chip(-1))
    twin = (gx, chip * 2 + (1 - core))
    x_next = (lax.rem(gx + 1, radial), gy)
    x_prev = (lax.rem(gx + radial - 1, radial), gy)

    barrier = pltpu.get_barrier_semaphore()
    for other in (right, left, twin, x_next, x_prev):
        pl.semaphore_signal(barrier, inc=1, device_id=other, device_id_type=MESH)
    pl.semaphore_wait(barrier, 5)

    def piece(block, part):
        return grid_ref.at[block, pl.ds(DEPTH + part * half, half)]

    def low_rows(block):
        return grid_ref.at[block, pl.ds(0, DEPTH)]

    def high_rows(block):
        return grid_ref.at[block, pl.ds(DEPTH + rows, DEPTH)]

    def send_rows(block, part, source):
        if part == 0:
            edge = source.at[pl.ds(0, DEPTH)]
            return block, 0, copies.start(edge, high_rows(block), x_prev)
        edge = source.at[pl.ds(half - DEPTH, DEPTH)]
        return block, 1, copies.start(edge, low_rows(block), x_next)

    to_twin = []

    def pass_rows(sent):
        for block, part, copy in sent:
            copy.wait_recv()
            strip = high_rows(block) if part == 0 else low_rows(block)
            to_twin.append(copies.start(strip, strip, twin))

    own = [state_ref.at[pl.ds(0, half)], state_ref.at[pl.ds(half, half)]]
    keep = pltpu.make_async_copy(state_ref, grid_ref.at[gy, pl.ds(DEPTH, rows)], local_sem)

    flights = []
    order = [(0, 0), (1, 1), (0, 1), (1, 0)] if chips > 2 else [(0, 0), (1, 1)]
    for way, part in order:
        flights.append(
            (way, part, copies.start(own[part], piece(gy, part), right if way == 0 else left))
        )
    sent = [send_rows(gy, part, own[part]) for part in (0, 1)]
    for part in (0, 1):
        to_twin.append(copies.start(own[part], piece(gy, part), twin))
    keep.start()
    pass_rows(sent)
    for step in range(1, chips // 2 + 1):
        later, sent = [], []
        for way, part, copy in flights:
            block = at_chip(-step if way == 0 else step)
            copy.wait_recv()
            ref = piece(block, part)
            if 2 * (step + 1) < chips or (2 * (step + 1) == chips and part == way):
                later.append((way, part, copies.start(ref, ref, right if way == 0 else left)))
            to_twin.append(copies.start(ref, ref, twin))
            sent.append(send_rows(block, part, ref))
        pass_rows(sent)
        flights = later
    keep.wait()
    for copy in to_twin:
        copy.wait_recv()
    for copy in copies.made:
        copy.wait_send()


def row_sweep(load, first_row, last_row, drift_of, emit):
    def y_ahead(a):
        return pltpu.roll(a, a.shape[1] - 1, 1)

    def y_behind(a):
        return pltpu.roll(a, 1, 1)

    def z_ahead(a):
        return pltpu.roll(a, a.shape[0] - 1, 0)

    def z_behind(a):
        return pltpu.roll(a, 1, 0)

    def cells(by, bz):
        return 0.5 * (by + y_ahead(by)), 0.5 * (bz + z_ahead(bz))

    def radial_edges(prev, cur, prev_drift, cur_drift):
        sum_x = prev[1] + cur[1]
        sum_w = (prev[2] + prev_drift) + (cur[2] + cur_drift)
        sum_z = prev[3] + cur[3]
        bx, by, bz = cur[5], cur[6], cur[7]
        bx_y, bx_z = y_behind(bx), z_behind(bx)
        emf_z = 0.125 * (
            (sum_w + y_behind(sum_w)) * (bx + bx_y) - (sum_x + y_behind(sum_x)) * (by + prev[6])
        ) + resist * ((by - prev[6]) - (bx - bx_y))
        emf_y = 0.125 * (
            (sum_x + z_behind(sum_x)) * (bz + prev[7]) - (sum_z + z_behind(sum_z)) * (bx + bx_z)
        ) + resist * ((bx - bx_z) - (bz - prev[7]))
        return emf_z, emf_y

    start_prev, start_cur = load(first_row - 1), load(first_row)
    carry = (
        *cells(start_prev[6], start_prev[7]),
        *cells(start_cur[6], start_cur[7]),
        *radial_edges(start_prev, start_cur, drift_of(first_row - 1), drift_of(first_row)),
    )

    def one(row, carry):
        cy_prev, cz_prev, cy, cz, emf_z, emf_y = carry
        prev, cur, nxt = load(row - 1), load(row), load(row + 1)
        drift = drift_of(row)
        log_rho, vx, vy, vz, ent, bx, by, bz = cur
        w = vy + drift
        cy_next, cz_next = cells(nxt[6], nxt[7])
        emf_z_next, emf_y_next = radial_edges(cur, nxt, drift, drift_of(row + 1))

        half_x, half_w, half_z = 0.5 * vx, 0.5 * w, 0.5 * vz
        diffs, advs = [], []
        for f in range(5):
            a = cur[f]
            ya, yb, za, zb = y_ahead(a), y_behind(a), z_ahead(a), z_behind(a)
            dx, dy, dz = nxt[f] - prev[f], ya - yb, za - zb
            lap = ((nxt[f] + prev[f]) + (ya + yb) + (za + zb)) - 6.0 * a
            diffs.append((dx, dy, dz))
            advs.append(viscous * lap - (half_x * dx + half_w * dy + half_z * dz))

        sum_bx = bx + nxt[5]
        cx = 0.5 * sum_bx
        cur_x = 0.5 * ((y_ahead(cz) - y_behind(cz)) - (z_ahead(cy) - z_behind(cy)))
        cur_y = 0.5 * ((z_ahead(cx) - z_behind(cx)) - (cz_next - cz_prev))
        cur_z = 0.5 * ((cy_next - cy_prev) - (y_ahead(cx) - y_behind(cx)))
        inverse = jnp.exp(-log_rho)
        force_x = inverse * (cur_y * cz - cur_z * cy)
        force_y = inverse * (cur_z * cx - cur_x * cz)
        force_z = inverse * (cur_x * cy - cur_y * cx)

        pairs = [diffs[0][d] + diffs[4][d] for d in range(3)]
        rates = [
            advs[0] - 0.5 * (diffs[1][0] + diffs[2][1] + diffs[3][2]),
            advs[1] - (0.5 * sound_sq) * pairs[0] + force_x + (2.0 * rotation) * vy,
            advs[2] - (0.5 * sound_sq) * pairs[1] + force_y - ((2.0 - shear_rate) * rotation) * vx,
            advs[3] - (0.5 * sound_sq) * pairs[2] + force_z,
            advs[4] + resist * inverse * (cur_x * cur_x + cur_y * cur_y + cur_z * cur_z),
        ]

        w_y, z_y = w + y_behind(w), vz + y_behind(vz)
        bz_y, by_z = y_behind(bz), z_behind(by)
        emf_x = 0.125 * (
            (z_y + z_behind(z_y)) * (by + by_z) - (w_y + z_behind(w_y)) * (bz + bz_y)
        ) + resist * ((bz - bz_y) - (by - by_z))
        stretch = 0.25 * (sum_bx + y_behind(sum_bx))
        rates.append((z_ahead(emf_y) - emf_y) - (y_ahead(emf_z) - emf_z))
        rates.append(
            (emf_z_next - emf_z) - (z_ahead(emf_x) - emf_x) - (shear_rate * rotation) * stretch
        )
        rates.append((y_ahead(emf_x) - emf_x) - (emf_y_next - emf_y))
        emit(row, cur, rates)
        return cy, cz, cy_next, cz_next, emf_z_next, emf_y_next

    if last_row - first_row < 3:
        for row in range(first_row, last_row + 1):
            carry = one(row, carry)
        return
    lax.fori_loop(first_row, last_row + 1, one, carry, unroll=2)


def step_kernel(
    groups, radial, state_ref, table_ref, drift_ref, out_ref,
    grid_ref, moved_ref, first_ref, send, recv, local_sem,
):
    rows, fields, _, cols = state_ref.shape
    gather(state_ref, grid_ref, Copies(send, recv), local_sem, groups, radial)

    lane = lax.broadcasted_iota(jnp.int32, state_ref.shape[2:], 1)

    def turn(row, _):
        amount = table_ref[4, row]
        inside = lane < cols - amount
        low_side = lane < cols // 2
        blocks = [table_ref[k, row] for k in range(4)]
        for f in range(fields):
            before, here, after, beyond = [
                pltpu.roll(grid_ref[b, row, f], cols - amount, 1) for b in blocks
            ]
            moved_ref[row, f, :, :cols] = jnp.where(inside, here, after)
            moved_ref[row, f, :, cols:] = jnp.where(
                low_side, jnp.where(inside, after, beyond), jnp.where(inside, before, here)
            )
        return 0

    lax.fori_loop(0, rows + 2 * DEPTH, turn, 0)

    def drift_of(row):
        return drift_ref[row]

    def emit_first(row, cur, rates):
        for f in range(fields):
            first_ref[row, f] = cur[f] + time_step * rates[f]

    def emit_out(row, cur, rates):
        for f in range(fields):
            second = cur[f][:, :cols] + time_step * rates[f][:, :cols]
            out_ref[row - DEPTH, f] = 0.5 * (moved_ref[row, f, :, :cols] + second)

    def load_from(ref):
        return lambda row: [ref[row, f] for f in range(fields)]

    row_sweep(load_from(moved_ref), 1, rows + 2, drift_of, emit_first)
    row_sweep(load_from(first_ref), 2, rows + 1, drift_of, emit_out)


def gathered(state, residual, shift_rows, shear_offset):
    fields, vertical, rows, cols = state.shape
    groups, radial = lax.axis_size("gy"), lax.axis_size("gx")
    gx, gy = lax.axis_index("gx"), lax.axis_index("gy")
    cells_y = cols * groups
    wide = rows + 2 * DEPTH

    up = [(i, (i + 1) % radial) for i in range(radial)]
    down = [(target, source) for source, target in up]
    low = lax.ppermute(shift_rows[-DEPTH:], "gx", up)
    high = lax.ppermute(shift_rows[:DEPTH], "gx", down)
    offset = shear_offset[0]
    low = low - jnp.where(gx == 0, offset, 0)
    high = high + jnp.where(gx == radial - 1, offset, 0)
    amounts = jnp.concatenate([low, shift_rows, high])
    origin = (cols * gy - amounts) % cells_y
    block, part = origin // cols, origin % cols
    table = jnp.stack(
        [(block + groups - 1) % groups, block, (block + 1) % groups, (block + 2) % groups, part]
    )
    padded = jnp.concatenate([residual[-DEPTH:], residual, residual[:DEPTH]])
    drift = lax.dynamic_slice_in_dim(padded, gx * rows, wide)

    count = copy_count(groups // 2)
    out = pl.pallas_call(
        functools.partial(step_kernel, groups, radial),
        out_shape=jax.ShapeDtypeStruct((rows, fields, vertical, cols), jnp.float32),
        in_specs=[
            pl.BlockSpec(memory_space=pltpu.VMEM),
            pl.BlockSpec(memory_space=pltpu.SMEM),
            pl.BlockSpec(memory_space=pltpu.SMEM),
        ],
        out_specs=pl.BlockSpec(memory_space=pltpu.VMEM),
        scratch_shapes=[
            pltpu.VMEM((groups, wide, fields, vertical, cols), jnp.float32),
            pltpu.VMEM((wide, fields, vertical, 2 * cols), jnp.float32),
            pltpu.VMEM((wide, fields, vertical, 2 * cols), jnp.float32),
            pltpu.SemaphoreType.DMA((count,)),
            pltpu.SemaphoreType.DMA((count,)),
            pltpu.SemaphoreType.DMA,
        ],
        compiler_params=pltpu.CompilerParams(collective_id=0, has_side_effects=True),
    )(jnp.transpose(state, (2, 0, 1, 3)), table, drift)
    return jnp.transpose(out, (1, 2, 0, 3))


def spread_kernel(
    groups, radial, state_ref, shift_hbm, offset_hbm, residual_hbm, out_ref,
    shift_ref, offset_ref, residual_ref, taken_0, taken_1, taken_2, taken_3, turned_ref, edge_ref,
    shear_ref, moved_ref, own_edges, low_edges, high_edges, first_ref, send, recv, local_sems,
):
    fields, vertical, rows, cols = state_ref.shape
    quarter = rows // 4
    taken = (taken_0, taken_1, taken_2, taken_3)
    cells_y = cols * groups
    gx, gy = lax.axis_index("gx"), lax.axis_index("gy")
    x_next = (lax.rem(gx + 1, radial), gy)
    x_prev = (lax.rem(gx + radial - 1, radial), gy)
    others = [(gx, lax.rem(gy + k, groups)) for k in range(1, groups)]
    first_x, last_x = gx == 0, gx == radial - 1
    not_first, not_last = gx > 0, gx < radial - 1
    out_sent, back_sent, edges_sent, shear_sent, ends_sent, down_sent, up_sent = range(7)
    back_got = {0: 4, 3: 5, 1: 6}
    edges_got, shear_got, ends_got, rows_got, sides_got = 7, 8, 9, (10, 11), (12, 13)

    def remote(source, target, device, sent, got):
        return pltpu.make_async_remote_copy(
            src_ref=source,
            dst_ref=target,
            send_sem=send.at[sent],
            recv_sem=recv.at[got],
            device_id=device,
            device_id_type=MESH,
        )

    def spread_out(source, target, sent, got):
        for other in others:
            remote(source(other[1]), target, other, sent, got).start()
        pltpu.make_async_copy(source(gy), target, recv.at[got]).start()

    def arrived(ref, got):
        pltpu.make_async_copy(ref, ref, recv.at[got]).wait()

    def left(ref, sent):
        pltpu.make_async_copy(ref, ref, send.at[sent]).wait()

    small = [
        pltpu.make_async_copy(source, target, local_sems.at[k])
        for k, (source, target) in enumerate(
            ((shift_hbm, shift_ref), (offset_hbm, offset_ref), (residual_hbm, residual_ref))
        )
    ]
    for copy in small:
        copy.start()
    barrier = pltpu.get_barrier_semaphore()
    for other in (*others, x_prev, x_next):
        pl.semaphore_signal(barrier, inc=1, device_id=other, device_id_type=MESH)
    pl.semaphore_wait(barrier, groups + 1)

    def quarter_rows(q):
        return pl.ds(q * quarter, quarter)

    for pair in ((0, 3), (1, 2)):
        for other in others:
            for q in pair:
                remote(
                    state_ref.at[other[1], :, quarter_rows(q)], taken[q].at[gy], other, out_sent, q
                ).start()
        for q in pair:
            pltpu.make_async_copy(
                state_ref.at[gy, :, quarter_rows(q)], taken[q].at[gy], recv.at[q]
            ).start()

    lane = lax.broadcasted_iota(jnp.int32, (vertical, cols), 1)
    empty = [jnp.zeros((vertical, cols), jnp.float32)] * groups

    def displace(block_of, amount, place, slot, packed):
        whole, part = amount // cols, amount % cols
        rolled = [
            pltpu.roll(block_of(lax.rem(k - whole + groups, groups)), part, 1)
            for k in range(groups)
        ]
        row = [jnp.where(lane < part, rolled[d - 1], rolled[d]) for d in range(groups)]
        mine = (lane >= 4 * place) & (lane < 4 * place + 4)
        result = []
        for d in range(groups):
            turned_ref[d, slot] = row[d]
            edges = jnp.where(lane < cols // 2, row[(d + 1) % groups], row[d - 1])
            result.append(jnp.where(mine, pltpu.roll(edges, 4 * place + 2, 1), packed[d]))
        return result

    def displace_quarter(q, packed):
        arrived(taken[q], q)
        for place in range(quarter):
            row = q * quarter + place
            packed = displace(
                lambda b: taken[q][b, :, place, :], shift_ref[row], row, row, packed
            )
        return packed

    def main_lanes(block, first_row, count):
        return moved_ref.at[block, pl.ds(first_row, count), :, pl.ds(0, cols)]

    def send_back(q, count):
        span = pl.ds(q * quarter, count)
        spread_out(
            lambda d: turned_ref.at[d, span],
            main_lanes(gy, DEPTH + q * quarter, count),
            back_sent,
            back_got[q],
        )

    for copy in small:
        copy.wait()
    packed = displace_quarter(0, empty)
    packed = displace_quarter(3, packed)
    to_last = remote(turned_ref.at[:, pl.ds(0, DEPTH)], shear_ref, x_prev, ends_sent, ends_got)
    to_first = remote(
        turned_ref.at[:, pl.ds(rows - DEPTH, DEPTH)], shear_ref, x_next, ends_sent, ends_got
    )
    pl.when(first_x)(to_last.start)
    pl.when(last_x)(to_first.start)
    for q in (0, 3):
        send_back(q, quarter)

    low_row, high_row = 0, DEPTH + rows
    offset = offset_ref[0]
    for d in range(groups):
        edge_ref[d] = empty[0]

    def sheared(first_row, amount):
        arrived(shear_ref, ends_got)
        edges = empty
        for place in range(DEPTH):
            edges = displace(
                lambda b: shear_ref[b, place], amount, rows + place, rows + place, edges
            )
        for d in range(groups):
            edge_ref[d] = edges[d]
        spread_out(
            lambda d: turned_ref.at[d, pl.ds(rows, DEPTH)],
            main_lanes(gy, first_row, DEPTH),
            shear_sent,
            shear_got,
        )

    @pl.when(first_x)
    def _():
        sheared(low_row, lax.rem(cells_y - offset, cells_y))

    @pl.when(last_x)
    def _():
        sheared(high_row, offset)

    packed = displace_quarter(1, packed)
    packed = displace_quarter(2, packed)
    for d in range(groups):
        edge_ref[d] = jnp.where(lane < 4 * rows, packed[d], edge_ref[d])
    spread_out(lambda d: edge_ref.at[d], own_edges.at[gy], edges_sent, edges_got)
    send_back(1, 2 * quarter)

    every = slice(None)
    for q in (0, 3):
        arrived(main_lanes(every, DEPTH + q * quarter, quarter), back_got[q])
    rows_down = remote(
        main_lanes(every, DEPTH, DEPTH), main_lanes(every, high_row, DEPTH),
        x_prev, down_sent, rows_got[1],
    )
    rows_up = remote(
        main_lanes(every, rows, DEPTH), main_lanes(every, low_row, DEPTH),
        x_next, up_sent, rows_got[0],
    )
    edges_down = remote(own_edges, high_edges, x_prev, down_sent, sides_got[1])
    edges_up = remote(own_edges, low_edges, x_next, up_sent, sides_got[0])
    pl.when(not_first)(rows_down.start)
    pl.when(not_last)(rows_up.start)
    arrived(own_edges, edges_got)
    pl.when(not_first)(edges_down.start)
    pl.when(not_last)(edges_up.start)

    def unpack(edges_ref, first_place, first_row, count):
        for f in range(fields):
            packed = edges_ref[f]
            for k in range(count):
                moved_ref[f, first_row + k, :, cols:] = pltpu.roll(
                    packed, (cols - 2 - 4 * (first_place + k)) % cols, 1
                )

    start = gx * rows - DEPTH + residual_ref.shape[0]

    def drift_of(row):
        return residual_ref[lax.rem(start + row, residual_ref.shape[0])]

    def emit_first(row, cur, rates):
        for f in range(fields):
            first_ref[row, f] = cur[f] + time_step * rates[f]

    def emit_out(row, cur, rates):
        for f in range(fields):
            second = cur[f][:, :cols] + time_step * rates[f][:, :cols]
            out_ref[f, :, row - DEPTH, :] = moved_ref[f, row, :, :cols] + second

    def stage_one(low, high):
        row_sweep(
            lambda row: [moved_ref[f, row] for f in range(fields)],
            DEPTH + low, DEPTH + high, drift_of, emit_first,
        )

    def stage_two(low, high):
        row_sweep(
            lambda row: [first_ref[row, f] for f in range(fields)],
            DEPTH + low, DEPTH + high, drift_of, emit_out,
        )

    unpack(own_edges, 0, DEPTH, rows)
    stage_one(1, quarter - 2)
    stage_one(3 * quarter + 1, rows - 2)

    @pl.when(first_x)
    def _():
        arrived(main_lanes(every, low_row, DEPTH), shear_got)
        unpack(own_edges, rows, low_row, DEPTH)

    @pl.when(not_first)
    def _():
        rows_up.wait_recv()
        edges_up.wait_recv()
        unpack(low_edges, rows - DEPTH, low_row, DEPTH)

    @pl.when(last_x)
    def _():
        arrived(main_lanes(every, high_row, DEPTH), shear_got)
        unpack(own_edges, rows, high_row, DEPTH)

    @pl.when(not_last)
    def _():
        rows_down.wait_recv()
        edges_down.wait_recv()
        unpack(high_edges, 0, high_row, DEPTH)

    stage_one(-1, 0)
    stage_one(rows - 1, rows)
    stage_two(0, quarter - 3)
    stage_two(3 * quarter + 2, rows - 1)
    arrived(main_lanes(every, DEPTH + quarter, 2 * quarter), back_got[1])
    stage_one(quarter - 1, 3 * quarter)
    stage_two(quarter - 2, 3 * quarter + 1)

    away = pl.ds(0, groups - 1)
    left(state_ref.at[away], out_sent)
    left(turned_ref.at[away, pl.ds(0, rows)], back_sent)
    left(edge_ref.at[away], edges_sent)

    @pl.when(first_x | last_x)
    def _():
        left(shear_ref, ends_sent)
        left(turned_ref.at[away, pl.ds(rows, DEPTH)], shear_sent)

    @pl.when(not_first)
    def _():
        rows_down.wait_send()
        edges_down.wait_send()

    @pl.when(not_last)
    def _():
        rows_up.wait_send()
        edges_up.wait_send()


def spread(state, residual, shift_rows, shear_offset):
    fields, vertical, rows, cols = state.shape
    groups, radial = lax.axis_size("gy"), lax.axis_size("gx")
    wide = rows + 2 * DEPTH
    anywhere = pl.BlockSpec(memory_space=pl.ANY)
    vmem = pl.BlockSpec(memory_space=pltpu.VMEM)
    edges = pltpu.VMEM((groups, vertical, cols), jnp.float32)
    out = pl.pallas_call(
        functools.partial(spread_kernel, groups, radial),
        out_shape=pltpu.VMEM(state.shape, jnp.float32),
        in_specs=[anywhere] * 4,
        out_specs=vmem,
        scratch_shapes=[
            pltpu.SMEM(shift_rows.shape, jnp.int32),
            pltpu.SMEM(shear_offset.shape, jnp.int32),
            pltpu.SMEM(residual.shape, jnp.float32),
            *[pltpu.VMEM((groups, vertical, rows // 4, cols), jnp.float32)] * 4,
            pltpu.VMEM((groups, rows + DEPTH, vertical, cols), jnp.float32),
            edges,
            pltpu.VMEM((groups, DEPTH, vertical, cols), jnp.float32),
            pltpu.VMEM((fields, wide, vertical, 2 * cols), jnp.float32),
            edges,
            edges,
            edges,
            pltpu.VMEM((wide, fields, vertical, 2 * cols), jnp.float32),
            pltpu.SemaphoreType.DMA((7,)),
            pltpu.SemaphoreType.DMA((14,)),
            pltpu.SemaphoreType.DMA((3,)),
        ],
        compiler_params=pltpu.CompilerParams(collective_id=1, has_side_effects=True),
    )(state, shift_rows, shear_offset, residual)
    return 0.5 * out


def local(state, residual, shift_rows, shear_offset):
    fields, _, rows, cols = state.shape
    paired = lax.axis_size("gy") == fields and lax.axis_size("gx") > 2
    if paired and rows % 16 == 0 and 4 * (rows + DEPTH) <= cols:
        return spread(state, residual, shift_rows, shear_offset)
    return gathered(state, residual, shift_rows, shear_offset)


def solution(mesh):
    return jax.shard_map(
        local,
        mesh=mesh,
        in_specs=(P(None, None, "gx", "gy"), P(), P("gx"), P()),
        out_specs=P(None, None, "gx", "gy"),
        check_vma=False,
    )
```

```python
import functools

import jax
import jax.numpy as jnp
from jax import lax
from jax.experimental import pallas as pl
from jax.experimental.pallas import tpu as pltpu
from jax.sharding import PartitionSpec as P

time_step = 0.2
viscous = 0.1
resist = 0.1
sound_sq = 1.0
rotation = 0.5
shear_rate = 1.5

MESH = pl.DeviceIdType.MESH
DEPTH = 2
WINDOW = 12


class Copies:
    def __init__(self, send, recv):
        self.send, self.recv, self.made = send, recv, []

    def start(self, source, target, device):
        k = len(self.made)
        copy = pltpu.make_async_remote_copy(
            src_ref=source,
            dst_ref=target,
            send_sem=self.send.at[k],
            recv_sem=self.recv.at[k],
            device_id=device,
            device_id_type=MESH,
        )
        copy.start()
        self.made.append(copy)
        return copy


def copy_count(chips):
    return 8 + sum(10 if 2 * s < chips else 6 for s in range(1, chips // 2 + 1)) + 8 * (chips // 2 + 1)


def gather(state_ref, grid_ref, copies, local_sem, groups, radial):
    rows = state_ref.shape[0]
    chips = groups // 2
    half = rows // 2
    gx, gy = lax.axis_index("gx"), lax.axis_index("gy")
    chip, core = gy // 2, gy % 2

    def at_chip(offset):
        return lax.rem(chip + offset + chips, chips) * 2 + core

    right, left = (gx, at_chip(1)), (gx, at_chip(-1))
    twin = (gx, chip * 2 + (1 - core))
    x_next = (lax.rem(gx + 1, radial), gy)
    x_prev = (lax.rem(gx + radial - 1, radial), gy)

    barrier = pltpu.get_barrier_semaphore()
    for other in (right, left, twin, x_next, x_prev):
        pl.semaphore_signal(barrier, inc=1, device_id=other, device_id_type=MESH)
    pl.semaphore_wait(barrier, 5)

    def piece(block, part):
        return grid_ref.at[block, pl.ds(DEPTH + part * half, half)]

    def low_rows(block):
        return grid_ref.at[block, pl.ds(0, DEPTH)]

    def high_rows(block):
        return grid_ref.at[block, pl.ds(DEPTH + rows, DEPTH)]

    def send_rows(block, part, source):
        if part == 0:
            edge = source.at[pl.ds(0, DEPTH)]
            return block, 0, copies.start(edge, high_rows(block), x_prev)
        edge = source.at[pl.ds(half - DEPTH, DEPTH)]
        return block, 1, copies.start(edge, low_rows(block), x_next)

    to_twin = []

    def pass_rows(sent):
        for block, part, copy in sent:
            copy.wait_recv()
            strip = high_rows(block) if part == 0 else low_rows(block)
            to_twin.append(copies.start(strip, strip, twin))

    own = [state_ref.at[pl.ds(0, half)], state_ref.at[pl.ds(half, half)]]
    keep = pltpu.make_async_copy(state_ref, grid_ref.at[gy, pl.ds(DEPTH, rows)], local_sem)

    flights = []
    order = [(0, 0), (1, 1), (0, 1), (1, 0)] if chips > 2 else [(0, 0), (1, 1)]
    for way, part in order:
        flights.append(
            (way, part, copies.start(own[part], piece(gy, part), right if way == 0 else left))
        )
    sent = [send_rows(gy, part, own[part]) for part in (0, 1)]
    for part in (0, 1):
        to_twin.append(copies.start(own[part], piece(gy, part), twin))
    keep.start()
    pass_rows(sent)
    for step in range(1, chips // 2 + 1):
        later, sent = [], []
        for way, part, copy in flights:
            block = at_chip(-step if way == 0 else step)
            copy.wait_recv()
            ref = piece(block, part)
            if 2 * (step + 1) < chips or (2 * (step + 1) == chips and part == way):
                later.append((way, part, copies.start(ref, ref, right if way == 0 else left)))
            to_twin.append(copies.start(ref, ref, twin))
            sent.append(send_rows(block, part, ref))
        pass_rows(sent)
        flights = later
    keep.wait()
    for copy in to_twin:
        copy.wait_recv()
    for copy in copies.made:
        copy.wait_send()


def row_sweep(load, first_row, last_row, drift_of, emit):
    def y_ahead(a):
        return pltpu.roll(a, a.shape[1] - 1, 1)

    def y_behind(a):
        return pltpu.roll(a, 1, 1)

    def z_ahead(a):
        return pltpu.roll(a, a.shape[0] - 1, 0)

    def z_behind(a):
        return pltpu.roll(a, 1, 0)

    def cells(by, bz):
        return 0.5 * (by + y_ahead(by)), 0.5 * (bz + z_ahead(bz))

    def radial_edges(prev, cur, prev_drift, cur_drift):
        sum_x = prev[1] + cur[1]
        sum_w = (prev[2] + prev_drift) + (cur[2] + cur_drift)
        sum_z = prev[3] + cur[3]
        bx, by, bz = cur[5], cur[6], cur[7]
        bx_y, bx_z = y_behind(bx), z_behind(bx)
        emf_z = 0.125 * (
            (sum_w + y_behind(sum_w)) * (bx + bx_y) - (sum_x + y_behind(sum_x)) * (by + prev[6])
        ) + resist * ((by - prev[6]) - (bx - bx_y))
        emf_y = 0.125 * (
            (sum_x + z_behind(sum_x)) * (bz + prev[7]) - (sum_z + z_behind(sum_z)) * (bx + bx_z)
        ) + resist * ((bx - bx_z) - (bz - prev[7]))
        return emf_z, emf_y

    start_prev, start_cur = load(first_row - 1), load(first_row)
    carry = (
        *cells(start_prev[6], start_prev[7]),
        *cells(start_cur[6], start_cur[7]),
        *radial_edges(start_prev, start_cur, drift_of(first_row - 1), drift_of(first_row)),
    )

    def one(row, carry):
        cy_prev, cz_prev, cy, cz, emf_z, emf_y = carry
        prev, cur, nxt = load(row - 1), load(row), load(row + 1)
        drift = drift_of(row)
        log_rho, vx, vy, vz, ent, bx, by, bz = cur
        w = vy + drift
        cy_next, cz_next = cells(nxt[6], nxt[7])
        emf_z_next, emf_y_next = radial_edges(cur, nxt, drift, drift_of(row + 1))

        half_x, half_w, half_z = 0.5 * vx, 0.5 * w, 0.5 * vz
        diffs, advs = [], []
        for f in range(5):
            a = cur[f]
            ya, yb, za, zb = y_ahead(a), y_behind(a), z_ahead(a), z_behind(a)
            dx, dy, dz = nxt[f] - prev[f], ya - yb, za - zb
            lap = ((nxt[f] + prev[f]) + (ya + yb) + (za + zb)) - 6.0 * a
            diffs.append((dx, dy, dz))
            advs.append(viscous * lap - (half_x * dx + half_w * dy + half_z * dz))

        sum_bx = bx + nxt[5]
        cx = 0.5 * sum_bx
        cur_x = 0.5 * ((y_ahead(cz) - y_behind(cz)) - (z_ahead(cy) - z_behind(cy)))
        cur_y = 0.5 * ((z_ahead(cx) - z_behind(cx)) - (cz_next - cz_prev))
        cur_z = 0.5 * ((cy_next - cy_prev) - (y_ahead(cx) - y_behind(cx)))
        inverse = jnp.exp(-log_rho)
        force_x = inverse * (cur_y * cz - cur_z * cy)
        force_y = inverse * (cur_z * cx - cur_x * cz)
        force_z = inverse * (cur_x * cy - cur_y * cx)

        pairs = [diffs[0][d] + diffs[4][d] for d in range(3)]
        rates = [
            advs[0] - 0.5 * (diffs[1][0] + diffs[2][1] + diffs[3][2]),
            advs[1] - (0.5 * sound_sq) * pairs[0] + force_x + (2.0 * rotation) * vy,
            advs[2] - (0.5 * sound_sq) * pairs[1] + force_y - ((2.0 - shear_rate) * rotation) * vx,
            advs[3] - (0.5 * sound_sq) * pairs[2] + force_z,
            advs[4] + resist * inverse * (cur_x * cur_x + cur_y * cur_y + cur_z * cur_z),
        ]

        w_y, z_y = w + y_behind(w), vz + y_behind(vz)
        bz_y, by_z = y_behind(bz), z_behind(by)
        emf_x = 0.125 * (
            (z_y + z_behind(z_y)) * (by + by_z) - (w_y + z_behind(w_y)) * (bz + bz_y)
        ) + resist * ((bz - bz_y) - (by - by_z))
        stretch = 0.25 * (sum_bx + y_behind(sum_bx))
        rates.append((z_ahead(emf_y) - emf_y) - (y_ahead(emf_z) - emf_z))
        rates.append(
            (emf_z_next - emf_z) - (z_ahead(emf_x) - emf_x) - (shear_rate * rotation) * stretch
        )
        rates.append((y_ahead(emf_x) - emf_x) - (emf_y_next - emf_y))
        emit(row, cur, rates)
        return cy, cz, cy_next, cz_next, emf_z_next, emf_y_next

    if last_row - first_row < 3:
        for row in range(first_row, last_row + 1):
            carry = one(row, carry)
        return
    lax.fori_loop(first_row, last_row + 1, one, carry, unroll=2)


def step_kernel(
    groups, radial, state_ref, table_ref, drift_ref, out_ref,
    grid_ref, moved_ref, first_ref, send, recv, local_sem,
):
    rows, fields, _, cols = state_ref.shape
    gather(state_ref, grid_ref, Copies(send, recv), local_sem, groups, radial)

    lane = lax.broadcasted_iota(jnp.int32, state_ref.shape[2:], 1)

    def turn(row, _):
        amount = table_ref[4, row]
        inside = lane < cols - amount
        low_side = lane < cols // 2
        blocks = [table_ref[k, row] for k in range(4)]
        for f in range(fields):
            before, here, after, beyond = [
                pltpu.roll(grid_ref[b, row, f], cols - amount, 1) for b in blocks
            ]
            moved_ref[row, f, :, :cols] = jnp.where(inside, here, after)
            moved_ref[row, f, :, cols:] = jnp.where(
                low_side, jnp.where(inside, after, beyond), jnp.where(inside, before, here)
            )
        return 0

    lax.fori_loop(0, rows + 2 * DEPTH, turn, 0)

    def drift_of(row):
        return drift_ref[row]

    def emit_first(row, cur, rates):
        for f in range(fields):
            first_ref[row, f] = cur[f] + time_step * rates[f]

    def emit_out(row, cur, rates):
        for f in range(fields):
            second = cur[f][:, :cols] + time_step * rates[f][:, :cols]
            out_ref[row - DEPTH, f] = 0.5 * (moved_ref[row, f, :, :cols] + second)

    def load_from(ref):
        return lambda row: [ref[row, f] for f in range(fields)]

    row_sweep(load_from(moved_ref), 1, rows + 2, drift_of, emit_first)
    row_sweep(load_from(first_ref), 2, rows + 1, drift_of, emit_out)


def gathered(state, residual, shift_rows, shear_offset):
    fields, vertical, rows, cols = state.shape
    groups, radial = lax.axis_size("gy"), lax.axis_size("gx")
    gx, gy = lax.axis_index("gx"), lax.axis_index("gy")
    cells_y = cols * groups
    wide = rows + 2 * DEPTH

    up = [(i, (i + 1) % radial) for i in range(radial)]
    down = [(target, source) for source, target in up]
    low = lax.ppermute(shift_rows[-DEPTH:], "gx", up)
    high = lax.ppermute(shift_rows[:DEPTH], "gx", down)
    offset = shear_offset[0]
    low = low - jnp.where(gx == 0, offset, 0)
    high = high + jnp.where(gx == radial - 1, offset, 0)
    amounts = jnp.concatenate([low, shift_rows, high])
    origin = (cols * gy - amounts) % cells_y
    block, part = origin // cols, origin % cols
    table = jnp.stack(
        [(block + groups - 1) % groups, block, (block + 1) % groups, (block + 2) % groups, part]
    )
    padded = jnp.concatenate([residual[-DEPTH:], residual, residual[:DEPTH]])
    drift = lax.dynamic_slice_in_dim(padded, gx * rows, wide)

    count = copy_count(groups // 2)
    out = pl.pallas_call(
        functools.partial(step_kernel, groups, radial),
        out_shape=jax.ShapeDtypeStruct((rows, fields, vertical, cols), jnp.float32),
        in_specs=[
            pl.BlockSpec(memory_space=pltpu.VMEM),
            pl.BlockSpec(memory_space=pltpu.SMEM),
            pl.BlockSpec(memory_space=pltpu.SMEM),
        ],
        out_specs=pl.BlockSpec(memory_space=pltpu.VMEM),
        scratch_shapes=[
            pltpu.VMEM((groups, wide, fields, vertical, cols), jnp.float32),
            pltpu.VMEM((wide, fields, vertical, 2 * cols), jnp.float32),
            pltpu.VMEM((wide, fields, vertical, 2 * cols), jnp.float32),
            pltpu.SemaphoreType.DMA((count,)),
            pltpu.SemaphoreType.DMA((count,)),
            pltpu.SemaphoreType.DMA,
        ],
        compiler_params=pltpu.CompilerParams(collective_id=0, has_side_effects=True),
    )(jnp.transpose(state, (2, 0, 1, 3)), table, drift)
    return jnp.transpose(out, (1, 2, 0, 3))


def spread_kernel(
    groups, radial, state_ref, shift_hbm, offset_hbm, residual_hbm, out_ref,
    shift_ref, offset_ref, residual_ref, taken_0, taken_1, taken_2, taken_3, turned_ref, edge_ref,
    shear_ref, moved_ref, own_edges, low_edges, high_edges, first_ref, windows_ref, drifts_ref, send, recv, local_sems,
):
    fields, vertical, rows, cols = state_ref.shape
    quarter = rows // 4
    taken = (taken_0, taken_1, taken_2, taken_3)
    cells_y = cols * groups
    gx, gy = lax.axis_index("gx"), lax.axis_index("gy")
    x_next = (lax.rem(gx + 1, radial), gy)
    x_prev = (lax.rem(gx + radial - 1, radial), gy)
    others = [(gx, lax.rem(gy + k, groups)) for k in range(1, groups)]
    first_x, last_x = gx == 0, gx == radial - 1
    not_first, not_last = gx > 0, gx < radial - 1
    out_sent, back_sent, edges_sent, shear_sent, ends_sent, down_sent, up_sent = range(7)
    back_got = {0: 4, 3: 5, 1: 6}
    edges_got, shear_got, ends_got, rows_got, sides_got = 7, 8, 9, (10, 11), (12, 13)

    def remote(source, target, device, sent, got):
        return pltpu.make_async_remote_copy(
            src_ref=source,
            dst_ref=target,
            send_sem=send.at[sent],
            recv_sem=recv.at[got],
            device_id=device,
            device_id_type=MESH,
        )

    def spread_out(source, target, sent, got):
        for other in others:
            remote(source(other[1]), target, other, sent, got).start()
        pltpu.make_async_copy(source(gy), target, recv.at[got]).start()

    def arrived(ref, got):
        pltpu.make_async_copy(ref, ref, recv.at[got]).wait()

    def left(ref, sent):
        pltpu.make_async_copy(ref, ref, send.at[sent]).wait()

    small = [
        pltpu.make_async_copy(source, target, local_sems.at[k])
        for k, (source, target) in enumerate(
            ((shift_hbm, shift_ref), (offset_hbm, offset_ref), (residual_hbm, residual_ref))
        )
    ]
    for copy in small:
        copy.start()
    barrier = pltpu.get_barrier_semaphore()
    for other in (*others, x_prev, x_next):
        pl.semaphore_signal(barrier, inc=1, device_id=other, device_id_type=MESH)
    pl.semaphore_wait(barrier, groups + 1)

    def quarter_rows(q):
        return pl.ds(q * quarter, quarter)

    for pair in ((0, 3), (1, 2)):
        for other in others:
            for q in pair:
                remote(
                    state_ref.at[other[1], :, quarter_rows(q)], taken[q].at[gy], other, out_sent, q
                ).start()
        for q in pair:
            pltpu.make_async_copy(
                state_ref.at[gy, :, quarter_rows(q)], taken[q].at[gy], recv.at[q]
            ).start()

    lane = lax.broadcasted_iota(jnp.int32, (vertical, cols), 1)
    empty = [jnp.zeros((vertical, cols), jnp.float32)] * groups

    def displace(block_of, amount, place, slot, packed):
        whole, part = amount // cols, amount % cols
        rolled = [
            pltpu.roll(block_of(lax.rem(k - whole + groups, groups)), part, 1)
            for k in range(groups)
        ]
        row = [jnp.where(lane < part, rolled[d - 1], rolled[d]) for d in range(groups)]
        mine = (lane >= 4 * place) & (lane < 4 * place + 4)
        result = []
        for d in range(groups):
            turned_ref[d, slot] = row[d]
            after = pltpu.roll(row[(d + 1) % groups], 4 * place, 1)
            before = pltpu.roll(row[d - 1], 4 * place + 4, 1)
            edges = jnp.where(lane < 4 * place + 2, after, before)
            result.append(jnp.where(mine, edges, packed[d]))
        return result

    def displace_quarter(q, packed):
        arrived(taken[q], q)
        for place in range(quarter):
            row = q * quarter + place
            packed = displace(
                lambda b: taken[q][b, :, place, :], shift_ref[row], row, row, packed
            )
        return packed

    def main_lanes(block, first_row, count):
        return moved_ref.at[block, pl.ds(first_row, count)]

    def send_back(q, count):
        span = pl.ds(q * quarter, count)
        spread_out(
            lambda d: turned_ref.at[d, span],
            main_lanes(gy, DEPTH + q * quarter, count),
            back_sent,
            back_got[q],
        )

    for copy in small:
        copy.wait()
    packed = displace_quarter(0, empty)
    packed = displace_quarter(3, packed)
    to_last = remote(turned_ref.at[:, pl.ds(0, DEPTH)], shear_ref, x_prev, ends_sent, ends_got)
    to_first = remote(
        turned_ref.at[:, pl.ds(rows - DEPTH, DEPTH)], shear_ref, x_next, ends_sent, ends_got
    )
    pl.when(first_x)(to_last.start)
    pl.when(last_x)(to_first.start)
    for q in (0, 3):
        send_back(q, quarter)

    low_row, high_row = 0, DEPTH + rows
    offset = offset_ref[0]
    for d in range(groups):
        edge_ref[d] = empty[0]

    def sheared(first_row, amount):
        arrived(shear_ref, ends_got)
        edges = empty
        for place in range(DEPTH):
            edges = displace(
                lambda b: shear_ref[b, place], amount, rows + place, rows + place, edges
            )
        for d in range(groups):
            edge_ref[d] = edges[d]
        spread_out(
            lambda d: turned_ref.at[d, pl.ds(rows, DEPTH)],
            main_lanes(gy, first_row, DEPTH),
            shear_sent,
            shear_got,
        )

    @pl.when(first_x)
    def _():
        sheared(low_row, lax.rem(cells_y - offset, cells_y))

    @pl.when(last_x)
    def _():
        sheared(high_row, offset)

    packed = displace_quarter(1, packed)
    packed = displace_quarter(2, packed)
    for d in range(groups):
        edge_ref[d] = jnp.where(lane < 4 * rows, packed[d], edge_ref[d])
    spread_out(lambda d: edge_ref.at[d], own_edges.at[gy], edges_sent, edges_got)

    every = slice(None)
    for q in (0, 3):
        arrived(main_lanes(every, DEPTH + q * quarter, quarter), back_got[q])
    rows_down = remote(
        main_lanes(every, DEPTH, DEPTH), main_lanes(every, high_row, DEPTH),
        x_prev, down_sent, rows_got[1],
    )
    rows_up = remote(
        main_lanes(every, rows, DEPTH), main_lanes(every, low_row, DEPTH),
        x_next, up_sent, rows_got[0],
    )
    edges_down = remote(own_edges, high_edges, x_prev, down_sent, sides_got[1])
    edges_up = remote(own_edges, low_edges, x_next, up_sent, sides_got[0])
    pl.when(not_first)(rows_down.start)
    pl.when(not_last)(rows_up.start)
    send_back(1, 2 * quarter)
    arrived(own_edges, edges_got)
    pl.when(not_first)(edges_down.start)
    pl.when(not_last)(edges_up.start)

    start = gx * rows - DEPTH + residual_ref.shape[0]

    def drift_of(row):
        return residual_ref[lax.rem(start + row, residual_ref.shape[0])]

    def emit_first(row, cur, rates):
        for f in range(fields):
            first_ref[row, f] = cur[f] + time_step * rates[f]

    def emit_out(row, cur, rates):
        for f in range(fields):
            second = cur[f] + time_step * rates[f]
            out_ref[f, :, row - DEPTH, :] = moved_ref[f, row] + second

    def stage_one(low, high):
        row_sweep(
            lambda row: [moved_ref[f, row] for f in range(fields)],
            DEPTH + low, DEPTH + high, drift_of, emit_first,
        )

    def stage_two(low, high):
        row_sweep(
            lambda row: [first_ref[row, f] for f in range(fields)],
            DEPTH + low, DEPTH + high, drift_of, emit_out,
        )

    windows = cols // WINDOW
    kept = windows - 2 * DEPTH
    starts = range(-DEPTH, rows - DEPTH, kept)

    def in_window(k, low, high):
        return (lane >= WINDOW * k + low) & (lane < WINDOW * k + high)

    def rows_of(start):
        return range(start, min(start + windows, rows + DEPTH))

    def window_drift(start):
        total = empty[0]
        for k, row in enumerate(rows_of(start)):
            total = jnp.where(in_window(k, 0, WINDOW), drift_of(DEPTH + row), total)
        return total

    def fill(i, first_row, count, edges_ref, first_place):
        for k, row in enumerate(rows_of(starts[i])):
            if not first_row <= row < first_row + count:
                continue
            base, place = WINDOW * k, first_place + row - first_row
            for f in range(fields):
                main, edges = moved_ref[f, DEPTH + row], edges_ref[f]
                value = jnp.where(
                    in_window(k, 0, 4),
                    pltpu.roll(main, (base + 4) % cols, 1),
                    jnp.where(
                        in_window(k, 4, 8),
                        pltpu.roll(edges, (base + 4 - 4 * place) % cols, 1),
                        pltpu.roll(main, (base + 8) % cols, 1),
                    ),
                )
                old = windows_ref[i, f]
                windows_ref[i, f] = jnp.where(in_window(k, 0, WINDOW), value, old)

    def fill_all(first_row, count, edges_ref, first_place):
        for i in range(len(starts)):
            fill(i, first_row, count, edges_ref, first_place)

    def window_step(values, drift):
        turned = [
            [pltpu.roll(a, (WINDOW * (1 - r)) % cols, 1) for a in values] for r in range(3)
        ]
        drifts = [pltpu.roll(drift, (WINDOW * (1 - r)) % cols, 1) for r in range(3)]
        got = []
        row_sweep(
            lambda r: turned[r], 1, 1, lambda r: drifts[r],
            lambda r, cur, rates: got.extend(a + time_step * b for a, b in zip(cur, rates)),
        )
        return got

    def window_stages(i):
        drift = drifts_ref[i]
        moved = [windows_ref[i, f] for f in range(fields)]
        second = window_step(window_step(moved, drift), drift)
        outer = (lane < 2) | (lane >= cols - 2)
        for k, row in enumerate(rows_of(starts[i])):
            if not DEPTH <= k < DEPTH + kept or row >= rows:
                continue
            base = WINDOW * k
            for f in range(fields):
                total = moved[f] + second[f]
                value = jnp.where(
                    lane < 2,
                    pltpu.roll(total, (cols - base - 8) % cols, 1),
                    pltpu.roll(total, (cols - base - 4) % cols, 1),
                )
                pltpu.store(out_ref.at[f, :, row, :], value, mask=outer)

    for i in range(len(starts)):
        drifts_ref[i] = window_drift(starts[i])
        for f in range(fields):
            windows_ref[i, f] = empty[0]
    stage_one(1, quarter - 2)
    stage_one(3 * quarter + 1, rows - 2)

    @pl.when(first_x)
    def _():
        arrived(main_lanes(every, low_row, DEPTH), shear_got)
        fill_all(-DEPTH, DEPTH, own_edges, rows)

    @pl.when(not_first)
    def _():
        rows_up.wait_recv()
        edges_up.wait_recv()
        fill_all(-DEPTH, DEPTH, low_edges, rows - DEPTH)

    @pl.when(last_x)
    def _():
        arrived(main_lanes(every, high_row, DEPTH), shear_got)
        fill_all(rows, DEPTH, own_edges, rows)

    @pl.when(not_last)
    def _():
        rows_down.wait_recv()
        edges_down.wait_recv()
        fill_all(rows, DEPTH, high_edges, 0)

    fill_all(0, quarter, own_edges, 0)
    fill_all(3 * quarter, quarter, own_edges, 3 * quarter)
    stage_one(-1, 0)
    stage_one(rows - 1, rows)
    stage_two(0, quarter - 3)
    stage_two(3 * quarter + 2, rows - 1)
    arrived(main_lanes(every, DEPTH + quarter, 2 * quarter), back_got[1])
    stage_one(quarter - 1, 3 * quarter)
    stage_two(quarter - 2, 3 * quarter + 1)
    fill_all(quarter, 2 * quarter, own_edges, quarter)
    for i in range(len(starts)):
        window_stages(i)

    away = pl.ds(0, groups - 1)
    left(state_ref.at[away], out_sent)
    left(turned_ref.at[away, pl.ds(0, rows)], back_sent)
    left(edge_ref.at[away], edges_sent)

    @pl.when(first_x | last_x)
    def _():
        left(shear_ref, ends_sent)
        left(turned_ref.at[away, pl.ds(rows, DEPTH)], shear_sent)

    @pl.when(not_first)
    def _():
        rows_down.wait_send()
        edges_down.wait_send()

    @pl.when(not_last)
    def _():
        rows_up.wait_send()
        edges_up.wait_send()


def spread(state, residual, shift_rows, shear_offset):
    fields, vertical, rows, cols = state.shape
    groups, radial = lax.axis_size("gy"), lax.axis_size("gx")
    wide = rows + 2 * DEPTH
    parts = len(range(0, rows, cols // WINDOW - 2 * DEPTH))
    anywhere = pl.BlockSpec(memory_space=pl.ANY)
    vmem = pl.BlockSpec(memory_space=pltpu.VMEM)
    edges = pltpu.VMEM((groups, vertical, cols), jnp.float32)
    out = pl.pallas_call(
        functools.partial(spread_kernel, groups, radial),
        out_shape=pltpu.VMEM(state.shape, jnp.float32),
        in_specs=[anywhere] * 4,
        out_specs=vmem,
        scratch_shapes=[
            pltpu.SMEM(shift_rows.shape, jnp.int32),
            pltpu.SMEM(shear_offset.shape, jnp.int32),
            pltpu.SMEM(residual.shape, jnp.float32),
            *[pltpu.VMEM((groups, vertical, rows // 4, cols), jnp.float32)] * 4,
            pltpu.VMEM((groups, rows + DEPTH, vertical, cols), jnp.float32),
            edges,
            pltpu.VMEM((groups, DEPTH, vertical, cols), jnp.float32),
            pltpu.VMEM((fields, wide, vertical, cols), jnp.float32),
            edges,
            edges,
            edges,
            pltpu.VMEM((wide, fields, vertical, cols), jnp.float32),
            pltpu.VMEM((parts, fields, vertical, cols), jnp.float32),
            pltpu.VMEM((parts, vertical, cols), jnp.float32),
            pltpu.SemaphoreType.DMA((7,)),
            pltpu.SemaphoreType.DMA((14,)),
            pltpu.SemaphoreType.DMA((3,)),
        ],
        compiler_params=pltpu.CompilerParams(collective_id=1, has_side_effects=True),
    )(state, shift_rows, shear_offset, residual)
    return 0.5 * out


def local(state, residual, shift_rows, shear_offset):
    fields, _, rows, cols = state.shape
    paired = lax.axis_size("gy") == fields and lax.axis_size("gx") > 2
    if paired and rows % 16 == 0 and 4 * (rows + DEPTH) <= cols:
        return spread(state, residual, shift_rows, shear_offset)
    return gathered(state, residual, shift_rows, shear_offset)


def solution(mesh):
    return jax.shard_map(
        local,
        mesh=mesh,
        in_specs=(P(None, None, "gx", "gy"), P(), P("gx"), P()),
        out_specs=P(None, None, "gx", "gy"),
        check_vma=False,
    )
```

```python
import functools

import jax
import jax.numpy as jnp
from jax import lax
from jax.experimental import pallas as pl
from jax.experimental.pallas import tpu as pltpu
from jax.sharding import PartitionSpec as P

time_step = 0.2
viscous = 0.1
resist = 0.1
sound_sq = 1.0
rotation = 0.5
shear_rate = 1.5

MESH = pl.DeviceIdType.MESH
DEPTH = 2
WINDOW = 12


class Copies:
    def __init__(self, send, recv):
        self.send, self.recv, self.made = send, recv, []

    def start(self, source, target, device):
        k = len(self.made)
        copy = pltpu.make_async_remote_copy(
            src_ref=source,
            dst_ref=target,
            send_sem=self.send.at[k],
            recv_sem=self.recv.at[k],
            device_id=device,
            device_id_type=MESH,
        )
        copy.start()
        self.made.append(copy)
        return copy


def copy_count(chips):
    return 8 + sum(10 if 2 * s < chips else 6 for s in range(1, chips // 2 + 1)) + 8 * (chips // 2 + 1)


def gather(state_ref, grid_ref, copies, local_sem, groups, radial):
    rows = state_ref.shape[0]
    chips = groups // 2
    half = rows // 2
    gx, gy = lax.axis_index("gx"), lax.axis_index("gy")
    chip, core = gy // 2, gy % 2

    def at_chip(offset):
        return lax.rem(chip + offset + chips, chips) * 2 + core

    right, left = (gx, at_chip(1)), (gx, at_chip(-1))
    twin = (gx, chip * 2 + (1 - core))
    x_next = (lax.rem(gx + 1, radial), gy)
    x_prev = (lax.rem(gx + radial - 1, radial), gy)

    barrier = pltpu.get_barrier_semaphore()
    for other in (right, left, twin, x_next, x_prev):
        pl.semaphore_signal(barrier, inc=1, device_id=other, device_id_type=MESH)
    pl.semaphore_wait(barrier, 5)

    def piece(block, part):
        return grid_ref.at[block, pl.ds(DEPTH + part * half, half)]

    def low_rows(block):
        return grid_ref.at[block, pl.ds(0, DEPTH)]

    def high_rows(block):
        return grid_ref.at[block, pl.ds(DEPTH + rows, DEPTH)]

    def send_rows(block, part, source):
        if part == 0:
            edge = source.at[pl.ds(0, DEPTH)]
            return block, 0, copies.start(edge, high_rows(block), x_prev)
        edge = source.at[pl.ds(half - DEPTH, DEPTH)]
        return block, 1, copies.start(edge, low_rows(block), x_next)

    to_twin = []

    def pass_rows(sent):
        for block, part, copy in sent:
            copy.wait_recv()
            strip = high_rows(block) if part == 0 else low_rows(block)
            to_twin.append(copies.start(strip, strip, twin))

    own = [state_ref.at[pl.ds(0, half)], state_ref.at[pl.ds(half, half)]]
    keep = pltpu.make_async_copy(state_ref, grid_ref.at[gy, pl.ds(DEPTH, rows)], local_sem)

    flights = []
    order = [(0, 0), (1, 1), (0, 1), (1, 0)] if chips > 2 else [(0, 0), (1, 1)]
    for way, part in order:
        flights.append(
            (way, part, copies.start(own[part], piece(gy, part), right if way == 0 else left))
        )
    sent = [send_rows(gy, part, own[part]) for part in (0, 1)]
    for part in (0, 1):
        to_twin.append(copies.start(own[part], piece(gy, part), twin))
    keep.start()
    pass_rows(sent)
    for step in range(1, chips // 2 + 1):
        later, sent = [], []
        for way, part, copy in flights:
            block = at_chip(-step if way == 0 else step)
            copy.wait_recv()
            ref = piece(block, part)
            if 2 * (step + 1) < chips or (2 * (step + 1) == chips and part == way):
                later.append((way, part, copies.start(ref, ref, right if way == 0 else left)))
            to_twin.append(copies.start(ref, ref, twin))
            sent.append(send_rows(block, part, ref))
        pass_rows(sent)
        flights = later
    keep.wait()
    for copy in to_twin:
        copy.wait_recv()
    for copy in copies.made:
        copy.wait_send()


def row_sweep(load, first_row, last_row, drift_of, emit):
    def y_ahead(a):
        return pltpu.roll(a, a.shape[1] - 1, 1)

    def y_behind(a):
        return pltpu.roll(a, 1, 1)

    def z_ahead(a):
        return pltpu.roll(a, a.shape[0] - 1, 0)

    def z_behind(a):
        return pltpu.roll(a, 1, 0)

    def cells(by, bz):
        return 0.5 * (by + y_ahead(by)), 0.5 * (bz + z_ahead(bz))

    def radial_edges(prev, cur, prev_drift, cur_drift):
        sum_x = prev[1] + cur[1]
        sum_w = (prev[2] + prev_drift) + (cur[2] + cur_drift)
        sum_z = prev[3] + cur[3]
        bx, by, bz = cur[5], cur[6], cur[7]
        bx_y, bx_z = y_behind(bx), z_behind(bx)
        emf_z = 0.125 * (
            (sum_w + y_behind(sum_w)) * (bx + bx_y) - (sum_x + y_behind(sum_x)) * (by + prev[6])
        ) + resist * ((by - prev[6]) - (bx - bx_y))
        emf_y = 0.125 * (
            (sum_x + z_behind(sum_x)) * (bz + prev[7]) - (sum_z + z_behind(sum_z)) * (bx + bx_z)
        ) + resist * ((bx - bx_z) - (bz - prev[7]))
        return emf_z, emf_y

    start_prev, start_cur = load(first_row - 1), load(first_row)
    carry = (
        *cells(start_prev[6], start_prev[7]),
        *cells(start_cur[6], start_cur[7]),
        *radial_edges(start_prev, start_cur, drift_of(first_row - 1), drift_of(first_row)),
    )

    def one(row, carry):
        cy_prev, cz_prev, cy, cz, emf_z, emf_y = carry
        prev, cur, nxt = load(row - 1), load(row), load(row + 1)
        drift = drift_of(row)
        log_rho, vx, vy, vz, ent, bx, by, bz = cur
        w = vy + drift
        cy_next, cz_next = cells(nxt[6], nxt[7])
        emf_z_next, emf_y_next = radial_edges(cur, nxt, drift, drift_of(row + 1))

        half_x, half_w, half_z = 0.5 * vx, 0.5 * w, 0.5 * vz
        diffs, advs = [], []
        for f in range(5):
            a = cur[f]
            ya, yb, za, zb = y_ahead(a), y_behind(a), z_ahead(a), z_behind(a)
            dx, dy, dz = nxt[f] - prev[f], ya - yb, za - zb
            lap = ((nxt[f] + prev[f]) + (ya + yb) + (za + zb)) - 6.0 * a
            diffs.append((dx, dy, dz))
            advs.append(viscous * lap - (half_x * dx + half_w * dy + half_z * dz))

        sum_bx = bx + nxt[5]
        cx = 0.5 * sum_bx
        cur_x = 0.5 * ((y_ahead(cz) - y_behind(cz)) - (z_ahead(cy) - z_behind(cy)))
        cur_y = 0.5 * ((z_ahead(cx) - z_behind(cx)) - (cz_next - cz_prev))
        cur_z = 0.5 * ((cy_next - cy_prev) - (y_ahead(cx) - y_behind(cx)))
        inverse = jnp.exp(-log_rho)
        force_x = inverse * (cur_y * cz - cur_z * cy)
        force_y = inverse * (cur_z * cx - cur_x * cz)
        force_z = inverse * (cur_x * cy - cur_y * cx)

        pairs = [diffs[0][d] + diffs[4][d] for d in range(3)]
        rates = [
            advs[0] - 0.5 * (diffs[1][0] + diffs[2][1] + diffs[3][2]),
            advs[1] - (0.5 * sound_sq) * pairs[0] + force_x + (2.0 * rotation) * vy,
            advs[2] - (0.5 * sound_sq) * pairs[1] + force_y - ((2.0 - shear_rate) * rotation) * vx,
            advs[3] - (0.5 * sound_sq) * pairs[2] + force_z,
            advs[4] + resist * inverse * (cur_x * cur_x + cur_y * cur_y + cur_z * cur_z),
        ]

        w_y, z_y = w + y_behind(w), vz + y_behind(vz)
        bz_y, by_z = y_behind(bz), z_behind(by)
        emf_x = 0.125 * (
            (z_y + z_behind(z_y)) * (by + by_z) - (w_y + z_behind(w_y)) * (bz + bz_y)
        ) + resist * ((bz - bz_y) - (by - by_z))
        stretch = 0.25 * (sum_bx + y_behind(sum_bx))
        rates.append((z_ahead(emf_y) - emf_y) - (y_ahead(emf_z) - emf_z))
        rates.append(
            (emf_z_next - emf_z) - (z_ahead(emf_x) - emf_x) - (shear_rate * rotation) * stretch
        )
        rates.append((y_ahead(emf_x) - emf_x) - (emf_y_next - emf_y))
        emit(row, cur, rates)
        return cy, cz, cy_next, cz_next, emf_z_next, emf_y_next

    if last_row - first_row < 3:
        for row in range(first_row, last_row + 1):
            carry = one(row, carry)
        return
    lax.fori_loop(first_row, last_row + 1, one, carry, unroll=4)


def step_kernel(
    groups, radial, state_ref, table_ref, drift_ref, out_ref,
    grid_ref, moved_ref, first_ref, send, recv, local_sem,
):
    rows, fields, _, cols = state_ref.shape
    gather(state_ref, grid_ref, Copies(send, recv), local_sem, groups, radial)

    lane = lax.broadcasted_iota(jnp.int32, state_ref.shape[2:], 1)

    def turn(row, _):
        amount = table_ref[4, row]
        inside = lane < cols - amount
        low_side = lane < cols // 2
        blocks = [table_ref[k, row] for k in range(4)]
        for f in range(fields):
            before, here, after, beyond = [
                pltpu.roll(grid_ref[b, row, f], cols - amount, 1) for b in blocks
            ]
            moved_ref[row, f, :, :cols] = jnp.where(inside, here, after)
            moved_ref[row, f, :, cols:] = jnp.where(
                low_side, jnp.where(inside, after, beyond), jnp.where(inside, before, here)
            )
        return 0

    lax.fori_loop(0, rows + 2 * DEPTH, turn, 0)

    def drift_of(row):
        return drift_ref[row]

    def emit_first(row, cur, rates):
        for f in range(fields):
            first_ref[row, f] = cur[f] + time_step * rates[f]

    def emit_out(row, cur, rates):
        for f in range(fields):
            second = cur[f][:, :cols] + time_step * rates[f][:, :cols]
            out_ref[row - DEPTH, f] = 0.5 * (moved_ref[row, f, :, :cols] + second)

    def load_from(ref):
        return lambda row: [ref[row, f] for f in range(fields)]

    row_sweep(load_from(moved_ref), 1, rows + 2, drift_of, emit_first)
    row_sweep(load_from(first_ref), 2, rows + 1, drift_of, emit_out)


def gathered(state, residual, shift_rows, shear_offset):
    fields, vertical, rows, cols = state.shape
    groups, radial = lax.axis_size("gy"), lax.axis_size("gx")
    gx, gy = lax.axis_index("gx"), lax.axis_index("gy")
    cells_y = cols * groups
    wide = rows + 2 * DEPTH

    up = [(i, (i + 1) % radial) for i in range(radial)]
    down = [(target, source) for source, target in up]
    low = lax.ppermute(shift_rows[-DEPTH:], "gx", up)
    high = lax.ppermute(shift_rows[:DEPTH], "gx", down)
    offset = shear_offset[0]
    low = low - jnp.where(gx == 0, offset, 0)
    high = high + jnp.where(gx == radial - 1, offset, 0)
    amounts = jnp.concatenate([low, shift_rows, high])
    origin = (cols * gy - amounts) % cells_y
    block, part = origin // cols, origin % cols
    table = jnp.stack(
        [(block + groups - 1) % groups, block, (block + 1) % groups, (block + 2) % groups, part]
    )
    padded = jnp.concatenate([residual[-DEPTH:], residual, residual[:DEPTH]])
    drift = lax.dynamic_slice_in_dim(padded, gx * rows, wide)

    count = copy_count(groups // 2)
    out = pl.pallas_call(
        functools.partial(step_kernel, groups, radial),
        out_shape=jax.ShapeDtypeStruct((rows, fields, vertical, cols), jnp.float32),
        in_specs=[
            pl.BlockSpec(memory_space=pltpu.VMEM),
            pl.BlockSpec(memory_space=pltpu.SMEM),
            pl.BlockSpec(memory_space=pltpu.SMEM),
        ],
        out_specs=pl.BlockSpec(memory_space=pltpu.VMEM),
        scratch_shapes=[
            pltpu.VMEM((groups, wide, fields, vertical, cols), jnp.float32),
            pltpu.VMEM((wide, fields, vertical, 2 * cols), jnp.float32),
            pltpu.VMEM((wide, fields, vertical, 2 * cols), jnp.float32),
            pltpu.SemaphoreType.DMA((count,)),
            pltpu.SemaphoreType.DMA((count,)),
            pltpu.SemaphoreType.DMA,
        ],
        compiler_params=pltpu.CompilerParams(collective_id=0, has_side_effects=True),
    )(jnp.transpose(state, (2, 0, 1, 3)), table, drift)
    return jnp.transpose(out, (1, 2, 0, 3))


def spread_kernel(
    groups, radial, state_ref, shift_hbm, offset_hbm, residual_hbm, out_ref,
    shift_ref, offset_ref, residual_ref, taken_0, taken_1, taken_2, taken_3, turned_ref, edge_ref,
    shear_ref, moved_ref, own_edges, low_edges, high_edges, first_ref, total_ref, windows_ref,
    drifts_ref, send, recv, local_sems,
):
    fields, vertical, rows, cols = state_ref.shape
    quarter = rows // 4
    taken = (taken_0, taken_1, taken_2, taken_3)
    cells_y = cols * groups
    gx, gy = lax.axis_index("gx"), lax.axis_index("gy")
    x_next = (lax.rem(gx + 1, radial), gy)
    x_prev = (lax.rem(gx + radial - 1, radial), gy)
    others = [(gx, lax.rem(gy + k, groups)) for k in range(1, groups)]
    first_x, last_x = gx == 0, gx == radial - 1
    not_first, not_last = gx > 0, gx < radial - 1
    out_sent, back_sent, edges_sent, shear_sent, ends_sent, down_sent, up_sent = range(7)
    back_got = {0: 4, 3: 5, 1: 6}
    edges_got, shear_got, ends_got, rows_got, sides_got = 7, 8, 9, (10, 11), (12, 13)

    def remote(source, target, device, sent, got):
        return pltpu.make_async_remote_copy(
            src_ref=source,
            dst_ref=target,
            send_sem=send.at[sent],
            recv_sem=recv.at[got],
            device_id=device,
            device_id_type=MESH,
        )

    def spread_out(source, target, sent, got):
        for other in others:
            remote(source(other[1]), target, other, sent, got).start()
        pltpu.make_async_copy(source(gy), target, recv.at[got]).start()

    def arrived(ref, got):
        pltpu.make_async_copy(ref, ref, recv.at[got]).wait()

    def left(ref, sent):
        pltpu.make_async_copy(ref, ref, send.at[sent]).wait()

    small = [
        pltpu.make_async_copy(source, target, local_sems.at[k])
        for k, (source, target) in enumerate(
            ((shift_hbm, shift_ref), (offset_hbm, offset_ref), (residual_hbm, residual_ref))
        )
    ]
    for copy in small:
        copy.start()
    barrier = pltpu.get_barrier_semaphore()
    for other in (*others, x_prev, x_next):
        pl.semaphore_signal(barrier, inc=1, device_id=other, device_id_type=MESH)
    pl.semaphore_wait(barrier, groups + 1)

    def quarter_rows(q):
        return pl.ds(q * quarter, quarter)

    for pair in ((0, 3), (1, 2)):
        for other in others:
            for q in pair:
                remote(
                    state_ref.at[other[1], :, quarter_rows(q)], taken[q].at[gy], other, out_sent, q
                ).start()
        for q in pair:
            pltpu.make_async_copy(
                state_ref.at[gy, :, quarter_rows(q)], taken[q].at[gy], recv.at[q]
            ).start()

    lane = lax.broadcasted_iota(jnp.int32, (vertical, cols), 1)
    empty = [jnp.zeros((vertical, cols), jnp.float32)] * groups

    def displace(block_of, amount, place, slot, packed):
        whole, part = amount // cols, amount % cols
        rolled = [
            pltpu.roll(block_of(lax.rem(k - whole + groups, groups)), part, 1)
            for k in range(groups)
        ]
        row = [jnp.where(lane < part, rolled[d - 1], rolled[d]) for d in range(groups)]
        mine = (lane >= 4 * place) & (lane < 4 * place + 4)
        result = []
        for d in range(groups):
            turned_ref[d, slot] = row[d]
            after = pltpu.roll(row[(d + 1) % groups], 4 * place, 1)
            before = pltpu.roll(row[d - 1], 4 * place + 4, 1)
            edges = jnp.where(lane < 4 * place + 2, after, before)
            result.append(jnp.where(mine, edges, packed[d]))
        return result

    def displace_quarter(q, packed):
        arrived(taken[q], q)
        for place in range(quarter):
            row = q * quarter + place
            packed = displace(
                lambda b: taken[q][b, :, place, :], shift_ref[row], row, row, packed
            )
        return packed

    def main_lanes(block, first_row, count):
        return moved_ref.at[block, pl.ds(first_row, count)]

    def send_back(q, count):
        span = pl.ds(q * quarter, count)
        spread_out(
            lambda d: turned_ref.at[d, span],
            main_lanes(gy, DEPTH + q * quarter, count),
            back_sent,
            back_got[q],
        )

    for copy in small:
        copy.wait()
    packed = displace_quarter(0, empty)
    packed = displace_quarter(3, packed)
    to_last = remote(turned_ref.at[:, pl.ds(0, DEPTH)], shear_ref, x_prev, ends_sent, ends_got)
    to_first = remote(
        turned_ref.at[:, pl.ds(rows - DEPTH, DEPTH)], shear_ref, x_next, ends_sent, ends_got
    )
    pl.when(first_x)(to_last.start)
    pl.when(last_x)(to_first.start)
    for q in (0, 3):
        send_back(q, quarter)

    low_row, high_row = 0, DEPTH + rows
    offset = offset_ref[0]
    for d in range(groups):
        edge_ref[d] = empty[0]

    def sheared(first_row, amount):
        arrived(shear_ref, ends_got)
        edges = empty
        for place in range(DEPTH):
            edges = displace(
                lambda b: shear_ref[b, place], amount, rows + place, rows + place, edges
            )
        for d in range(groups):
            edge_ref[d] = edges[d]
        spread_out(
            lambda d: turned_ref.at[d, pl.ds(rows, DEPTH)],
            main_lanes(gy, first_row, DEPTH),
            shear_sent,
            shear_got,
        )

    @pl.when(first_x)
    def _():
        sheared(low_row, lax.rem(cells_y - offset, cells_y))

    @pl.when(last_x)
    def _():
        sheared(high_row, offset)

    packed = displace_quarter(1, packed)
    packed = displace_quarter(2, packed)
    for d in range(groups):
        edge_ref[d] = jnp.where(lane < 4 * rows, packed[d], edge_ref[d])
    spread_out(lambda d: edge_ref.at[d], own_edges.at[gy], edges_sent, edges_got)

    every = slice(None)
    for q in (0, 3):
        arrived(main_lanes(every, DEPTH + q * quarter, quarter), back_got[q])
    rows_down = remote(
        main_lanes(every, DEPTH, DEPTH), main_lanes(every, high_row, DEPTH),
        x_prev, down_sent, rows_got[1],
    )
    rows_up = remote(
        main_lanes(every, rows, DEPTH), main_lanes(every, low_row, DEPTH),
        x_next, up_sent, rows_got[0],
    )
    edges_down = remote(own_edges, high_edges, x_prev, down_sent, sides_got[1])
    edges_up = remote(own_edges, low_edges, x_next, up_sent, sides_got[0])
    pl.when(not_first)(rows_down.start)
    pl.when(not_last)(rows_up.start)
    send_back(1, 2 * quarter)
    arrived(own_edges, edges_got)
    pl.when(not_first)(edges_down.start)
    pl.when(not_last)(edges_up.start)

    start = gx * rows - DEPTH + residual_ref.shape[0]

    def drift_of(row):
        return residual_ref[lax.rem(start + row, residual_ref.shape[0])]

    windows = cols // WINDOW
    kept = windows - 2 * DEPTH

    def emit_first(row, cur, rates):
        for f in range(fields):
            first_ref[row, f] = cur[f] + time_step * rates[f]

    def emit_out(row, cur, rates):
        for f in range(fields):
            second = cur[f] + time_step * rates[f]
            total_ref[row - DEPTH, f] = moved_ref[f, row] + second

    def emit_whole(row, cur, rates):
        i = (row - DEPTH) // kept
        base = WINDOW * (row - i * kept)
        for f in range(fields):
            sides = windows_ref[i, f]
            low = pltpu.roll(sides, 2 * cols - base - 8, 1)
            high = pltpu.roll(sides, 2 * cols - base - 4, 1)
            total = moved_ref[f, row] + (cur[f] + time_step * rates[f])
            middle = jnp.where(lane >= cols - 2, high, total)
            out_ref[f, :, row - DEPTH, :] = jnp.where(lane < 2, low, middle)

    def stage_one(low, high):
        row_sweep(
            lambda row: [moved_ref[f, row] for f in range(fields)],
            DEPTH + low, DEPTH + high, drift_of, emit_first,
        )

    def stage_two(low, high, emit):
        row_sweep(
            lambda row: [first_ref[row, f] for f in range(fields)],
            DEPTH + low, DEPTH + high, drift_of, emit,
        )

    starts = range(-DEPTH, rows - DEPTH, kept)

    def in_window(k, low, high):
        return (lane >= WINDOW * k + low) & (lane < WINDOW * k + high)

    def rows_of(start):
        return range(start, min(start + windows, rows + DEPTH))

    def window_drift(start):
        total = empty[0]
        for k, row in enumerate(rows_of(start)):
            total = jnp.where(in_window(k, 0, WINDOW), drift_of(DEPTH + row), total)
        return total

    def fill_all(first_row, count, edges_ref, first_place):
        for i in range(len(starts)):
            held = [
                (k, row) for k, row in enumerate(rows_of(starts[i]))
                if first_row <= row < first_row + count
            ]
            for f in range(fields):
                packed, value = edges_ref[f], windows_ref[i, f]
                for k, row in held:
                    base, place = WINDOW * k, first_place + row - first_row
                    main = moved_ref[f, DEPTH + row]
                    for low, source, turn in (
                        (0, main, base + 4), (4, packed, base + 4 - 4 * place), (8, main, base + 8)
                    ):
                        value = jnp.where(
                            in_window(k, low, low + 4), pltpu.roll(source, turn % cols, 1), value
                        )
                if held:
                    windows_ref[i, f] = value

    def window_step(values, drift):
        turned = [
            [pltpu.roll(a, (WINDOW * (1 - r)) % cols, 1) for a in values] for r in range(3)
        ]
        drifts = [pltpu.roll(drift, (WINDOW * (1 - r)) % cols, 1) for r in range(3)]
        got = []
        row_sweep(
            lambda r: turned[r], 1, 1, lambda r: drifts[r],
            lambda r, cur, rates: got.extend(a + time_step * b for a, b in zip(cur, rates)),
        )
        return got

    def window_stages(i):
        drift = drifts_ref[i]
        moved = [windows_ref[i, f] for f in range(fields)]
        second = window_step(window_step(moved, drift), drift)
        for f in range(fields):
            windows_ref[i, f] = moved[f] + second[f]

    def finish(row):
        i = row // kept
        base = WINDOW * (row - i * kept + DEPTH)
        for f in range(fields):
            sides = windows_ref[i, f]
            low = pltpu.roll(sides, (cols - base - 8) % cols, 1)
            high = pltpu.roll(sides, (cols - base - 4) % cols, 1)
            middle = jnp.where(lane >= cols - 2, high, total_ref[row, f])
            out_ref[f, :, row, :] = jnp.where(lane < 2, low, middle)

    for i in range(len(starts)):
        drifts_ref[i] = window_drift(starts[i])
        for f in range(fields):
            windows_ref[i, f] = empty[0]
    stage_one(1, quarter - 2)
    stage_one(3 * quarter + 1, rows - 2)

    @pl.when(first_x)
    def _():
        arrived(main_lanes(every, low_row, DEPTH), shear_got)
        fill_all(-DEPTH, DEPTH, own_edges, rows)

    @pl.when(not_first)
    def _():
        rows_up.wait_recv()
        edges_up.wait_recv()
        fill_all(-DEPTH, DEPTH, low_edges, rows - DEPTH)

    @pl.when(last_x)
    def _():
        arrived(main_lanes(every, high_row, DEPTH), shear_got)
        fill_all(rows, DEPTH, own_edges, rows)

    @pl.when(not_last)
    def _():
        rows_down.wait_recv()
        edges_down.wait_recv()
        fill_all(rows, DEPTH, high_edges, 0)

    fill_all(0, quarter, own_edges, 0)
    fill_all(3 * quarter, quarter, own_edges, 3 * quarter)
    stage_one(-1, 0)
    stage_one(rows - 1, rows)
    stage_two(0, quarter - 3, emit_out)
    stage_two(3 * quarter + 2, rows - 1, emit_out)
    arrived(main_lanes(every, DEPTH + quarter, 2 * quarter), back_got[1])
    fill_all(quarter, 2 * quarter, own_edges, quarter)
    for i in range(len(starts)):
        window_stages(i)
    stage_one(quarter - 1, 3 * quarter)
    stage_two(quarter - 2, 3 * quarter + 1, emit_whole)
    for row in (*range(quarter - 2), *range(3 * quarter + 2, rows)):
        finish(row)

    away = pl.ds(0, groups - 1)
    left(state_ref.at[away], out_sent)
    left(turned_ref.at[away, pl.ds(0, rows)], back_sent)
    left(edge_ref.at[away], edges_sent)

    @pl.when(first_x | last_x)
    def _():
        left(shear_ref, ends_sent)
        left(turned_ref.at[away, pl.ds(rows, DEPTH)], shear_sent)

    @pl.when(not_first)
    def _():
        rows_down.wait_send()
        edges_down.wait_send()

    @pl.when(not_last)
    def _():
        rows_up.wait_send()
        edges_up.wait_send()


def spread(state, residual, shift_rows, shear_offset):
    fields, vertical, rows, cols = state.shape
    groups, radial = lax.axis_size("gy"), lax.axis_size("gx")
    wide = rows + 2 * DEPTH
    parts = len(range(0, rows, cols // WINDOW - 2 * DEPTH))
    anywhere = pl.BlockSpec(memory_space=pl.ANY)
    vmem = pl.BlockSpec(memory_space=pltpu.VMEM)
    edges = pltpu.VMEM((groups, vertical, cols), jnp.float32)
    out = pl.pallas_call(
        functools.partial(spread_kernel, groups, radial),
        out_shape=pltpu.VMEM(state.shape, jnp.float32),
        in_specs=[anywhere] * 4,
        out_specs=vmem,
        scratch_shapes=[
            pltpu.SMEM(shift_rows.shape, jnp.int32),
            pltpu.SMEM(shear_offset.shape, jnp.int32),
            pltpu.SMEM(residual.shape, jnp.float32),
            *[pltpu.VMEM((groups, vertical, rows // 4, cols), jnp.float32)] * 4,
            pltpu.VMEM((groups, rows + DEPTH, vertical, cols), jnp.float32),
            edges,
            pltpu.VMEM((groups, DEPTH, vertical, cols), jnp.float32),
            pltpu.VMEM((fields, wide, vertical, cols), jnp.float32),
            edges,
            edges,
            edges,
            pltpu.VMEM((wide, fields, vertical, cols), jnp.float32),
            pltpu.VMEM((rows, fields, vertical, cols), jnp.float32),
            pltpu.VMEM((parts, fields, vertical, cols), jnp.float32),
            pltpu.VMEM((parts, vertical, cols), jnp.float32),
            pltpu.SemaphoreType.DMA((7,)),
            pltpu.SemaphoreType.DMA((14,)),
            pltpu.SemaphoreType.DMA((3,)),
        ],
        compiler_params=pltpu.CompilerParams(collective_id=1, has_side_effects=True),
    )(state, shift_rows, shear_offset, residual)
    return 0.5 * out


def local(state, residual, shift_rows, shear_offset):
    fields, _, rows, cols = state.shape
    paired = lax.axis_size("gy") == fields and lax.axis_size("gx") > 2
    if paired and rows % 16 == 0 and 4 * (rows + DEPTH) <= cols:
        return spread(state, residual, shift_rows, shear_offset)
    return gathered(state, residual, shift_rows, shear_offset)


def solution(mesh):
    return jax.shard_map(
        local,
        mesh=mesh,
        in_specs=(P(None, None, "gx", "gy"), P(), P("gx"), P()),
        out_specs=P(None, None, "gx", "gy"),
        check_vma=False,
    )
```

```python
import functools

import jax
import jax.numpy as jnp
from jax import lax
from jax.experimental import pallas as pl
from jax.experimental.pallas import tpu as pltpu
from jax.sharding import PartitionSpec as P

time_step = 0.2
viscous = 0.1
resist = 0.1
sound_sq = 1.0
rotation = 0.5
shear_rate = 1.5

MESH = pl.DeviceIdType.MESH
DEPTH = 2
WINDOW = 12
EARLY = (1, 0)


def late_rows(rows):
    return range(rows // 4 + EARLY[0], 3 * rows // 4 - EARLY[1])


class Copies:
    def __init__(self, send, recv):
        self.send, self.recv, self.made = send, recv, []

    def start(self, source, target, device):
        k = len(self.made)
        copy = pltpu.make_async_remote_copy(
            src_ref=source,
            dst_ref=target,
            send_sem=self.send.at[k],
            recv_sem=self.recv.at[k],
            device_id=device,
            device_id_type=MESH,
        )
        copy.start()
        self.made.append(copy)
        return copy


def copy_count(chips):
    return 8 + sum(10 if 2 * s < chips else 6 for s in range(1, chips // 2 + 1)) + 8 * (chips // 2 + 1)


def gather(state_ref, grid_ref, copies, local_sem, groups, radial):
    rows = state_ref.shape[0]
    chips = groups // 2
    half = rows // 2
    gx, gy = lax.axis_index("gx"), lax.axis_index("gy")
    chip, core = gy // 2, gy % 2

    def at_chip(offset):
        return lax.rem(chip + offset + chips, chips) * 2 + core

    right, left = (gx, at_chip(1)), (gx, at_chip(-1))
    twin = (gx, chip * 2 + (1 - core))
    x_next = (lax.rem(gx + 1, radial), gy)
    x_prev = (lax.rem(gx + radial - 1, radial), gy)

    barrier = pltpu.get_barrier_semaphore()
    for other in (right, left, twin, x_next, x_prev):
        pl.semaphore_signal(barrier, inc=1, device_id=other, device_id_type=MESH)
    pl.semaphore_wait(barrier, 5)

    def piece(block, part):
        return grid_ref.at[block, pl.ds(DEPTH + part * half, half)]

    def low_rows(block):
        return grid_ref.at[block, pl.ds(0, DEPTH)]

    def high_rows(block):
        return grid_ref.at[block, pl.ds(DEPTH + rows, DEPTH)]

    def send_rows(block, part, source):
        if part == 0:
            edge = source.at[pl.ds(0, DEPTH)]
            return block, 0, copies.start(edge, high_rows(block), x_prev)
        edge = source.at[pl.ds(half - DEPTH, DEPTH)]
        return block, 1, copies.start(edge, low_rows(block), x_next)

    to_twin = []

    def pass_rows(sent):
        for block, part, copy in sent:
            copy.wait_recv()
            strip = high_rows(block) if part == 0 else low_rows(block)
            to_twin.append(copies.start(strip, strip, twin))

    own = [state_ref.at[pl.ds(0, half)], state_ref.at[pl.ds(half, half)]]
    keep = pltpu.make_async_copy(state_ref, grid_ref.at[gy, pl.ds(DEPTH, rows)], local_sem)

    flights = []
    order = [(0, 0), (1, 1), (0, 1), (1, 0)] if chips > 2 else [(0, 0), (1, 1)]
    for way, part in order:
        flights.append(
            (way, part, copies.start(own[part], piece(gy, part), right if way == 0 else left))
        )
    sent = [send_rows(gy, part, own[part]) for part in (0, 1)]
    for part in (0, 1):
        to_twin.append(copies.start(own[part], piece(gy, part), twin))
    keep.start()
    pass_rows(sent)
    for step in range(1, chips // 2 + 1):
        later, sent = [], []
        for way, part, copy in flights:
            block = at_chip(-step if way == 0 else step)
            copy.wait_recv()
            ref = piece(block, part)
            if 2 * (step + 1) < chips or (2 * (step + 1) == chips and part == way):
                later.append((way, part, copies.start(ref, ref, right if way == 0 else left)))
            to_twin.append(copies.start(ref, ref, twin))
            sent.append(send_rows(block, part, ref))
        pass_rows(sent)
        flights = later
    keep.wait()
    for copy in to_twin:
        copy.wait_recv()
    for copy in copies.made:
        copy.wait_send()


def row_sweep(load, first_row, last_row, drift_of, emit):
    def y_ahead(a):
        return pltpu.roll(a, a.shape[1] - 1, 1)

    def y_behind(a):
        return pltpu.roll(a, 1, 1)

    def z_ahead(a):
        return pltpu.roll(a, a.shape[0] - 1, 0)

    def z_behind(a):
        return pltpu.roll(a, 1, 0)

    def cells(by, bz):
        return 0.5 * (by + y_ahead(by)), 0.5 * (bz + z_ahead(bz))

    def radial_edges(prev, cur, prev_drift, cur_drift):
        sum_x = prev[1] + cur[1]
        sum_w = (prev[2] + prev_drift) + (cur[2] + cur_drift)
        sum_z = prev[3] + cur[3]
        bx, by, bz = cur[5], cur[6], cur[7]
        bx_y, bx_z = y_behind(bx), z_behind(bx)
        emf_z = 0.125 * (
            (sum_w + y_behind(sum_w)) * (bx + bx_y) - (sum_x + y_behind(sum_x)) * (by + prev[6])
        ) + resist * ((by - prev[6]) - (bx - bx_y))
        emf_y = 0.125 * (
            (sum_x + z_behind(sum_x)) * (bz + prev[7]) - (sum_z + z_behind(sum_z)) * (bx + bx_z)
        ) + resist * ((bx - bx_z) - (bz - prev[7]))
        return emf_z, emf_y

    start_prev, start_cur = load(first_row - 1), load(first_row)
    carry = (
        *cells(start_prev[6], start_prev[7]),
        *cells(start_cur[6], start_cur[7]),
        *radial_edges(start_prev, start_cur, drift_of(first_row - 1), drift_of(first_row)),
    )

    def one(row, carry):
        cy_prev, cz_prev, cy, cz, emf_z, emf_y = carry
        prev, cur, nxt = load(row - 1), load(row), load(row + 1)
        drift = drift_of(row)
        log_rho, vx, vy, vz, ent, bx, by, bz = cur
        w = vy + drift
        cy_next, cz_next = cells(nxt[6], nxt[7])
        emf_z_next, emf_y_next = radial_edges(cur, nxt, drift, drift_of(row + 1))

        half_x, half_w, half_z = 0.5 * vx, 0.5 * w, 0.5 * vz
        diffs, advs = [], []
        for f in range(5):
            a = cur[f]
            ya, yb, za, zb = y_ahead(a), y_behind(a), z_ahead(a), z_behind(a)
            dx, dy, dz = nxt[f] - prev[f], ya - yb, za - zb
            lap = ((nxt[f] + prev[f]) + (ya + yb) + (za + zb)) - 6.0 * a
            diffs.append((dx, dy, dz))
            advs.append(viscous * lap - (half_x * dx + half_w * dy + half_z * dz))

        sum_bx = bx + nxt[5]
        cx = 0.5 * sum_bx
        cur_x = 0.5 * ((y_ahead(cz) - y_behind(cz)) - (z_ahead(cy) - z_behind(cy)))
        cur_y = 0.5 * ((z_ahead(cx) - z_behind(cx)) - (cz_next - cz_prev))
        cur_z = 0.5 * ((cy_next - cy_prev) - (y_ahead(cx) - y_behind(cx)))
        inverse = jnp.exp(-log_rho)
        force_x = inverse * (cur_y * cz - cur_z * cy)
        force_y = inverse * (cur_z * cx - cur_x * cz)
        force_z = inverse * (cur_x * cy - cur_y * cx)

        pairs = [diffs[0][d] + diffs[4][d] for d in range(3)]
        rates = [
            advs[0] - 0.5 * (diffs[1][0] + diffs[2][1] + diffs[3][2]),
            advs[1] - (0.5 * sound_sq) * pairs[0] + force_x + (2.0 * rotation) * vy,
            advs[2] - (0.5 * sound_sq) * pairs[1] + force_y - ((2.0 - shear_rate) * rotation) * vx,
            advs[3] - (0.5 * sound_sq) * pairs[2] + force_z,
            advs[4] + resist * inverse * (cur_x * cur_x + cur_y * cur_y + cur_z * cur_z),
        ]

        w_y, z_y = w + y_behind(w), vz + y_behind(vz)
        bz_y, by_z = y_behind(bz), z_behind(by)
        emf_x = 0.125 * (
            (z_y + z_behind(z_y)) * (by + by_z) - (w_y + z_behind(w_y)) * (bz + bz_y)
        ) + resist * ((bz - bz_y) - (by - by_z))
        stretch = 0.25 * (sum_bx + y_behind(sum_bx))
        rates.append((z_ahead(emf_y) - emf_y) - (y_ahead(emf_z) - emf_z))
        rates.append(
            (emf_z_next - emf_z) - (z_ahead(emf_x) - emf_x) - (shear_rate * rotation) * stretch
        )
        rates.append((y_ahead(emf_x) - emf_x) - (emf_y_next - emf_y))
        emit(row, cur, rates)
        return cy, cz, cy_next, cz_next, emf_z_next, emf_y_next

    if last_row - first_row < 3:
        for row in range(first_row, last_row + 1):
            carry = one(row, carry)
        return
    lax.fori_loop(first_row, last_row + 1, one, carry, unroll=4)


def step_kernel(
    groups, radial, state_ref, table_ref, drift_ref, out_ref,
    grid_ref, moved_ref, first_ref, send, recv, local_sem,
):
    rows, fields, _, cols = state_ref.shape
    gather(state_ref, grid_ref, Copies(send, recv), local_sem, groups, radial)

    lane = lax.broadcasted_iota(jnp.int32, state_ref.shape[2:], 1)

    def turn(row, _):
        amount = table_ref[4, row]
        inside = lane < cols - amount
        low_side = lane < cols // 2
        blocks = [table_ref[k, row] for k in range(4)]
        for f in range(fields):
            before, here, after, beyond = [
                pltpu.roll(grid_ref[b, row, f], cols - amount, 1) for b in blocks
            ]
            moved_ref[row, f, :, :cols] = jnp.where(inside, here, after)
            moved_ref[row, f, :, cols:] = jnp.where(
                low_side, jnp.where(inside, after, beyond), jnp.where(inside, before, here)
            )
        return 0

    lax.fori_loop(0, rows + 2 * DEPTH, turn, 0)

    def drift_of(row):
        return drift_ref[row]

    def emit_first(row, cur, rates):
        for f in range(fields):
            first_ref[row, f] = cur[f] + time_step * rates[f]

    def emit_out(row, cur, rates):
        for f in range(fields):
            second = cur[f][:, :cols] + time_step * rates[f][:, :cols]
            out_ref[row - DEPTH, f] = 0.5 * (moved_ref[row, f, :, :cols] + second)

    def load_from(ref):
        return lambda row: [ref[row, f] for f in range(fields)]

    row_sweep(load_from(moved_ref), 1, rows + 2, drift_of, emit_first)
    row_sweep(load_from(first_ref), 2, rows + 1, drift_of, emit_out)


def gathered(state, residual, shift_rows, shear_offset):
    fields, vertical, rows, cols = state.shape
    groups, radial = lax.axis_size("gy"), lax.axis_size("gx")
    gx, gy = lax.axis_index("gx"), lax.axis_index("gy")
    cells_y = cols * groups
    wide = rows + 2 * DEPTH

    up = [(i, (i + 1) % radial) for i in range(radial)]
    down = [(target, source) for source, target in up]
    low = lax.ppermute(shift_rows[-DEPTH:], "gx", up)
    high = lax.ppermute(shift_rows[:DEPTH], "gx", down)
    offset = shear_offset[0]
    low = low - jnp.where(gx == 0, offset, 0)
    high = high + jnp.where(gx == radial - 1, offset, 0)
    amounts = jnp.concatenate([low, shift_rows, high])
    origin = (cols * gy - amounts) % cells_y
    block, part = origin // cols, origin % cols
    table = jnp.stack(
        [(block + groups - 1) % groups, block, (block + 1) % groups, (block + 2) % groups, part]
    )
    padded = jnp.concatenate([residual[-DEPTH:], residual, residual[:DEPTH]])
    drift = lax.dynamic_slice_in_dim(padded, gx * rows, wide)

    count = copy_count(groups // 2)
    out = pl.pallas_call(
        functools.partial(step_kernel, groups, radial),
        out_shape=jax.ShapeDtypeStruct((rows, fields, vertical, cols), jnp.float32),
        in_specs=[
            pl.BlockSpec(memory_space=pltpu.VMEM),
            pl.BlockSpec(memory_space=pltpu.SMEM),
            pl.BlockSpec(memory_space=pltpu.SMEM),
        ],
        out_specs=pl.BlockSpec(memory_space=pltpu.VMEM),
        scratch_shapes=[
            pltpu.VMEM((groups, wide, fields, vertical, cols), jnp.float32),
            pltpu.VMEM((wide, fields, vertical, 2 * cols), jnp.float32),
            pltpu.VMEM((wide, fields, vertical, 2 * cols), jnp.float32),
            pltpu.SemaphoreType.DMA((count,)),
            pltpu.SemaphoreType.DMA((count,)),
            pltpu.SemaphoreType.DMA,
        ],
        compiler_params=pltpu.CompilerParams(collective_id=0, has_side_effects=True),
    )(jnp.transpose(state, (2, 0, 1, 3)), table, drift)
    return jnp.transpose(out, (1, 2, 0, 3))


def spread_kernel(
    groups, radial, state_ref, shift_hbm, offset_hbm, residual_hbm, out_ref,
    shift_ref, offset_ref, residual_ref, taken_0, taken_1, taken_2, taken_3, turned_ref, edge_ref,
    shear_ref, moved_ref, own_edges, low_edges, high_edges, first_ref, windows_ref, drifts_ref, send, recv, local_sems,
):
    fields, vertical, rows, cols = state_ref.shape
    quarter = rows // 4
    taken = (taken_0, taken_1, taken_2, taken_3)
    late = late_rows(rows)
    others_start = WINDOW * len(late)
    short = [row for row in range(rows + DEPTH) if row not in late]
    lane_of = {row: WINDOW * k for k, row in enumerate(late)}
    lane_of.update({row: others_start + 4 * k for k, row in enumerate(short)})
    cells_y = cols * groups
    gx, gy = lax.axis_index("gx"), lax.axis_index("gy")
    x_next = (lax.rem(gx + 1, radial), gy)
    x_prev = (lax.rem(gx + radial - 1, radial), gy)
    others = [(gx, lax.rem(gy + k, groups)) for k in range(1, groups)]
    first_x, last_x = gx == 0, gx == radial - 1
    not_first, not_last = gx > 0, gx < radial - 1
    out_sent, back_sent, edges_sent, shear_sent, ends_sent, down_sent, up_sent = range(7)
    back_got = (4, 5, 6, 14, 15)
    edges_got, shear_got, ends_got, rows_got, sides_got = 7, 8, 9, (10, 11), (12, 13)

    def remote(source, target, device, sent, got):
        return pltpu.make_async_remote_copy(
            src_ref=source,
            dst_ref=target,
            send_sem=send.at[sent],
            recv_sem=recv.at[got],
            device_id=device,
            device_id_type=MESH,
        )

    def spread_out(source, target, sent, got):
        for other in others:
            remote(source(other[1]), target, other, sent, got).start()
        pltpu.make_async_copy(source(gy), target, recv.at[got]).start()

    def arrived(ref, got):
        pltpu.make_async_copy(ref, ref, recv.at[got]).wait()

    def left(ref, sent):
        pltpu.make_async_copy(ref, ref, send.at[sent]).wait()

    small = [
        pltpu.make_async_copy(source, target, local_sems.at[k])
        for k, (source, target) in enumerate(
            ((shift_hbm, shift_ref), (offset_hbm, offset_ref), (residual_hbm, residual_ref))
        )
    ]
    for copy in small:
        copy.start()
    barrier = pltpu.get_barrier_semaphore()
    for other in (*others, x_prev, x_next):
        pl.semaphore_signal(barrier, inc=1, device_id=other, device_id_type=MESH)
    pl.semaphore_wait(barrier, groups + 1)

    def quarter_rows(q):
        return pl.ds(q * quarter, quarter)

    for pair in ((0, 3), (1, 2)):
        for other in others:
            for q in pair:
                remote(
                    state_ref.at[other[1], :, quarter_rows(q)], taken[q].at[gy], other, out_sent, q
                ).start()
        for q in pair:
            pltpu.make_async_copy(
                state_ref.at[gy, :, quarter_rows(q)], taken[q].at[gy], recv.at[q]
            ).start()

    lane = lax.broadcasted_iota(jnp.int32, (vertical, cols), 1)
    empty = [jnp.zeros((vertical, cols), jnp.float32)] * groups

    def displace(block_of, amount, slot, packed):
        whole, part = amount // cols, amount % cols
        rolled = [
            pltpu.roll(block_of(lax.rem(k - whole + groups, groups)), part, 1)
            for k in range(groups)
        ]
        row = [jnp.where(lane < part, rolled[d - 1], rolled[d]) for d in range(groups)]
        base, long = lane_of[slot], slot in late
        width = WINDOW if long else 4
        mine = (lane >= base) & (lane < base + width)
        result = []
        for d in range(groups):
            turned_ref[d, slot] = row[d]
            before, here, after = row[d - 1], row[d], row[(d + 1) % groups]
            if long:
                after = jnp.where(lane < cols // 2, after, here)
                before = jnp.where(lane < cols // 2, here, before)
            turn = base + 4
            edges = jnp.where(
                lane < base + width // 2,
                pltpu.roll(after, turn % cols if long else base, 1),
                pltpu.roll(before, (base + width - 4 if long else base + 4) % cols, 1),
            )
            result.append(jnp.where(mine, edges, packed[d]))
        return result

    def displace_quarter(q, packed):
        arrived(taken[q], q)
        for place in range(quarter):
            row = q * quarter + place
            packed = displace(
                lambda b: taken[q][b, :, place, :], shift_ref[row], row, packed
            )
        return packed

    def main_lanes(block, first_row, count):
        return moved_ref.at[block, pl.ds(first_row, count)]

    pieces = (
        (0, quarter),
        (3 * quarter, quarter),
        (quarter, EARLY[0]),
        (3 * quarter - EARLY[1], EARLY[1]),
        (late[0], len(late)),
    )

    def send_back(piece):
        first, count = pieces[piece]
        if count:
            spread_out(
                lambda d: turned_ref.at[d, pl.ds(first, count)],
                main_lanes(gy, DEPTH + first, count),
                back_sent,
                back_got[piece],
            )

    def wait_back(piece):
        first, count = pieces[piece]
        if count:
            arrived(main_lanes(slice(None), DEPTH + first, count), back_got[piece])

    for copy in small:
        copy.wait()
    packed = displace_quarter(0, empty)
    packed = displace_quarter(3, packed)
    to_last = remote(turned_ref.at[:, pl.ds(0, DEPTH)], shear_ref, x_prev, ends_sent, ends_got)
    to_first = remote(
        turned_ref.at[:, pl.ds(rows - DEPTH, DEPTH)], shear_ref, x_next, ends_sent, ends_got
    )
    pl.when(first_x)(to_last.start)
    pl.when(last_x)(to_first.start)
    for piece in (0, 1):
        send_back(piece)

    low_row, high_row = 0, DEPTH + rows
    offset = offset_ref[0]
    for d in range(groups):
        edge_ref[d] = empty[0]

    def sheared(first_row, amount):
        arrived(shear_ref, ends_got)
        edges = empty
        for place in range(DEPTH):
            edges = displace(
                lambda b: shear_ref[b, place], amount, rows + place, edges
            )
        for d in range(groups):
            edge_ref[d] = edges[d]
        spread_out(
            lambda d: turned_ref.at[d, pl.ds(rows, DEPTH)],
            main_lanes(gy, first_row, DEPTH),
            shear_sent,
            shear_got,
        )

    @pl.when(first_x)
    def _():
        sheared(low_row, lax.rem(cells_y - offset, cells_y))

    @pl.when(last_x)
    def _():
        sheared(high_row, offset)

    packed = displace_quarter(1, packed)
    packed = displace_quarter(2, packed)
    for d in range(groups):
        edge_ref[d] = jnp.where(lane < lane_of[rows], packed[d], edge_ref[d])
    spread_out(lambda d: edge_ref.at[d], own_edges.at[gy], edges_sent, edges_got)
    for piece in (2, 3):
        send_back(piece)

    every = slice(None)
    for piece in (0, 1):
        wait_back(piece)
    rows_down = remote(
        main_lanes(every, DEPTH, DEPTH), main_lanes(every, high_row, DEPTH),
        x_prev, down_sent, rows_got[1],
    )
    rows_up = remote(
        main_lanes(every, rows, DEPTH), main_lanes(every, low_row, DEPTH),
        x_next, up_sent, rows_got[0],
    )
    edges_down = remote(own_edges, high_edges, x_prev, down_sent, sides_got[1])
    edges_up = remote(own_edges, low_edges, x_next, up_sent, sides_got[0])
    pl.when(not_first)(rows_down.start)
    pl.when(not_last)(rows_up.start)
    send_back(4)
    arrived(own_edges, edges_got)
    pl.when(not_first)(edges_down.start)
    pl.when(not_last)(edges_up.start)

    start = gx * rows - DEPTH + residual_ref.shape[0]

    def drift_of(row):
        return residual_ref[lax.rem(start + row, residual_ref.shape[0])]

    windows = cols // WINDOW
    kept = windows - 2 * DEPTH

    def emit_first(row, cur, rates):
        for f in range(fields):
            first_ref[row, f] = cur[f] + time_step * rates[f]

    def emit_whole(row, cur, rates):
        i = (row - DEPTH) // kept
        base = WINDOW * (row - i * kept)
        for f in range(fields):
            sides = windows_ref[i, f]
            low = pltpu.roll(sides, 2 * cols - base - 8, 1)
            high = pltpu.roll(sides, 2 * cols - base - 4, 1)
            total = moved_ref[f, row] + (cur[f] + time_step * rates[f])
            middle = jnp.where(lane >= cols - 2, high, total)
            out_ref[f, :, row - DEPTH, :] = jnp.where(lane < 2, low, middle)

    def stage_one(low, high):
        row_sweep(
            lambda row: [moved_ref[f, row] for f in range(fields)],
            DEPTH + low, DEPTH + high, drift_of, emit_first,
        )

    def stage_two(low, high):
        row_sweep(
            lambda row: [first_ref[row, f] for f in range(fields)],
            DEPTH + low, DEPTH + high, drift_of, emit_whole,
        )

    starts = range(-DEPTH, rows - DEPTH, kept)

    def in_window(k, low, high):
        return (lane >= WINDOW * k + low) & (lane < WINDOW * k + high)

    def rows_of(start):
        return range(start, min(start + windows, rows + DEPTH))

    def window_drift(start):
        total = empty[0]
        for k, row in enumerate(rows_of(start)):
            total = jnp.where(in_window(k, 0, WINDOW), drift_of(DEPTH + row), total)
        return total

    def fill_all(first_row, count, edges_ref, first_place):
        for i in range(len(starts)):
            held = [
                (k, row) for k, row in enumerate(rows_of(starts[i]))
                if first_row <= row < first_row + count and row not in late
            ]
            for f in range(fields):
                packed, value = edges_ref[f], windows_ref[i, f]
                for k, row in held:
                    base, from_lane = WINDOW * k, lane_of[first_place + row - first_row]
                    main = moved_ref[f, DEPTH + row]
                    for low, source, turn in (
                        (0, main, base + 4), (4, packed, base + 4 - from_lane), (8, main, base + 8)
                    ):
                        value = jnp.where(
                            in_window(k, low, low + 4), pltpu.roll(source, turn % cols, 1), value
                        )
                if held:
                    windows_ref[i, f] = value

    def fill_late():
        for i in range(len(starts)):
            held = [k for k, row in enumerate(rows_of(starts[i])) if row in late]
            if not held:
                continue
            from_lane = lane_of[starts[i] + held[0]]
            mine = (lane >= WINDOW * held[0]) & (lane < WINDOW * (held[-1] + 1))
            for f in range(fields):
                value = pltpu.roll(own_edges[f], (WINDOW * held[0] - from_lane) % cols, 1)
                windows_ref[i, f] = jnp.where(mine, value, windows_ref[i, f])

    def window_step(values, drift):
        turned = [
            [pltpu.roll(a, (WINDOW * (1 - r)) % cols, 1) for a in values] for r in range(3)
        ]
        drifts = [pltpu.roll(drift, (WINDOW * (1 - r)) % cols, 1) for r in range(3)]
        got = []
        row_sweep(
            lambda r: turned[r], 1, 1, lambda r: drifts[r],
            lambda r, cur, rates: got.extend(a + time_step * b for a, b in zip(cur, rates)),
        )
        return got

    def window_stages(i):
        drift = drifts_ref[i]
        moved = [windows_ref[i, f] for f in range(fields)]
        second = window_step(window_step(moved, drift), drift)
        for f in range(fields):
            windows_ref[i, f] = moved[f] + second[f]

    for i in range(len(starts)):
        drifts_ref[i] = window_drift(starts[i])
        for f in range(fields):
            windows_ref[i, f] = empty[0]
    fill_late()
    for piece in (2, 3):
        wait_back(piece)
    fill_all(0, rows, own_edges, 0)
    stage_one(1, late[0] - 2)
    stage_one(late[-1] + 2, rows - 2)

    @pl.when(first_x)
    def _():
        arrived(main_lanes(every, low_row, DEPTH), shear_got)
        fill_all(-DEPTH, DEPTH, own_edges, rows)

    @pl.when(not_first)
    def _():
        rows_up.wait_recv()
        edges_up.wait_recv()
        fill_all(-DEPTH, DEPTH, low_edges, rows - DEPTH)

    @pl.when(last_x)
    def _():
        arrived(main_lanes(every, high_row, DEPTH), shear_got)
        fill_all(rows, DEPTH, own_edges, rows)

    @pl.when(not_last)
    def _():
        rows_down.wait_recv()
        edges_down.wait_recv()
        fill_all(rows, DEPTH, high_edges, 0)

    for i in range(len(starts)):
        window_stages(i)
    stage_one(-1, 0)
    stage_one(rows - 1, rows)
    stage_two(0, late[0] - 3)
    stage_two(late[-1] + 3, rows - 1)
    wait_back(4)
    stage_one(late[0] - 1, late[-1] + 1)
    stage_two(late[0] - 2, late[-1] + 2)

    away = pl.ds(0, groups - 1)
    left(state_ref.at[away], out_sent)
    left(turned_ref.at[away, pl.ds(0, rows)], back_sent)
    left(edge_ref.at[away], edges_sent)

    @pl.when(first_x | last_x)
    def _():
        left(shear_ref, ends_sent)
        left(turned_ref.at[away, pl.ds(rows, DEPTH)], shear_sent)

    @pl.when(not_first)
    def _():
        rows_down.wait_send()
        edges_down.wait_send()

    @pl.when(not_last)
    def _():
        rows_up.wait_send()
        edges_up.wait_send()


def spread(state, residual, shift_rows, shear_offset):
    fields, vertical, rows, cols = state.shape
    groups, radial = lax.axis_size("gy"), lax.axis_size("gx")
    wide = rows + 2 * DEPTH
    parts = len(range(0, rows, cols // WINDOW - 2 * DEPTH))
    anywhere = pl.BlockSpec(memory_space=pl.ANY)
    vmem = pl.BlockSpec(memory_space=pltpu.VMEM)
    edges = pltpu.VMEM((groups, vertical, cols), jnp.float32)
    out = pl.pallas_call(
        functools.partial(spread_kernel, groups, radial),
        out_shape=pltpu.VMEM(state.shape, jnp.float32),
        in_specs=[anywhere] * 4,
        out_specs=vmem,
        scratch_shapes=[
            pltpu.SMEM(shift_rows.shape, jnp.int32),
            pltpu.SMEM(shear_offset.shape, jnp.int32),
            pltpu.SMEM(residual.shape, jnp.float32),
            *[pltpu.VMEM((groups, vertical, rows // 4, cols), jnp.float32)] * 4,
            pltpu.VMEM((groups, rows + DEPTH, vertical, cols), jnp.float32),
            edges,
            pltpu.VMEM((groups, DEPTH, vertical, cols), jnp.float32),
            pltpu.VMEM((fields, wide, vertical, cols), jnp.float32),
            edges,
            edges,
            edges,
            pltpu.VMEM((wide, fields, vertical, cols), jnp.float32),
            pltpu.VMEM((parts, fields, vertical, cols), jnp.float32),
            pltpu.VMEM((parts, vertical, cols), jnp.float32),
            pltpu.SemaphoreType.DMA((7,)),
            pltpu.SemaphoreType.DMA((16,)),
            pltpu.SemaphoreType.DMA((3,)),
        ],
        compiler_params=pltpu.CompilerParams(collective_id=1, has_side_effects=True),
    )(state, shift_rows, shear_offset, residual)
    return 0.5 * out


def local(state, residual, shift_rows, shear_offset):
    fields, _, rows, cols = state.shape
    paired = lax.axis_size("gy") == fields and lax.axis_size("gx") > 2
    late = len(late_rows(rows))
    if paired and rows % 16 == 0 and WINDOW * late + 4 * (rows + DEPTH - late) <= cols:
        return spread(state, residual, shift_rows, shear_offset)
    return gathered(state, residual, shift_rows, shear_offset)


def solution(mesh):
    return jax.shard_map(
        local,
        mesh=mesh,
        in_specs=(P(None, None, "gx", "gy"), P(), P("gx"), P()),
        out_specs=P(None, None, "gx", "gy"),
        check_vma=False,
    )
```

```python
import functools

import jax
import jax.numpy as jnp
from jax import lax
from jax.experimental import pallas as pl
from jax.experimental.pallas import tpu as pltpu
from jax.sharding import PartitionSpec as P

time_step = 0.2
viscous = 0.1
resist = 0.1
sound_sq = 1.0
rotation = 0.5
shear_rate = 1.5

MESH = pl.DeviceIdType.MESH
DEPTH = 2
WINDOW = 12
EARLY = (1, 0)


def late_rows(rows):
    return range(rows // 4 + EARLY[0], 3 * rows // 4 - EARLY[1])


class Copies:
    def __init__(self, send, recv):
        self.send, self.recv, self.made = send, recv, []

    def start(self, source, target, device):
        k = len(self.made)
        copy = pltpu.make_async_remote_copy(
            src_ref=source,
            dst_ref=target,
            send_sem=self.send.at[k],
            recv_sem=self.recv.at[k],
            device_id=device,
            device_id_type=MESH,
        )
        copy.start()
        self.made.append(copy)
        return copy


def copy_count(chips):
    return 8 + sum(10 if 2 * s < chips else 6 for s in range(1, chips // 2 + 1)) + 8 * (chips // 2 + 1)


def gather(state_ref, grid_ref, copies, local_sem, groups, radial):
    rows = state_ref.shape[0]
    chips = groups // 2
    half = rows // 2
    gx, gy = lax.axis_index("gx"), lax.axis_index("gy")
    chip, core = gy // 2, gy % 2

    def at_chip(offset):
        return lax.rem(chip + offset + chips, chips) * 2 + core

    right, left = (gx, at_chip(1)), (gx, at_chip(-1))
    twin = (gx, chip * 2 + (1 - core))
    x_next = (lax.rem(gx + 1, radial), gy)
    x_prev = (lax.rem(gx + radial - 1, radial), gy)

    barrier = pltpu.get_barrier_semaphore()
    for other in (right, left, twin, x_next, x_prev):
        pl.semaphore_signal(barrier, inc=1, device_id=other, device_id_type=MESH)
    pl.semaphore_wait(barrier, 5)

    def piece(block, part):
        return grid_ref.at[block, pl.ds(DEPTH + part * half, half)]

    def low_rows(block):
        return grid_ref.at[block, pl.ds(0, DEPTH)]

    def high_rows(block):
        return grid_ref.at[block, pl.ds(DEPTH + rows, DEPTH)]

    def send_rows(block, part, source):
        if part == 0:
            edge = source.at[pl.ds(0, DEPTH)]
            return block, 0, copies.start(edge, high_rows(block), x_prev)
        edge = source.at[pl.ds(half - DEPTH, DEPTH)]
        return block, 1, copies.start(edge, low_rows(block), x_next)

    to_twin = []

    def pass_rows(sent):
        for block, part, copy in sent:
            copy.wait_recv()
            strip = high_rows(block) if part == 0 else low_rows(block)
            to_twin.append(copies.start(strip, strip, twin))

    own = [state_ref.at[pl.ds(0, half)], state_ref.at[pl.ds(half, half)]]
    keep = pltpu.make_async_copy(state_ref, grid_ref.at[gy, pl.ds(DEPTH, rows)], local_sem)

    flights = []
    order = [(0, 0), (1, 1), (0, 1), (1, 0)] if chips > 2 else [(0, 0), (1, 1)]
    for way, part in order:
        flights.append(
            (way, part, copies.start(own[part], piece(gy, part), right if way == 0 else left))
        )
    sent = [send_rows(gy, part, own[part]) for part in (0, 1)]
    for part in (0, 1):
        to_twin.append(copies.start(own[part], piece(gy, part), twin))
    keep.start()
    pass_rows(sent)
    for step in range(1, chips // 2 + 1):
        later, sent = [], []
        for way, part, copy in flights:
            block = at_chip(-step if way == 0 else step)
            copy.wait_recv()
            ref = piece(block, part)
            if 2 * (step + 1) < chips or (2 * (step + 1) == chips and part == way):
                later.append((way, part, copies.start(ref, ref, right if way == 0 else left)))
            to_twin.append(copies.start(ref, ref, twin))
            sent.append(send_rows(block, part, ref))
        pass_rows(sent)
        flights = later
    keep.wait()
    for copy in to_twin:
        copy.wait_recv()
    for copy in copies.made:
        copy.wait_send()


def row_sweep(load, first_row, last_row, drift_of, emit, unroll=4):
    def y_ahead(a):
        return pltpu.roll(a, a.shape[1] - 1, 1)

    def y_behind(a):
        return pltpu.roll(a, 1, 1)

    def z_ahead(a):
        return pltpu.roll(a, a.shape[0] - 1, 0)

    def z_behind(a):
        return pltpu.roll(a, 1, 0)

    def cells(by, bz):
        return 0.5 * (by + y_ahead(by)), 0.5 * (bz + z_ahead(bz))

    def radial_edges(prev, cur, prev_drift, cur_drift):
        sum_x = prev[1] + cur[1]
        sum_w = (prev[2] + prev_drift) + (cur[2] + cur_drift)
        sum_z = prev[3] + cur[3]
        bx, by, bz = cur[5], cur[6], cur[7]
        bx_y, bx_z = y_behind(bx), z_behind(bx)
        emf_z = 0.125 * (
            (sum_w + y_behind(sum_w)) * (bx + bx_y) - (sum_x + y_behind(sum_x)) * (by + prev[6])
        ) + resist * ((by - prev[6]) - (bx - bx_y))
        emf_y = 0.125 * (
            (sum_x + z_behind(sum_x)) * (bz + prev[7]) - (sum_z + z_behind(sum_z)) * (bx + bx_z)
        ) + resist * ((bx - bx_z) - (bz - prev[7]))
        return emf_z, emf_y

    start_prev, start_cur = load(first_row - 1), load(first_row)
    carry = (
        *cells(start_prev[6], start_prev[7]),
        *cells(start_cur[6], start_cur[7]),
        *radial_edges(start_prev, start_cur, drift_of(first_row - 1), drift_of(first_row)),
    )

    def one(row, carry):
        cy_prev, cz_prev, cy, cz, emf_z, emf_y = carry
        prev, cur, nxt = load(row - 1), load(row), load(row + 1)
        drift = drift_of(row)
        log_rho, vx, vy, vz, ent, bx, by, bz = cur
        w = vy + drift
        cy_next, cz_next = cells(nxt[6], nxt[7])
        emf_z_next, emf_y_next = radial_edges(cur, nxt, drift, drift_of(row + 1))

        half_x, half_w, half_z = 0.5 * vx, 0.5 * w, 0.5 * vz
        diffs, advs = [], []
        for f in range(5):
            a = cur[f]
            ya, yb, za, zb = y_ahead(a), y_behind(a), z_ahead(a), z_behind(a)
            dx, dy, dz = nxt[f] - prev[f], ya - yb, za - zb
            lap = ((nxt[f] + prev[f]) + (ya + yb) + (za + zb)) - 6.0 * a
            diffs.append((dx, dy, dz))
            advs.append(viscous * lap - (half_x * dx + half_w * dy + half_z * dz))

        sum_bx = bx + nxt[5]
        cx = 0.5 * sum_bx
        cur_x = 0.5 * ((y_ahead(cz) - y_behind(cz)) - (z_ahead(cy) - z_behind(cy)))
        cur_y = 0.5 * ((z_ahead(cx) - z_behind(cx)) - (cz_next - cz_prev))
        cur_z = 0.5 * ((cy_next - cy_prev) - (y_ahead(cx) - y_behind(cx)))
        inverse = jnp.exp(-log_rho)
        force_x = inverse * (cur_y * cz - cur_z * cy)
        force_y = inverse * (cur_z * cx - cur_x * cz)
        force_z = inverse * (cur_x * cy - cur_y * cx)

        pairs = [diffs[0][d] + diffs[4][d] for d in range(3)]
        rates = [
            advs[0] - 0.5 * (diffs[1][0] + diffs[2][1] + diffs[3][2]),
            advs[1] - (0.5 * sound_sq) * pairs[0] + force_x + (2.0 * rotation) * vy,
            advs[2] - (0.5 * sound_sq) * pairs[1] + force_y - ((2.0 - shear_rate) * rotation) * vx,
            advs[3] - (0.5 * sound_sq) * pairs[2] + force_z,
            advs[4] + resist * inverse * (cur_x * cur_x + cur_y * cur_y + cur_z * cur_z),
        ]

        w_y, z_y = w + y_behind(w), vz + y_behind(vz)
        bz_y, by_z = y_behind(bz), z_behind(by)
        emf_x = 0.125 * (
            (z_y + z_behind(z_y)) * (by + by_z) - (w_y + z_behind(w_y)) * (bz + bz_y)
        ) + resist * ((bz - bz_y) - (by - by_z))
        stretch = 0.25 * (sum_bx + y_behind(sum_bx))
        rates.append((z_ahead(emf_y) - emf_y) - (y_ahead(emf_z) - emf_z))
        rates.append(
            (emf_z_next - emf_z) - (z_ahead(emf_x) - emf_x) - (shear_rate * rotation) * stretch
        )
        rates.append((y_ahead(emf_x) - emf_x) - (emf_y_next - emf_y))
        emit(row, cur, rates)
        return cy, cz, cy_next, cz_next, emf_z_next, emf_y_next

    if last_row - first_row < 3:
        for row in range(first_row, last_row + 1):
            carry = one(row, carry)
        return
    lax.fori_loop(first_row, last_row + 1, one, carry, unroll=unroll)


def step_kernel(
    groups, radial, state_ref, table_ref, drift_ref, out_ref,
    grid_ref, moved_ref, first_ref, send, recv, local_sem,
):
    rows, fields, _, cols = state_ref.shape
    gather(state_ref, grid_ref, Copies(send, recv), local_sem, groups, radial)

    lane = lax.broadcasted_iota(jnp.int32, state_ref.shape[2:], 1)

    def turn(row, _):
        amount = table_ref[4, row]
        inside = lane < cols - amount
        low_side = lane < cols // 2
        blocks = [table_ref[k, row] for k in range(4)]
        for f in range(fields):
            before, here, after, beyond = [
                pltpu.roll(grid_ref[b, row, f], cols - amount, 1) for b in blocks
            ]
            moved_ref[row, f, :, :cols] = jnp.where(inside, here, after)
            moved_ref[row, f, :, cols:] = jnp.where(
                low_side, jnp.where(inside, after, beyond), jnp.where(inside, before, here)
            )
        return 0

    lax.fori_loop(0, rows + 2 * DEPTH, turn, 0)

    def drift_of(row):
        return drift_ref[row]

    def emit_first(row, cur, rates):
        for f in range(fields):
            first_ref[row, f] = cur[f] + time_step * rates[f]

    def emit_out(row, cur, rates):
        for f in range(fields):
            second = cur[f][:, :cols] + time_step * rates[f][:, :cols]
            out_ref[row - DEPTH, f] = 0.5 * (moved_ref[row, f, :, :cols] + second)

    def load_from(ref):
        return lambda row: [ref[row, f] for f in range(fields)]

    row_sweep(load_from(moved_ref), 1, rows + 2, drift_of, emit_first)
    row_sweep(load_from(first_ref), 2, rows + 1, drift_of, emit_out)


def gathered(state, residual, shift_rows, shear_offset):
    fields, vertical, rows, cols = state.shape
    groups, radial = lax.axis_size("gy"), lax.axis_size("gx")
    gx, gy = lax.axis_index("gx"), lax.axis_index("gy")
    cells_y = cols * groups
    wide = rows + 2 * DEPTH

    up = [(i, (i + 1) % radial) for i in range(radial)]
    down = [(target, source) for source, target in up]
    low = lax.ppermute(shift_rows[-DEPTH:], "gx", up)
    high = lax.ppermute(shift_rows[:DEPTH], "gx", down)
    offset = shear_offset[0]
    low = low - jnp.where(gx == 0, offset, 0)
    high = high + jnp.where(gx == radial - 1, offset, 0)
    amounts = jnp.concatenate([low, shift_rows, high])
    origin = (cols * gy - amounts) % cells_y
    block, part = origin // cols, origin % cols
    table = jnp.stack(
        [(block + groups - 1) % groups, block, (block + 1) % groups, (block + 2) % groups, part]
    )
    padded = jnp.concatenate([residual[-DEPTH:], residual, residual[:DEPTH]])
    drift = lax.dynamic_slice_in_dim(padded, gx * rows, wide)

    count = copy_count(groups // 2)
    out = pl.pallas_call(
        functools.partial(step_kernel, groups, radial),
        out_shape=jax.ShapeDtypeStruct((rows, fields, vertical, cols), jnp.float32),
        in_specs=[
            pl.BlockSpec(memory_space=pltpu.VMEM),
            pl.BlockSpec(memory_space=pltpu.SMEM),
            pl.BlockSpec(memory_space=pltpu.SMEM),
        ],
        out_specs=pl.BlockSpec(memory_space=pltpu.VMEM),
        scratch_shapes=[
            pltpu.VMEM((groups, wide, fields, vertical, cols), jnp.float32),
            pltpu.VMEM((wide, fields, vertical, 2 * cols), jnp.float32),
            pltpu.VMEM((wide, fields, vertical, 2 * cols), jnp.float32),
            pltpu.SemaphoreType.DMA((count,)),
            pltpu.SemaphoreType.DMA((count,)),
            pltpu.SemaphoreType.DMA,
        ],
        compiler_params=pltpu.CompilerParams(collective_id=0, has_side_effects=True),
    )(jnp.transpose(state, (2, 0, 1, 3)), table, drift)
    return jnp.transpose(out, (1, 2, 0, 3))


def spread_kernel(
    groups, radial, state_ref, shift_hbm, offset_hbm, residual_hbm, out_ref,
    shift_ref, offset_ref, residual_ref, taken_0, taken_1, taken_2, taken_3, turned_ref, edge_ref,
    shear_ref, moved_ref, own_edges, low_edges, high_edges, first_ref, windows_ref, drifts_ref, send, recv, local_sems,
):
    fields, vertical, rows, cols = state_ref.shape
    quarter = rows // 4
    taken = (taken_0, taken_1, taken_2, taken_3)
    late = late_rows(rows)
    others_start = WINDOW * len(late)
    short = [row for row in range(rows + DEPTH) if row not in late]
    lane_of = {row: WINDOW * k for k, row in enumerate(late)}
    lane_of.update({row: others_start + 4 * k for k, row in enumerate(short)})
    cells_y = cols * groups
    gx, gy = lax.axis_index("gx"), lax.axis_index("gy")
    x_next = (lax.rem(gx + 1, radial), gy)
    x_prev = (lax.rem(gx + radial - 1, radial), gy)
    others = [(gx, lax.rem(gy + k, groups)) for k in range(1, groups)]
    first_x, last_x = gx == 0, gx == radial - 1
    not_first, not_last = gx > 0, gx < radial - 1
    out_sent, back_sent, edges_sent, shear_sent, ends_sent, down_sent, up_sent = range(7)
    back_got = (4, 5, 6, 14, 15)
    edges_got, shear_got, ends_got, rows_got, sides_got = 7, 8, 9, (10, 11), (12, 13)

    def remote(source, target, device, sent, got):
        return pltpu.make_async_remote_copy(
            src_ref=source,
            dst_ref=target,
            send_sem=send.at[sent],
            recv_sem=recv.at[got],
            device_id=device,
            device_id_type=MESH,
        )

    def spread_out(source, target, sent, got):
        for other in others:
            remote(source(other[1]), target, other, sent, got).start()
        pltpu.make_async_copy(source(gy), target, recv.at[got]).start()

    def arrived(ref, got):
        pltpu.make_async_copy(ref, ref, recv.at[got]).wait()

    def left(ref, sent):
        pltpu.make_async_copy(ref, ref, send.at[sent]).wait()

    small = [
        pltpu.make_async_copy(source, target, local_sems.at[k])
        for k, (source, target) in enumerate(
            ((shift_hbm, shift_ref), (offset_hbm, offset_ref), (residual_hbm, residual_ref))
        )
    ]
    for copy in small:
        copy.start()
    barrier = pltpu.get_barrier_semaphore()
    for other in (*others, x_prev, x_next):
        pl.semaphore_signal(barrier, inc=1, device_id=other, device_id_type=MESH)
    pl.semaphore_wait(barrier, groups + 1)

    def quarter_rows(q):
        return pl.ds(q * quarter, quarter)

    for pair in ((0, 3), (1, 2)):
        for other in others:
            for q in pair:
                remote(
                    state_ref.at[other[1], :, quarter_rows(q)], taken[q].at[gy], other, out_sent, q
                ).start()
        for q in pair:
            pltpu.make_async_copy(
                state_ref.at[gy, :, quarter_rows(q)], taken[q].at[gy], recv.at[q]
            ).start()

    lane = lax.broadcasted_iota(jnp.int32, (vertical, cols), 1)
    empty = [jnp.zeros((vertical, cols), jnp.float32)] * groups

    def displace(block_of, amount, slot, packed):
        whole, part = amount // cols, amount % cols
        rolled = [
            pltpu.roll(block_of(lax.rem(k - whole + groups, groups)), part, 1)
            for k in range(groups)
        ]
        row = [jnp.where(lane < part, rolled[d - 1], rolled[d]) for d in range(groups)]
        base, long = lane_of[slot], slot in late
        width = WINDOW if long else 4
        mine = (lane >= base) & (lane < base + width)
        result = []
        for d in range(groups):
            turned_ref[d, slot] = row[d]
            before, here, after = row[d - 1], row[d], row[(d + 1) % groups]
            if long:
                after = jnp.where(lane < cols // 2, after, here)
                before = jnp.where(lane < cols // 2, here, before)
            turn = base + 4
            edges = jnp.where(
                lane < base + width // 2,
                pltpu.roll(after, turn % cols if long else base, 1),
                pltpu.roll(before, (base + width - 4 if long else base + 4) % cols, 1),
            )
            result.append(jnp.where(mine, edges, packed[d]))
        return result

    def displace_quarter(q, packed):
        arrived(taken[q], q)
        for place in range(quarter):
            row = q * quarter + place
            packed = displace(
                lambda b: taken[q][b, :, place, :], shift_ref[row], row, packed
            )
        return packed

    def main_lanes(block, first_row, count):
        return moved_ref.at[block, pl.ds(first_row, count)]

    pieces = (
        (0, quarter),
        (3 * quarter, quarter),
        (quarter, EARLY[0]),
        (3 * quarter - EARLY[1], EARLY[1]),
        (late[0], len(late)),
    )

    def send_back(piece):
        first, count = pieces[piece]
        if count:
            spread_out(
                lambda d: turned_ref.at[d, pl.ds(first, count)],
                main_lanes(gy, DEPTH + first, count),
                back_sent,
                back_got[piece],
            )

    def wait_back(piece):
        first, count = pieces[piece]
        if count:
            arrived(main_lanes(slice(None), DEPTH + first, count), back_got[piece])

    for copy in small:
        copy.wait()
    packed = displace_quarter(0, empty)
    packed = displace_quarter(3, packed)
    to_last = remote(turned_ref.at[:, pl.ds(0, DEPTH)], shear_ref, x_prev, ends_sent, ends_got)
    to_first = remote(
        turned_ref.at[:, pl.ds(rows - DEPTH, DEPTH)], shear_ref, x_next, ends_sent, ends_got
    )
    pl.when(first_x)(to_last.start)
    pl.when(last_x)(to_first.start)
    for piece in (0, 1):
        send_back(piece)

    low_row, high_row = 0, DEPTH + rows
    offset = offset_ref[0]
    for d in range(groups):
        edge_ref[d] = empty[0]

    def sheared(first_row, amount):
        arrived(shear_ref, ends_got)
        edges = empty
        for place in range(DEPTH):
            edges = displace(
                lambda b: shear_ref[b, place], amount, rows + place, edges
            )
        for d in range(groups):
            edge_ref[d] = edges[d]
        spread_out(
            lambda d: turned_ref.at[d, pl.ds(rows, DEPTH)],
            main_lanes(gy, first_row, DEPTH),
            shear_sent,
            shear_got,
        )

    @pl.when(first_x)
    def _():
        sheared(low_row, lax.rem(cells_y - offset, cells_y))

    @pl.when(last_x)
    def _():
        sheared(high_row, offset)

    packed = displace_quarter(1, packed)
    packed = displace_quarter(2, packed)
    for d in range(groups):
        edge_ref[d] = jnp.where(lane < lane_of[rows], packed[d], edge_ref[d])
    spread_out(lambda d: edge_ref.at[d], own_edges.at[gy], edges_sent, edges_got)
    for piece in (2, 3):
        send_back(piece)

    every = slice(None)
    for piece in (0, 1):
        wait_back(piece)
    rows_down = remote(
        main_lanes(every, DEPTH, DEPTH), main_lanes(every, high_row, DEPTH),
        x_prev, down_sent, rows_got[1],
    )
    rows_up = remote(
        main_lanes(every, rows, DEPTH), main_lanes(every, low_row, DEPTH),
        x_next, up_sent, rows_got[0],
    )
    edges_down = remote(own_edges, high_edges, x_prev, down_sent, sides_got[1])
    edges_up = remote(own_edges, low_edges, x_next, up_sent, sides_got[0])
    pl.when(not_first)(rows_down.start)
    pl.when(not_last)(rows_up.start)
    send_back(4)
    arrived(own_edges, edges_got)
    pl.when(not_first)(edges_down.start)
    pl.when(not_last)(edges_up.start)

    start = gx * rows - DEPTH + residual_ref.shape[0]

    def drift_of(row):
        return residual_ref[lax.rem(start + row, residual_ref.shape[0])]

    windows = cols // WINDOW
    kept = windows - 2 * DEPTH

    def emit_first(row, cur, rates):
        for f in range(fields):
            first_ref[row, f] = cur[f] + time_step * rates[f]

    def emit_whole(row, cur, rates):
        i = (row - DEPTH) // kept
        base = WINDOW * (row - i * kept)
        for f in range(fields):
            sides = windows_ref[i, f]
            low = pltpu.roll(sides, 2 * cols - base - 8, 1)
            high = pltpu.roll(sides, 2 * cols - base - 4, 1)
            total = moved_ref[f, row] + (cur[f] + time_step * rates[f])
            middle = jnp.where(lane >= cols - 2, high, total)
            out_ref[f, :, row - DEPTH, :] = jnp.where(lane < 2, low, middle)

    def stage_one(low, high):
        row_sweep(
            lambda row: [moved_ref[f, row] for f in range(fields)],
            DEPTH + low, DEPTH + high, drift_of, emit_first, 3,
        )

    def stage_two(low, high):
        row_sweep(
            lambda row: [first_ref[row, f] for f in range(fields)],
            DEPTH + low, DEPTH + high, drift_of, emit_whole, 4,
        )

    starts = range(-DEPTH, rows - DEPTH, kept)

    def in_window(k, low, high):
        return (lane >= WINDOW * k + low) & (lane < WINDOW * k + high)

    def rows_of(start):
        return range(start, min(start + windows, rows + DEPTH))

    def window_drift(start):
        total = empty[0]
        for k, row in enumerate(rows_of(start)):
            total = jnp.where(in_window(k, 0, WINDOW), drift_of(DEPTH + row), total)
        return total

    def fill_all(first_row, count, edges_ref, first_place):
        for i in range(len(starts)):
            held = [
                (k, row) for k, row in enumerate(rows_of(starts[i]))
                if first_row <= row < first_row + count and row not in late
            ]
            for f in range(fields):
                packed, value = edges_ref[f], windows_ref[i, f]
                for k, row in held:
                    base, from_lane = WINDOW * k, lane_of[first_place + row - first_row]
                    main = moved_ref[f, DEPTH + row]
                    for low, source, turn in (
                        (0, main, base + 4), (4, packed, base + 4 - from_lane), (8, main, base + 8)
                    ):
                        value = jnp.where(
                            in_window(k, low, low + 4), pltpu.roll(source, turn % cols, 1), value
                        )
                if held:
                    windows_ref[i, f] = value

    def fill_late():
        for i in range(len(starts)):
            held = [k for k, row in enumerate(rows_of(starts[i])) if row in late]
            if not held:
                continue
            from_lane = lane_of[starts[i] + held[0]]
            mine = (lane >= WINDOW * held[0]) & (lane < WINDOW * (held[-1] + 1))
            for f in range(fields):
                value = pltpu.roll(own_edges[f], (WINDOW * held[0] - from_lane) % cols, 1)
                windows_ref[i, f] = jnp.where(mine, value, windows_ref[i, f])

    def window_step(values, drift):
        turned = [
            [pltpu.roll(a, (WINDOW * (1 - r)) % cols, 1) for a in values] for r in range(3)
        ]
        drifts = [pltpu.roll(drift, (WINDOW * (1 - r)) % cols, 1) for r in range(3)]
        got = []
        row_sweep(
            lambda r: turned[r], 1, 1, lambda r: drifts[r],
            lambda r, cur, rates: got.extend(a + time_step * b for a, b in zip(cur, rates)),
        )
        return got

    def window_stages(i):
        drift = drifts_ref[i]
        moved = [windows_ref[i, f] for f in range(fields)]
        second = window_step(window_step(moved, drift), drift)
        for f in range(fields):
            windows_ref[i, f] = moved[f] + second[f]

    for i in range(len(starts)):
        drifts_ref[i] = window_drift(starts[i])
        for f in range(fields):
            windows_ref[i, f] = empty[0]
    fill_late()
    for piece in (2, 3):
        wait_back(piece)
    fill_all(0, rows, own_edges, 0)
    inside = [i for i in range(len(starts)) if starts[i] >= 0 and rows_of(starts[i])[-1] < rows]
    for i in inside:
        window_stages(i)
    stage_one(1, late[0] - 2)
    stage_one(late[-1] + 2, rows - 2)

    @pl.when(first_x)
    def _():
        arrived(main_lanes(every, low_row, DEPTH), shear_got)
        fill_all(-DEPTH, DEPTH, own_edges, rows)

    @pl.when(last_x)
    def _():
        arrived(main_lanes(every, high_row, DEPTH), shear_got)
        fill_all(rows, DEPTH, own_edges, rows)

    pl.when(not_first)(rows_up.wait_recv)
    pl.when(not_last)(rows_down.wait_recv)
    stage_one(-1, 0)
    stage_one(rows - 1, rows)

    @pl.when(not_first)
    def _():
        edges_up.wait_recv()
        fill_all(-DEPTH, DEPTH, low_edges, rows - DEPTH)

    @pl.when(not_last)
    def _():
        edges_down.wait_recv()
        fill_all(rows, DEPTH, high_edges, 0)

    for i in range(len(starts)):
        if i not in inside:
            window_stages(i)
    stage_two(0, late[0] - 3)
    stage_two(late[-1] + 3, rows - 1)
    wait_back(4)
    stage_one(late[0] - 1, late[-1] + 1)
    stage_two(late[0] - 2, late[-1] + 2)

    away = pl.ds(0, groups - 1)
    left(state_ref.at[away], out_sent)
    left(turned_ref.at[away, pl.ds(0, rows)], back_sent)
    left(edge_ref.at[away], edges_sent)

    @pl.when(first_x | last_x)
    def _():
        left(shear_ref, ends_sent)
        left(turned_ref.at[away, pl.ds(rows, DEPTH)], shear_sent)

    @pl.when(not_first)
    def _():
        rows_down.wait_send()
        edges_down.wait_send()

    @pl.when(not_last)
    def _():
        rows_up.wait_send()
        edges_up.wait_send()


def spread(state, residual, shift_rows, shear_offset):
    fields, vertical, rows, cols = state.shape
    groups, radial = lax.axis_size("gy"), lax.axis_size("gx")
    wide = rows + 2 * DEPTH
    parts = len(range(0, rows, cols // WINDOW - 2 * DEPTH))
    anywhere = pl.BlockSpec(memory_space=pl.ANY)
    vmem = pl.BlockSpec(memory_space=pltpu.VMEM)
    edges = pltpu.VMEM((groups, vertical, cols), jnp.float32)
    out = pl.pallas_call(
        functools.partial(spread_kernel, groups, radial),
        out_shape=pltpu.VMEM(state.shape, jnp.float32),
        in_specs=[anywhere] * 4,
        out_specs=vmem,
        scratch_shapes=[
            pltpu.SMEM(shift_rows.shape, jnp.int32),
            pltpu.SMEM(shear_offset.shape, jnp.int32),
            pltpu.SMEM(residual.shape, jnp.float32),
            *[pltpu.VMEM((groups, vertical, rows // 4, cols), jnp.float32)] * 4,
            pltpu.VMEM((groups, rows + DEPTH, vertical, cols), jnp.float32),
            edges,
            pltpu.VMEM((groups, DEPTH, vertical, cols), jnp.float32),
            pltpu.VMEM((fields, wide, vertical, cols), jnp.float32),
            edges,
            edges,
            edges,
            pltpu.VMEM((wide, fields, vertical, cols), jnp.float32),
            pltpu.VMEM((parts, fields, vertical, cols), jnp.float32),
            pltpu.VMEM((parts, vertical, cols), jnp.float32),
            pltpu.SemaphoreType.DMA((7,)),
            pltpu.SemaphoreType.DMA((16,)),
            pltpu.SemaphoreType.DMA((3,)),
        ],
        compiler_params=pltpu.CompilerParams(collective_id=1, has_side_effects=True),
    )(state, shift_rows, shear_offset, residual)
    return 0.5 * out


def local(state, residual, shift_rows, shear_offset):
    fields, _, rows, cols = state.shape
    paired = lax.axis_size("gy") == fields and lax.axis_size("gx") > 2
    late = len(late_rows(rows))
    if paired and rows % 16 == 0 and WINDOW * late + 4 * (rows + DEPTH - late) <= cols:
        return spread(state, residual, shift_rows, shear_offset)
    return gathered(state, residual, shift_rows, shear_offset)


def solution(mesh):
    return jax.shard_map(
        local,
        mesh=mesh,
        in_specs=(P(None, None, "gx", "gy"), P(), P("gx"), P()),
        out_specs=P(None, None, "gx", "gy"),
        check_vma=False,
    )
```

```python
import functools

import jax
import jax.numpy as jnp
from jax import lax
from jax.experimental import pallas as pl
from jax.experimental.pallas import tpu as pltpu
from jax.sharding import PartitionSpec as P

time_step = 0.2
viscous = 0.1
resist = 0.1
sound_sq = 1.0
rotation = 0.5
shear_rate = 1.5

MESH = pl.DeviceIdType.MESH
DEPTH = 2
WINDOW = 12
EARLY = (1, 0)


def late_rows(rows):
    return range(rows // 4 + EARLY[0], 3 * rows // 4 - EARLY[1])


class Copies:
    def __init__(self, send, recv):
        self.send, self.recv, self.made = send, recv, []

    def start(self, source, target, device):
        k = len(self.made)
        copy = pltpu.make_async_remote_copy(
            src_ref=source,
            dst_ref=target,
            send_sem=self.send.at[k],
            recv_sem=self.recv.at[k],
            device_id=device,
            device_id_type=MESH,
        )
        copy.start()
        self.made.append(copy)
        return copy


def copy_count(chips):
    return 8 + sum(10 if 2 * s < chips else 6 for s in range(1, chips // 2 + 1)) + 8 * (chips // 2 + 1)


def gather(state_ref, grid_ref, copies, local_sem, groups, radial):
    rows = state_ref.shape[0]
    chips = groups // 2
    half = rows // 2
    gx, gy = lax.axis_index("gx"), lax.axis_index("gy")
    chip, core = gy // 2, gy % 2

    def at_chip(offset):
        return lax.rem(chip + offset + chips, chips) * 2 + core

    right, left = (gx, at_chip(1)), (gx, at_chip(-1))
    twin = (gx, chip * 2 + (1 - core))
    x_next = (lax.rem(gx + 1, radial), gy)
    x_prev = (lax.rem(gx + radial - 1, radial), gy)

    barrier = pltpu.get_barrier_semaphore()
    for other in (right, left, twin, x_next, x_prev):
        pl.semaphore_signal(barrier, inc=1, device_id=other, device_id_type=MESH)
    pl.semaphore_wait(barrier, 5)

    def piece(block, part):
        return grid_ref.at[block, pl.ds(DEPTH + part * half, half)]

    def low_rows(block):
        return grid_ref.at[block, pl.ds(0, DEPTH)]

    def high_rows(block):
        return grid_ref.at[block, pl.ds(DEPTH + rows, DEPTH)]

    def send_rows(block, part, source):
        if part == 0:
            edge = source.at[pl.ds(0, DEPTH)]
            return block, 0, copies.start(edge, high_rows(block), x_prev)
        edge = source.at[pl.ds(half - DEPTH, DEPTH)]
        return block, 1, copies.start(edge, low_rows(block), x_next)

    to_twin = []

    def pass_rows(sent):
        for block, part, copy in sent:
            copy.wait_recv()
            strip = high_rows(block) if part == 0 else low_rows(block)
            to_twin.append(copies.start(strip, strip, twin))

    own = [state_ref.at[pl.ds(0, half)], state_ref.at[pl.ds(half, half)]]
    keep = pltpu.make_async_copy(state_ref, grid_ref.at[gy, pl.ds(DEPTH, rows)], local_sem)

    flights = []
    order = [(0, 0), (1, 1), (0, 1), (1, 0)] if chips > 2 else [(0, 0), (1, 1)]
    for way, part in order:
        flights.append(
            (way, part, copies.start(own[part], piece(gy, part), right if way == 0 else left))
        )
    sent = [send_rows(gy, part, own[part]) for part in (0, 1)]
    for part in (0, 1):
        to_twin.append(copies.start(own[part], piece(gy, part), twin))
    keep.start()
    pass_rows(sent)
    for step in range(1, chips // 2 + 1):
        later, sent = [], []
        for way, part, copy in flights:
            block = at_chip(-step if way == 0 else step)
            copy.wait_recv()
            ref = piece(block, part)
            if 2 * (step + 1) < chips or (2 * (step + 1) == chips and part == way):
                later.append((way, part, copies.start(ref, ref, right if way == 0 else left)))
            to_twin.append(copies.start(ref, ref, twin))
            sent.append(send_rows(block, part, ref))
        pass_rows(sent)
        flights = later
    keep.wait()
    for copy in to_twin:
        copy.wait_recv()
    for copy in copies.made:
        copy.wait_send()


def row_sweep(load, first_row, last_row, drift_of, emit, unroll=4):
    def y_ahead(a):
        return pltpu.roll(a, a.shape[1] - 1, 1)

    def y_behind(a):
        return pltpu.roll(a, 1, 1)

    def z_ahead(a):
        return pltpu.roll(a, a.shape[0] - 1, 0)

    def z_behind(a):
        return pltpu.roll(a, 1, 0)

    def cells(by, bz):
        return 0.5 * (by + y_ahead(by)), 0.5 * (bz + z_ahead(bz))

    def radial_edges(prev, cur, prev_drift, cur_drift):
        sum_x = prev[1] + cur[1]
        sum_w = (prev[2] + prev_drift) + (cur[2] + cur_drift)
        sum_z = prev[3] + cur[3]
        bx, by, bz = cur[5], cur[6], cur[7]
        bx_y, bx_z = y_behind(bx), z_behind(bx)
        emf_z = 0.125 * (
            (sum_w + y_behind(sum_w)) * (bx + bx_y) - (sum_x + y_behind(sum_x)) * (by + prev[6])
        ) + resist * ((by - prev[6]) - (bx - bx_y))
        emf_y = 0.125 * (
            (sum_x + z_behind(sum_x)) * (bz + prev[7]) - (sum_z + z_behind(sum_z)) * (bx + bx_z)
        ) + resist * ((bx - bx_z) - (bz - prev[7]))
        return emf_z, emf_y

    start_prev, start_cur = load(first_row - 1), load(first_row)
    carry = (
        *cells(start_prev[6], start_prev[7]),
        *cells(start_cur[6], start_cur[7]),
        *radial_edges(start_prev, start_cur, drift_of(first_row - 1), drift_of(first_row)),
    )

    def one(row, carry):
        cy_prev, cz_prev, cy, cz, emf_z, emf_y = carry
        prev, cur, nxt = load(row - 1), load(row), load(row + 1)
        drift = drift_of(row)
        log_rho, vx, vy, vz, ent, bx, by, bz = cur
        w = vy + drift
        cy_next, cz_next = cells(nxt[6], nxt[7])
        emf_z_next, emf_y_next = radial_edges(cur, nxt, drift, drift_of(row + 1))

        half_x, half_w, half_z = 0.5 * vx, 0.5 * w, 0.5 * vz
        diffs, advs = [], []
        for f in range(5):
            a = cur[f]
            ya, yb, za, zb = y_ahead(a), y_behind(a), z_ahead(a), z_behind(a)
            dx, dy, dz = nxt[f] - prev[f], ya - yb, za - zb
            lap = ((nxt[f] + prev[f]) + (ya + yb) + (za + zb)) - 6.0 * a
            diffs.append((dx, dy, dz))
            advs.append(viscous * lap - (half_x * dx + half_w * dy + half_z * dz))

        sum_bx = bx + nxt[5]
        cx = 0.5 * sum_bx
        cur_x = 0.5 * ((y_ahead(cz) - y_behind(cz)) - (z_ahead(cy) - z_behind(cy)))
        cur_y = 0.5 * ((z_ahead(cx) - z_behind(cx)) - (cz_next - cz_prev))
        cur_z = 0.5 * ((cy_next - cy_prev) - (y_ahead(cx) - y_behind(cx)))
        inverse = jnp.exp(-log_rho)
        force_x = inverse * (cur_y * cz - cur_z * cy)
        force_y = inverse * (cur_z * cx - cur_x * cz)
        force_z = inverse * (cur_x * cy - cur_y * cx)

        pairs = [diffs[0][d] + diffs[4][d] for d in range(3)]
        rates = [
            advs[0] - 0.5 * (diffs[1][0] + diffs[2][1] + diffs[3][2]),
            advs[1] - (0.5 * sound_sq) * pairs[0] + force_x + (2.0 * rotation) * vy,
            advs[2] - (0.5 * sound_sq) * pairs[1] + force_y - ((2.0 - shear_rate) * rotation) * vx,
            advs[3] - (0.5 * sound_sq) * pairs[2] + force_z,
            advs[4] + resist * inverse * (cur_x * cur_x + cur_y * cur_y + cur_z * cur_z),
        ]

        w_y, z_y = w + y_behind(w), vz + y_behind(vz)
        bz_y, by_z = y_behind(bz), z_behind(by)
        emf_x = 0.125 * (
            (z_y + z_behind(z_y)) * (by + by_z) - (w_y + z_behind(w_y)) * (bz + bz_y)
        ) + resist * ((bz - bz_y) - (by - by_z))
        stretch = 0.25 * (sum_bx + y_behind(sum_bx))
        rates.append((z_ahead(emf_y) - emf_y) - (y_ahead(emf_z) - emf_z))
        rates.append(
            (emf_z_next - emf_z) - (z_ahead(emf_x) - emf_x) - (shear_rate * rotation) * stretch
        )
        rates.append((y_ahead(emf_x) - emf_x) - (emf_y_next - emf_y))
        emit(row, cur, rates)
        return cy, cz, cy_next, cz_next, emf_z_next, emf_y_next

    if last_row - first_row < 3:
        for row in range(first_row, last_row + 1):
            carry = one(row, carry)
        return
    lax.fori_loop(first_row, last_row + 1, one, carry, unroll=unroll)


def step_kernel(
    groups, radial, state_ref, table_ref, drift_ref, out_ref,
    grid_ref, moved_ref, first_ref, send, recv, local_sem,
):
    rows, fields, _, cols = state_ref.shape
    gather(state_ref, grid_ref, Copies(send, recv), local_sem, groups, radial)

    lane = lax.broadcasted_iota(jnp.int32, state_ref.shape[2:], 1)

    def turn(row, _):
        amount = table_ref[4, row]
        inside = lane < cols - amount
        low_side = lane < cols // 2
        blocks = [table_ref[k, row] for k in range(4)]
        for f in range(fields):
            before, here, after, beyond = [
                pltpu.roll(grid_ref[b, row, f], cols - amount, 1) for b in blocks
            ]
            moved_ref[row, f, :, :cols] = jnp.where(inside, here, after)
            moved_ref[row, f, :, cols:] = jnp.where(
                low_side, jnp.where(inside, after, beyond), jnp.where(inside, before, here)
            )
        return 0

    lax.fori_loop(0, rows + 2 * DEPTH, turn, 0)

    def drift_of(row):
        return drift_ref[row]

    def emit_first(row, cur, rates):
        for f in range(fields):
            first_ref[row, f] = cur[f] + time_step * rates[f]

    def emit_out(row, cur, rates):
        for f in range(fields):
            second = cur[f][:, :cols] + time_step * rates[f][:, :cols]
            out_ref[row - DEPTH, f] = 0.5 * (moved_ref[row, f, :, :cols] + second)

    def load_from(ref):
        return lambda row: [ref[row, f] for f in range(fields)]

    row_sweep(load_from(moved_ref), 1, rows + 2, drift_of, emit_first)
    row_sweep(load_from(first_ref), 2, rows + 1, drift_of, emit_out)


def gathered(state, residual, shift_rows, shear_offset):
    fields, vertical, rows, cols = state.shape
    groups, radial = lax.axis_size("gy"), lax.axis_size("gx")
    gx, gy = lax.axis_index("gx"), lax.axis_index("gy")
    cells_y = cols * groups
    wide = rows + 2 * DEPTH

    up = [(i, (i + 1) % radial) for i in range(radial)]
    down = [(target, source) for source, target in up]
    low = lax.ppermute(shift_rows[-DEPTH:], "gx", up)
    high = lax.ppermute(shift_rows[:DEPTH], "gx", down)
    offset = shear_offset[0]
    low = low - jnp.where(gx == 0, offset, 0)
    high = high + jnp.where(gx == radial - 1, offset, 0)
    amounts = jnp.concatenate([low, shift_rows, high])
    origin = (cols * gy - amounts) % cells_y
    block, part = origin // cols, origin % cols
    table = jnp.stack(
        [(block + groups - 1) % groups, block, (block + 1) % groups, (block + 2) % groups, part]
    )
    padded = jnp.concatenate([residual[-DEPTH:], residual, residual[:DEPTH]])
    drift = lax.dynamic_slice_in_dim(padded, gx * rows, wide)

    count = copy_count(groups // 2)
    out = pl.pallas_call(
        functools.partial(step_kernel, groups, radial),
        out_shape=jax.ShapeDtypeStruct((rows, fields, vertical, cols), jnp.float32),
        in_specs=[
            pl.BlockSpec(memory_space=pltpu.VMEM),
            pl.BlockSpec(memory_space=pltpu.SMEM),
            pl.BlockSpec(memory_space=pltpu.SMEM),
        ],
        out_specs=pl.BlockSpec(memory_space=pltpu.VMEM),
        scratch_shapes=[
            pltpu.VMEM((groups, wide, fields, vertical, cols), jnp.float32),
            pltpu.VMEM((wide, fields, vertical, 2 * cols), jnp.float32),
            pltpu.VMEM((wide, fields, vertical, 2 * cols), jnp.float32),
            pltpu.SemaphoreType.DMA((count,)),
            pltpu.SemaphoreType.DMA((count,)),
            pltpu.SemaphoreType.DMA,
        ],
        compiler_params=pltpu.CompilerParams(collective_id=0, has_side_effects=True),
    )(jnp.transpose(state, (2, 0, 1, 3)), table, drift)
    return jnp.transpose(out, (1, 2, 0, 3))


def spread_kernel(
    groups, radial, state_ref, shift_hbm, offset_hbm, residual_hbm, out_ref,
    shift_ref, offset_ref, residual_ref, taken_0, taken_1, taken_2, taken_3, turned_ref, edge_ref,
    shear_ref, moved_ref, own_edges, low_edges, high_edges, first_ref, windows_ref, drifts_ref, send, recv, local_sems,
):
    fields, vertical, rows, cols = state_ref.shape
    quarter = rows // 4
    taken = (taken_0, taken_1, taken_2, taken_3)
    late = late_rows(rows)
    others_start = WINDOW * len(late)
    short = [row for row in range(rows + DEPTH) if row not in late]
    lane_of = {row: WINDOW * k for k, row in enumerate(late)}
    lane_of.update({row: others_start + 4 * k for k, row in enumerate(short)})
    cells_y = cols * groups
    gx, gy = lax.axis_index("gx"), lax.axis_index("gy")
    x_next = (lax.rem(gx + 1, radial), gy)
    x_prev = (lax.rem(gx + radial - 1, radial), gy)
    others = [(gx, lax.rem(gy + k, groups)) for k in range(1, groups)]
    first_x, last_x = gx == 0, gx == radial - 1
    not_first, not_last = gx > 0, gx < radial - 1
    out_sent, back_sent, edges_sent, shear_sent, ends_sent, down_sent, up_sent = range(7)
    back_got = (4, 5, 6, 14, 15, 16)
    edges_got, shear_got, ends_got, rows_got, sides_got = 7, 8, 9, (10, 11), (12, 13)

    def remote(source, target, device, sent, got):
        return pltpu.make_async_remote_copy(
            src_ref=source,
            dst_ref=target,
            send_sem=send.at[sent],
            recv_sem=recv.at[got],
            device_id=device,
            device_id_type=MESH,
        )

    def spread_out(source, target, sent, got):
        for other in others:
            remote(source(other[1]), target, other, sent, got).start()
        pltpu.make_async_copy(source(gy), target, recv.at[got]).start()

    def arrived(ref, got):
        pltpu.make_async_copy(ref, ref, recv.at[got]).wait()

    def left(ref, sent):
        pltpu.make_async_copy(ref, ref, send.at[sent]).wait()

    small = [
        pltpu.make_async_copy(source, target, local_sems.at[k])
        for k, (source, target) in enumerate(
            ((shift_hbm, shift_ref), (offset_hbm, offset_ref), (residual_hbm, residual_ref))
        )
    ]
    for copy in small:
        copy.start()
    barrier = pltpu.get_barrier_semaphore()
    for other in (*others, x_prev, x_next):
        pl.semaphore_signal(barrier, inc=1, device_id=other, device_id_type=MESH)
    pl.semaphore_wait(barrier, groups + 1)

    def quarter_rows(q):
        return pl.ds(q * quarter, quarter)

    for pair in ((0, 3), (1, 2)):
        for other in others:
            for q in pair:
                remote(
                    state_ref.at[other[1], :, quarter_rows(q)], taken[q].at[gy], other, out_sent, q
                ).start()
        for q in pair:
            pltpu.make_async_copy(
                state_ref.at[gy, :, quarter_rows(q)], taken[q].at[gy], recv.at[q]
            ).start()

    lane = lax.broadcasted_iota(jnp.int32, (vertical, cols), 1)
    empty = [jnp.zeros((vertical, cols), jnp.float32)] * groups

    def displace(block_of, amount, slot, packed):
        whole, part = amount // cols, amount % cols
        rolled = [
            pltpu.roll(block_of(lax.rem(k - whole + groups, groups)), part, 1)
            for k in range(groups)
        ]
        row = [jnp.where(lane < part, rolled[d - 1], rolled[d]) for d in range(groups)]
        base, long = lane_of[slot], slot in late
        width = WINDOW if long else 4
        mine = (lane >= base) & (lane < base + width)
        result = []
        for d in range(groups):
            turned_ref[d, slot] = row[d]
            before, here, after = row[d - 1], row[d], row[(d + 1) % groups]
            if long:
                after = jnp.where(lane < cols // 2, after, here)
                before = jnp.where(lane < cols // 2, here, before)
            turn = base + 4
            edges = jnp.where(
                lane < base + width // 2,
                pltpu.roll(after, turn % cols if long else base, 1),
                pltpu.roll(before, (base + width - 4 if long else base + 4) % cols, 1),
            )
            result.append(jnp.where(mine, edges, packed[d]))
        return result

    def displace_quarter(q, packed):
        arrived(taken[q], q)
        for place in range(quarter):
            row = q * quarter + place
            packed = displace(
                lambda b: taken[q][b, :, place, :], shift_ref[row], row, packed
            )
        return packed

    def main_lanes(block, first_row, count):
        return moved_ref.at[block, pl.ds(first_row, count)]

    pieces = (
        (0, quarter),
        (3 * quarter, quarter),
        (quarter, EARLY[0]),
        (3 * quarter - EARLY[1], EARLY[1]),
        (late[0], len(late) // 2),
        (late[len(late) // 2], len(late) - len(late) // 2),
    )

    def send_back(piece):
        first, count = pieces[piece]
        if count:
            spread_out(
                lambda d: turned_ref.at[d, pl.ds(first, count)],
                main_lanes(gy, DEPTH + first, count),
                back_sent,
                back_got[piece],
            )

    def wait_back(piece):
        first, count = pieces[piece]
        if count:
            arrived(main_lanes(slice(None), DEPTH + first, count), back_got[piece])

    for copy in small:
        copy.wait()
    packed = displace_quarter(0, empty)
    packed = displace_quarter(3, packed)
    to_last = remote(turned_ref.at[:, pl.ds(0, DEPTH)], shear_ref, x_prev, ends_sent, ends_got)
    to_first = remote(
        turned_ref.at[:, pl.ds(rows - DEPTH, DEPTH)], shear_ref, x_next, ends_sent, ends_got
    )
    pl.when(first_x)(to_last.start)
    pl.when(last_x)(to_first.start)
    for piece in (0, 1):
        send_back(piece)

    low_row, high_row = 0, DEPTH + rows
    offset = offset_ref[0]
    for d in range(groups):
        edge_ref[d] = empty[0]

    def sheared(first_row, amount):
        arrived(shear_ref, ends_got)
        edges = empty
        for place in range(DEPTH):
            edges = displace(
                lambda b: shear_ref[b, place], amount, rows + place, edges
            )
        for d in range(groups):
            edge_ref[d] = edges[d]
        spread_out(
            lambda d: turned_ref.at[d, pl.ds(rows, DEPTH)],
            main_lanes(gy, first_row, DEPTH),
            shear_sent,
            shear_got,
        )

    @pl.when(first_x)
    def _():
        sheared(low_row, lax.rem(cells_y - offset, cells_y))

    @pl.when(last_x)
    def _():
        sheared(high_row, offset)

    packed = displace_quarter(1, packed)
    packed = displace_quarter(2, packed)
    for d in range(groups):
        edge_ref[d] = jnp.where(lane < lane_of[rows], packed[d], edge_ref[d])
    spread_out(lambda d: edge_ref.at[d], own_edges.at[gy], edges_sent, edges_got)
    for piece in (2, 3):
        send_back(piece)

    every = slice(None)
    for piece in (0, 1):
        wait_back(piece)
    rows_down = remote(
        main_lanes(every, DEPTH, DEPTH), main_lanes(every, high_row, DEPTH),
        x_prev, down_sent, rows_got[1],
    )
    rows_up = remote(
        main_lanes(every, rows, DEPTH), main_lanes(every, low_row, DEPTH),
        x_next, up_sent, rows_got[0],
    )
    edges_down = remote(own_edges, high_edges, x_prev, down_sent, sides_got[1])
    edges_up = remote(own_edges, low_edges, x_next, up_sent, sides_got[0])
    pl.when(not_first)(rows_down.start)
    pl.when(not_last)(rows_up.start)
    send_back(4)
    send_back(5)
    arrived(own_edges, edges_got)
    pl.when(not_first)(edges_down.start)
    pl.when(not_last)(edges_up.start)

    start = gx * rows - DEPTH + residual_ref.shape[0]

    def drift_of(row):
        return residual_ref[lax.rem(start + row, residual_ref.shape[0])]

    windows = cols // WINDOW
    kept = windows - 2 * DEPTH

    def emit_first(row, cur, rates):
        for f in range(fields):
            first_ref[row, f] = cur[f] + time_step * rates[f]

    def emit_whole(row, cur, rates):
        i = (row - DEPTH) // kept
        base = WINDOW * (row - i * kept)
        for f in range(fields):
            sides = windows_ref[i, f]
            low = pltpu.roll(sides, 2 * cols - base - 8, 1)
            high = pltpu.roll(sides, 2 * cols - base - 4, 1)
            total = moved_ref[f, row] + (cur[f] + time_step * rates[f])
            middle = jnp.where(lane >= cols - 2, high, total)
            out_ref[f, :, row - DEPTH, :] = jnp.where(lane < 2, low, middle)

    def stage_one(low, high):
        row_sweep(
            lambda row: [moved_ref[f, row] for f in range(fields)],
            DEPTH + low, DEPTH + high, drift_of, emit_first, 3,
        )

    def stage_two(low, high):
        row_sweep(
            lambda row: [first_ref[row, f] for f in range(fields)],
            DEPTH + low, DEPTH + high, drift_of, emit_whole, 4,
        )

    starts = range(-DEPTH, rows - DEPTH, kept)

    def in_window(k, low, high):
        return (lane >= WINDOW * k + low) & (lane < WINDOW * k + high)

    def rows_of(start):
        return range(start, min(start + windows, rows + DEPTH))

    def window_drift(start):
        total = empty[0]
        for k, row in enumerate(rows_of(start)):
            total = jnp.where(in_window(k, 0, WINDOW), drift_of(DEPTH + row), total)
        return total

    def fill_all(first_row, count, edges_ref, first_place):
        for i in range(len(starts)):
            held = [
                (k, row) for k, row in enumerate(rows_of(starts[i]))
                if first_row <= row < first_row + count and row not in late
            ]
            for f in range(fields):
                packed, value = edges_ref[f], windows_ref[i, f]
                for k, row in held:
                    base, from_lane = WINDOW * k, lane_of[first_place + row - first_row]
                    main = moved_ref[f, DEPTH + row]
                    for low, source, turn in (
                        (0, main, base + 4), (4, packed, base + 4 - from_lane), (8, main, base + 8)
                    ):
                        value = jnp.where(
                            in_window(k, low, low + 4), pltpu.roll(source, turn % cols, 1), value
                        )
                if held:
                    windows_ref[i, f] = value

    def fill_late():
        for i in range(len(starts)):
            held = [k for k, row in enumerate(rows_of(starts[i])) if row in late]
            if not held:
                continue
            from_lane = lane_of[starts[i] + held[0]]
            mine = (lane >= WINDOW * held[0]) & (lane < WINDOW * (held[-1] + 1))
            for f in range(fields):
                value = pltpu.roll(own_edges[f], (WINDOW * held[0] - from_lane) % cols, 1)
                windows_ref[i, f] = jnp.where(mine, value, windows_ref[i, f])

    def window_step(values, drift):
        turned = [
            [pltpu.roll(a, (WINDOW * (1 - r)) % cols, 1) for a in values] for r in range(3)
        ]
        drifts = [pltpu.roll(drift, (WINDOW * (1 - r)) % cols, 1) for r in range(3)]
        got = []
        row_sweep(
            lambda r: turned[r], 1, 1, lambda r: drifts[r],
            lambda r, cur, rates: got.extend(a + time_step * b for a, b in zip(cur, rates)),
        )
        return got

    def window_stages(i):
        drift = drifts_ref[i]
        moved = [windows_ref[i, f] for f in range(fields)]
        second = window_step(window_step(moved, drift), drift)
        for f in range(fields):
            windows_ref[i, f] = moved[f] + second[f]

    for i in range(len(starts)):
        drifts_ref[i] = window_drift(starts[i])
        for f in range(fields):
            windows_ref[i, f] = empty[0]
    fill_late()
    for piece in (2, 3):
        wait_back(piece)
    fill_all(0, rows, own_edges, 0)
    inside = [i for i in range(len(starts)) if starts[i] >= 0 and rows_of(starts[i])[-1] < rows]
    for i in inside:
        window_stages(i)
    stage_one(1, late[0] - 2)
    stage_one(late[-1] + 2, rows - 2)

    @pl.when(first_x)
    def _():
        arrived(main_lanes(every, low_row, DEPTH), shear_got)
        fill_all(-DEPTH, DEPTH, own_edges, rows)

    @pl.when(last_x)
    def _():
        arrived(main_lanes(every, high_row, DEPTH), shear_got)
        fill_all(rows, DEPTH, own_edges, rows)

    pl.when(not_first)(rows_up.wait_recv)
    pl.when(not_last)(rows_down.wait_recv)
    stage_one(-1, 0)
    stage_one(rows - 1, rows)

    @pl.when(not_first)
    def _():
        edges_up.wait_recv()
        fill_all(-DEPTH, DEPTH, low_edges, rows - DEPTH)

    @pl.when(not_last)
    def _():
        edges_down.wait_recv()
        fill_all(rows, DEPTH, high_edges, 0)

    for i in range(len(starts)):
        if i not in inside:
            window_stages(i)
    stage_two(0, late[0] - 3)
    stage_two(late[-1] + 3, rows - 1)
    wait_back(4)
    middle = late[len(late) // 2]
    stage_one(late[0] - 1, middle - 2)
    stage_two(late[0] - 2, middle - 3)
    wait_back(5)
    stage_one(middle - 1, late[-1] + 1)
    stage_two(middle - 2, late[-1] + 2)

    away = pl.ds(0, groups - 1)
    left(state_ref.at[away], out_sent)
    left(turned_ref.at[away, pl.ds(0, rows)], back_sent)
    left(edge_ref.at[away], edges_sent)

    @pl.when(first_x | last_x)
    def _():
        left(shear_ref, ends_sent)
        left(turned_ref.at[away, pl.ds(rows, DEPTH)], shear_sent)

    @pl.when(not_first)
    def _():
        rows_down.wait_send()
        edges_down.wait_send()

    @pl.when(not_last)
    def _():
        rows_up.wait_send()
        edges_up.wait_send()


def spread(state, residual, shift_rows, shear_offset):
    fields, vertical, rows, cols = state.shape
    groups, radial = lax.axis_size("gy"), lax.axis_size("gx")
    wide = rows + 2 * DEPTH
    parts = len(range(0, rows, cols // WINDOW - 2 * DEPTH))
    anywhere = pl.BlockSpec(memory_space=pl.ANY)
    vmem = pl.BlockSpec(memory_space=pltpu.VMEM)
    edges = pltpu.VMEM((groups, vertical, cols), jnp.float32)
    out = pl.pallas_call(
        functools.partial(spread_kernel, groups, radial),
        out_shape=pltpu.VMEM(state.shape, jnp.float32),
        in_specs=[anywhere] * 4,
        out_specs=vmem,
        scratch_shapes=[
            pltpu.SMEM(shift_rows.shape, jnp.int32),
            pltpu.SMEM(shear_offset.shape, jnp.int32),
            pltpu.SMEM(residual.shape, jnp.float32),
            *[pltpu.VMEM((groups, vertical, rows // 4, cols), jnp.float32)] * 4,
            pltpu.VMEM((groups, rows + DEPTH, vertical, cols), jnp.float32),
            edges,
            pltpu.VMEM((groups, DEPTH, vertical, cols), jnp.float32),
            pltpu.VMEM((fields, wide, vertical, cols), jnp.float32),
            edges,
            edges,
            edges,
            pltpu.VMEM((wide, fields, vertical, cols), jnp.float32),
            pltpu.VMEM((parts, fields, vertical, cols), jnp.float32),
            pltpu.VMEM((parts, vertical, cols), jnp.float32),
            pltpu.SemaphoreType.DMA((7,)),
            pltpu.SemaphoreType.DMA((17,)),
            pltpu.SemaphoreType.DMA((3,)),
        ],
        compiler_params=pltpu.CompilerParams(collective_id=1, has_side_effects=True),
    )(state, shift_rows, shear_offset, residual)
    return 0.5 * out


def local(state, residual, shift_rows, shear_offset):
    fields, _, rows, cols = state.shape
    paired = lax.axis_size("gy") == fields and lax.axis_size("gx") > 2
    late = len(late_rows(rows))
    if paired and rows % 16 == 0 and WINDOW * late + 4 * (rows + DEPTH - late) <= cols:
        return spread(state, residual, shift_rows, shear_offset)
    return gathered(state, residual, shift_rows, shear_offset)


def solution(mesh):
    return jax.shard_map(
        local,
        mesh=mesh,
        in_specs=(P(None, None, "gx", "gy"), P(), P("gx"), P()),
        out_specs=P(None, None, "gx", "gy"),
        check_vma=False,
    )
```

```python
import functools

import jax
import jax.numpy as jnp
from jax import lax
from jax.experimental import pallas as pl
from jax.experimental.pallas import tpu as pltpu
from jax.sharding import PartitionSpec as P

time_step = 0.2
viscous = 0.1
resist = 0.1
sound_sq = 1.0
rotation = 0.5
shear_rate = 1.5

MESH = pl.DeviceIdType.MESH
DEPTH = 2
WINDOW = 12
EARLY = (1, 0)


def late_rows(rows):
    return range(rows // 4 + EARLY[0], 3 * rows // 4 - EARLY[1])


class Copies:
    def __init__(self, send, recv):
        self.send, self.recv, self.made = send, recv, []

    def start(self, source, target, device):
        k = len(self.made)
        copy = pltpu.make_async_remote_copy(
            src_ref=source,
            dst_ref=target,
            send_sem=self.send.at[k],
            recv_sem=self.recv.at[k],
            device_id=device,
            device_id_type=MESH,
        )
        copy.start()
        self.made.append(copy)
        return copy


def copy_count(chips):
    return 8 + sum(10 if 2 * s < chips else 6 for s in range(1, chips // 2 + 1)) + 8 * (chips // 2 + 1)


def gather(state_ref, grid_ref, copies, local_sem, groups, radial):
    rows = state_ref.shape[0]
    chips = groups // 2
    half = rows // 2
    gx, gy = lax.axis_index("gx"), lax.axis_index("gy")
    chip, core = gy // 2, gy % 2

    def at_chip(offset):
        return lax.rem(chip + offset + chips, chips) * 2 + core

    right, left = (gx, at_chip(1)), (gx, at_chip(-1))
    twin = (gx, chip * 2 + (1 - core))
    x_next = (lax.rem(gx + 1, radial), gy)
    x_prev = (lax.rem(gx + radial - 1, radial), gy)

    barrier = pltpu.get_barrier_semaphore()
    for other in (right, left, twin, x_next, x_prev):
        pl.semaphore_signal(barrier, inc=1, device_id=other, device_id_type=MESH)
    pl.semaphore_wait(barrier, 5)

    def piece(block, part):
        return grid_ref.at[block, pl.ds(DEPTH + part * half, half)]

    def low_rows(block):
        return grid_ref.at[block, pl.ds(0, DEPTH)]

    def high_rows(block):
        return grid_ref.at[block, pl.ds(DEPTH + rows, DEPTH)]

    def send_rows(block, part, source):
        if part == 0:
            edge = source.at[pl.ds(0, DEPTH)]
            return block, 0, copies.start(edge, high_rows(block), x_prev)
        edge = source.at[pl.ds(half - DEPTH, DEPTH)]
        return block, 1, copies.start(edge, low_rows(block), x_next)

    to_twin = []

    def pass_rows(sent):
        for block, part, copy in sent:
            copy.wait_recv()
            strip = high_rows(block) if part == 0 else low_rows(block)
            to_twin.append(copies.start(strip, strip, twin))

    own = [state_ref.at[pl.ds(0, half)], state_ref.at[pl.ds(half, half)]]
    keep = pltpu.make_async_copy(state_ref, grid_ref.at[gy, pl.ds(DEPTH, rows)], local_sem)

    flights = []
    order = [(0, 0), (1, 1), (0, 1), (1, 0)] if chips > 2 else [(0, 0), (1, 1)]
    for way, part in order:
        flights.append(
            (way, part, copies.start(own[part], piece(gy, part), right if way == 0 else left))
        )
    sent = [send_rows(gy, part, own[part]) for part in (0, 1)]
    for part in (0, 1):
        to_twin.append(copies.start(own[part], piece(gy, part), twin))
    keep.start()
    pass_rows(sent)
    for step in range(1, chips // 2 + 1):
        later, sent = [], []
        for way, part, copy in flights:
            block = at_chip(-step if way == 0 else step)
            copy.wait_recv()
            ref = piece(block, part)
            if 2 * (step + 1) < chips or (2 * (step + 1) == chips and part == way):
                later.append((way, part, copies.start(ref, ref, right if way == 0 else left)))
            to_twin.append(copies.start(ref, ref, twin))
            sent.append(send_rows(block, part, ref))
        pass_rows(sent)
        flights = later
    keep.wait()
    for copy in to_twin:
        copy.wait_recv()
    for copy in copies.made:
        copy.wait_send()


def row_sweep(load, first_row, last_row, drift_of, emit, unroll=4, base=0):
    def y_ahead(a):
        return pltpu.roll(a, a.shape[1] - 1, 1)

    def y_behind(a):
        return pltpu.roll(a, 1, 1)

    def z_ahead(a):
        return pltpu.roll(a, a.shape[0] - 1, 0)

    def z_behind(a):
        return pltpu.roll(a, 1, 0)

    def cells(by, bz):
        return 0.5 * (by + y_ahead(by)), 0.5 * (bz + z_ahead(bz))

    def radial_edges(prev, cur, prev_drift, cur_drift):
        sum_x = prev[1] + cur[1]
        sum_w = (prev[2] + prev_drift) + (cur[2] + cur_drift)
        sum_z = prev[3] + cur[3]
        bx, by, bz = cur[5], cur[6], cur[7]
        bx_y, bx_z = y_behind(bx), z_behind(bx)
        emf_z = 0.125 * (
            (sum_w + y_behind(sum_w)) * (bx + bx_y) - (sum_x + y_behind(sum_x)) * (by + prev[6])
        ) + resist * ((by - prev[6]) - (bx - bx_y))
        emf_y = 0.125 * (
            (sum_x + z_behind(sum_x)) * (bz + prev[7]) - (sum_z + z_behind(sum_z)) * (bx + bx_z)
        ) + resist * ((bx - bx_z) - (bz - prev[7]))
        return emf_z, emf_y

    start_prev, start_cur = load(first_row - 1), load(first_row)
    carry = (
        *cells(start_prev[6], start_prev[7]),
        *cells(start_cur[6], start_cur[7]),
        *radial_edges(start_prev, start_cur, drift_of(first_row - 1), drift_of(first_row)),
    )

    def one(row, carry):
        cy_prev, cz_prev, cy, cz, emf_z, emf_y = carry
        prev, cur, nxt = load(row - 1), load(row), load(row + 1)
        drift = drift_of(row)
        log_rho, vx, vy, vz, ent, bx, by, bz = cur
        w = vy + drift
        cy_next, cz_next = cells(nxt[6], nxt[7])
        emf_z_next, emf_y_next = radial_edges(cur, nxt, drift, drift_of(row + 1))

        half_x, half_w, half_z = 0.5 * vx, 0.5 * w, 0.5 * vz
        diffs, advs = [], []
        for f in range(5):
            a = cur[f]
            ya, yb, za, zb = y_ahead(a), y_behind(a), z_ahead(a), z_behind(a)
            dx, dy, dz = nxt[f] - prev[f], ya - yb, za - zb
            lap = ((nxt[f] + prev[f]) + (ya + yb) + (za + zb)) - 6.0 * a
            diffs.append((dx, dy, dz))
            advs.append(viscous * lap - (half_x * dx + half_w * dy + half_z * dz))

        sum_bx = bx + nxt[5]
        cx = 0.5 * sum_bx
        cur_x = 0.5 * ((y_ahead(cz) - y_behind(cz)) - (z_ahead(cy) - z_behind(cy)))
        cur_y = 0.5 * ((z_ahead(cx) - z_behind(cx)) - (cz_next - cz_prev))
        cur_z = 0.5 * ((cy_next - cy_prev) - (y_ahead(cx) - y_behind(cx)))
        inverse = jnp.exp(-log_rho)
        force_x = inverse * (cur_y * cz - cur_z * cy)
        force_y = inverse * (cur_z * cx - cur_x * cz)
        force_z = inverse * (cur_x * cy - cur_y * cx)

        pairs = [diffs[0][d] + diffs[4][d] for d in range(3)]
        rates = [
            advs[0] - 0.5 * (diffs[1][0] + diffs[2][1] + diffs[3][2]),
            advs[1] - (0.5 * sound_sq) * pairs[0] + force_x + (2.0 * rotation) * vy,
            advs[2] - (0.5 * sound_sq) * pairs[1] + force_y - ((2.0 - shear_rate) * rotation) * vx,
            advs[3] - (0.5 * sound_sq) * pairs[2] + force_z,
            advs[4] + resist * inverse * (cur_x * cur_x + cur_y * cur_y + cur_z * cur_z),
        ]

        w_y, z_y = w + y_behind(w), vz + y_behind(vz)
        bz_y, by_z = y_behind(bz), z_behind(by)
        emf_x = 0.125 * (
            (z_y + z_behind(z_y)) * (by + by_z) - (w_y + z_behind(w_y)) * (bz + bz_y)
        ) + resist * ((bz - bz_y) - (by - by_z))
        stretch = 0.25 * (sum_bx + y_behind(sum_bx))
        rates.append((z_ahead(emf_y) - emf_y) - (y_ahead(emf_z) - emf_z))
        rates.append(
            (emf_z_next - emf_z) - (z_ahead(emf_x) - emf_x) - (shear_rate * rotation) * stretch
        )
        rates.append((y_ahead(emf_x) - emf_x) - (emf_y_next - emf_y))
        emit(row, cur, rates)
        return cy, cz, cy_next, cz_next, emf_z_next, emf_y_next

    if last_row - first_row < 6:
        for row in range(first_row, last_row + 1):
            carry = one(row + base, carry)
        return
    lax.fori_loop(first_row, last_row + 1, one, carry, unroll=unroll)


def step_kernel(
    groups, radial, state_ref, table_ref, drift_ref, out_ref,
    grid_ref, moved_ref, first_ref, send, recv, local_sem,
):
    rows, fields, _, cols = state_ref.shape
    gather(state_ref, grid_ref, Copies(send, recv), local_sem, groups, radial)

    lane = lax.broadcasted_iota(jnp.int32, state_ref.shape[2:], 1)

    def turn(row, _):
        amount = table_ref[4, row]
        inside = lane < cols - amount
        low_side = lane < cols // 2
        blocks = [table_ref[k, row] for k in range(4)]
        for f in range(fields):
            before, here, after, beyond = [
                pltpu.roll(grid_ref[b, row, f], cols - amount, 1) for b in blocks
            ]
            moved_ref[row, f, :, :cols] = jnp.where(inside, here, after)
            moved_ref[row, f, :, cols:] = jnp.where(
                low_side, jnp.where(inside, after, beyond), jnp.where(inside, before, here)
            )
        return 0

    lax.fori_loop(0, rows + 2 * DEPTH, turn, 0)

    def drift_of(row):
        return drift_ref[row]

    def emit_first(row, cur, rates):
        for f in range(fields):
            first_ref[row, f] = cur[f] + time_step * rates[f]

    def emit_out(row, cur, rates):
        for f in range(fields):
            second = cur[f][:, :cols] + time_step * rates[f][:, :cols]
            out_ref[row - DEPTH, f] = 0.5 * (moved_ref[row, f, :, :cols] + second)

    def load_from(ref):
        return lambda row: [ref[row, f] for f in range(fields)]

    row_sweep(load_from(moved_ref), 1, rows + 2, drift_of, emit_first)
    row_sweep(load_from(first_ref), 2, rows + 1, drift_of, emit_out)


def gathered(state, residual, shift_rows, shear_offset):
    fields, vertical, rows, cols = state.shape
    groups, radial = lax.axis_size("gy"), lax.axis_size("gx")
    gx, gy = lax.axis_index("gx"), lax.axis_index("gy")
    cells_y = cols * groups
    wide = rows + 2 * DEPTH

    up = [(i, (i + 1) % radial) for i in range(radial)]
    down = [(target, source) for source, target in up]
    low = lax.ppermute(shift_rows[-DEPTH:], "gx", up)
    high = lax.ppermute(shift_rows[:DEPTH], "gx", down)
    offset = shear_offset[0]
    low = low - jnp.where(gx == 0, offset, 0)
    high = high + jnp.where(gx == radial - 1, offset, 0)
    amounts = jnp.concatenate([low, shift_rows, high])
    origin = (cols * gy - amounts) % cells_y
    block, part = origin // cols, origin % cols
    table = jnp.stack(
        [(block + groups - 1) % groups, block, (block + 1) % groups, (block + 2) % groups, part]
    )
    padded = jnp.concatenate([residual[-DEPTH:], residual, residual[:DEPTH]])
    drift = lax.dynamic_slice_in_dim(padded, gx * rows, wide)

    count = copy_count(groups // 2)
    out = pl.pallas_call(
        functools.partial(step_kernel, groups, radial),
        out_shape=jax.ShapeDtypeStruct((rows, fields, vertical, cols), jnp.float32),
        in_specs=[
            pl.BlockSpec(memory_space=pltpu.VMEM),
            pl.BlockSpec(memory_space=pltpu.SMEM),
            pl.BlockSpec(memory_space=pltpu.SMEM),
        ],
        out_specs=pl.BlockSpec(memory_space=pltpu.VMEM),
        scratch_shapes=[
            pltpu.VMEM((groups, wide, fields, vertical, cols), jnp.float32),
            pltpu.VMEM((wide, fields, vertical, 2 * cols), jnp.float32),
            pltpu.VMEM((wide, fields, vertical, 2 * cols), jnp.float32),
            pltpu.SemaphoreType.DMA((count,)),
            pltpu.SemaphoreType.DMA((count,)),
            pltpu.SemaphoreType.DMA,
        ],
        compiler_params=pltpu.CompilerParams(collective_id=0, has_side_effects=True),
    )(jnp.transpose(state, (2, 0, 1, 3)), table, drift)
    return jnp.transpose(out, (1, 2, 0, 3))


def spread_kernel(
    groups, radial, state_ref, shift_hbm, offset_hbm, residual_hbm, out_ref,
    shift_ref, offset_ref, residual_ref, taken_0, taken_1, taken_2, taken_3, turned_ref, edge_ref,
    shear_ref, moved_ref, own_edges, low_edges, high_edges, first_ref, windows_ref, drifts_ref, send, recv, local_sems,
):
    fields, vertical, rows, cols = state_ref.shape
    quarter = rows // 4
    taken = (taken_0, taken_1, taken_2, taken_3)
    late = late_rows(rows)
    others_start = WINDOW * len(late)
    short = [row for row in range(rows + DEPTH) if row not in late]
    lane_of = {row: WINDOW * k for k, row in enumerate(late)}
    lane_of.update({row: others_start + 4 * k for k, row in enumerate(short)})
    cells_y = cols * groups
    gx, gy = lax.axis_index("gx"), lax.axis_index("gy")
    x_next = (lax.rem(gx + 1, radial), gy)
    x_prev = (lax.rem(gx + radial - 1, radial), gy)
    others = [(gx, lax.rem(gy + k, groups)) for k in range(1, groups)]
    first_x, last_x = gx == 0, gx == radial - 1
    zero = gx // radial
    not_first, not_last = gx > 0, gx < radial - 1
    out_sent, back_sent, edges_sent, shear_sent, ends_sent, down_sent, up_sent = range(7)
    back_got = (4, 5, 6, 14, 15, 16)
    edges_got, shear_got, ends_got, rows_got, sides_got = 7, 8, 9, (10, 11), (12, 13)

    def remote(source, target, device, sent, got):
        return pltpu.make_async_remote_copy(
            src_ref=source,
            dst_ref=target,
            send_sem=send.at[sent],
            recv_sem=recv.at[got],
            device_id=device,
            device_id_type=MESH,
        )

    def spread_out(source, target, sent, got):
        for other in others:
            remote(source(other[1]), target, other, sent, got).start()
        pltpu.make_async_copy(source(gy), target, recv.at[got]).start()

    def arrived(ref, got):
        pltpu.make_async_copy(ref, ref, recv.at[got]).wait()

    def left(ref, sent):
        pltpu.make_async_copy(ref, ref, send.at[sent]).wait()

    small = [
        pltpu.make_async_copy(source, target, local_sems.at[k])
        for k, (source, target) in enumerate(
            ((shift_hbm, shift_ref), (offset_hbm, offset_ref), (residual_hbm, residual_ref))
        )
    ]
    for copy in small:
        copy.start()
    barrier = pltpu.get_barrier_semaphore()
    for other in (*others, x_prev, x_next):
        pl.semaphore_signal(barrier, inc=1, device_id=other, device_id_type=MESH)
    pl.semaphore_wait(barrier, groups + 1)

    def quarter_rows(q):
        return pl.ds(q * quarter, quarter)

    for pair in ((0, 3), (1, 2)):
        for other in others:
            for q in pair:
                remote(
                    state_ref.at[other[1], :, quarter_rows(q)], taken[q].at[gy], other, out_sent, q
                ).start()
        for q in pair:
            pltpu.make_async_copy(
                state_ref.at[gy, :, quarter_rows(q)], taken[q].at[gy], recv.at[q]
            ).start()

    lane = lax.broadcasted_iota(jnp.int32, (vertical, cols), 1)
    empty = [jnp.zeros((vertical, cols), jnp.float32)] * groups

    def displace(block_of, amount, slot, packed):
        whole, part = amount // cols, amount % cols
        rolled = [
            pltpu.roll(block_of(lax.rem(k - whole + groups, groups)), part, 1)
            for k in range(groups)
        ]
        row = [jnp.where(lane < part, rolled[d - 1], rolled[d]) for d in range(groups)]
        base, long = lane_of[slot], slot in late
        width = WINDOW if long else 4
        mine = (lane >= base) & (lane < base + width)
        result = []
        for d in range(groups):
            turned_ref[d, slot] = row[d]
            before, here, after = row[d - 1], row[d], row[(d + 1) % groups]
            if long:
                after = jnp.where(lane < cols // 2, after, here)
                before = jnp.where(lane < cols // 2, here, before)
            turn = base + 4
            edges = jnp.where(
                lane < base + width // 2,
                pltpu.roll(after, turn % cols if long else base, 1),
                pltpu.roll(before, (base + width - 4 if long else base + 4) % cols, 1),
            )
            result.append(jnp.where(mine, edges, packed[d]))
        return result

    def displace_quarter(q, packed):
        arrived(taken[q], q)
        for place in range(quarter):
            row = q * quarter + place
            packed = displace(
                lambda b: taken[q][b, :, place, :], shift_ref[row], row, packed
            )
        return packed

    def main_lanes(block, first_row, count):
        return moved_ref.at[block, pl.ds(first_row, count)]

    pieces = (
        (0, quarter),
        (3 * quarter, quarter),
        (quarter, EARLY[0]),
        (3 * quarter - EARLY[1], EARLY[1]),
        (late[0], len(late) // 2),
        (late[len(late) // 2], len(late) - len(late) // 2),
    )

    def send_back(piece):
        first, count = pieces[piece]
        if count:
            spread_out(
                lambda d: turned_ref.at[d, pl.ds(first, count)],
                main_lanes(gy, DEPTH + first, count),
                back_sent,
                back_got[piece],
            )

    def wait_back(piece):
        first, count = pieces[piece]
        if count:
            arrived(main_lanes(slice(None), DEPTH + first, count), back_got[piece])

    for copy in small:
        copy.wait()
    packed = displace_quarter(0, empty)
    packed = displace_quarter(3, packed)
    to_last = remote(turned_ref.at[:, pl.ds(0, DEPTH)], shear_ref, x_prev, ends_sent, ends_got)
    to_first = remote(
        turned_ref.at[:, pl.ds(rows - DEPTH, DEPTH)], shear_ref, x_next, ends_sent, ends_got
    )
    pl.when(first_x)(to_last.start)
    pl.when(last_x)(to_first.start)
    for piece in (0, 1):
        send_back(piece)

    low_row, high_row = 0, DEPTH + rows
    offset = offset_ref[0]
    for d in range(groups):
        edge_ref[d] = empty[0]

    def sheared(first_row, amount):
        arrived(shear_ref, ends_got)
        edges = empty
        for place in range(DEPTH):
            edges = displace(
                lambda b: shear_ref[b, place], amount, rows + place, edges
            )
        for d in range(groups):
            edge_ref[d] = edges[d]
        spread_out(
            lambda d: turned_ref.at[d, pl.ds(rows, DEPTH)],
            main_lanes(gy, first_row, DEPTH),
            shear_sent,
            shear_got,
        )

    @pl.when(first_x)
    def _():
        sheared(low_row, lax.rem(cells_y - offset, cells_y))

    @pl.when(last_x)
    def _():
        sheared(high_row, offset)

    packed = displace_quarter(1, packed)
    packed = displace_quarter(2, packed)
    for d in range(groups):
        edge_ref[d] = jnp.where(lane < lane_of[rows], packed[d], edge_ref[d])
    spread_out(lambda d: edge_ref.at[d], own_edges.at[gy], edges_sent, edges_got)
    for piece in (2, 3):
        send_back(piece)

    every = slice(None)
    for piece in (0, 1):
        wait_back(piece)
    rows_down = remote(
        main_lanes(every, DEPTH, DEPTH), main_lanes(every, high_row, DEPTH),
        x_prev, down_sent, rows_got[1],
    )
    rows_up = remote(
        main_lanes(every, rows, DEPTH), main_lanes(every, low_row, DEPTH),
        x_next, up_sent, rows_got[0],
    )
    edges_down = remote(own_edges, high_edges, x_prev, down_sent, sides_got[1])
    edges_up = remote(own_edges, low_edges, x_next, up_sent, sides_got[0])
    pl.when(not_first)(rows_down.start)
    pl.when(not_last)(rows_up.start)
    send_back(4)
    send_back(5)
    arrived(own_edges, edges_got)
    pl.when(not_first)(edges_down.start)
    pl.when(not_last)(edges_up.start)

    start = gx * rows - DEPTH + residual_ref.shape[0]

    def drift_of(row):
        return residual_ref[lax.rem(start + row, residual_ref.shape[0])]

    windows = cols // WINDOW
    kept = windows - 2 * DEPTH

    def emit_first(row, cur, rates):
        for f in range(fields):
            first_ref[row, f] = cur[f] + time_step * rates[f]

    def emit_whole(row, cur, rates):
        i = (row - DEPTH) // kept
        base = WINDOW * (row - i * kept)
        for f in range(fields):
            sides = windows_ref[i, f]
            low = pltpu.roll(sides, 2 * cols - base - 8, 1)
            high = pltpu.roll(sides, 2 * cols - base - 4, 1)
            total = moved_ref[f, row] + (cur[f] + time_step * rates[f])
            middle = jnp.where(lane >= cols - 2, high, total)
            out_ref[f, :, row - DEPTH, :] = jnp.where(lane < 2, low, middle)

    def stage_one(low, high):
        row_sweep(
            lambda row: [moved_ref[f, row] for f in range(fields)],
            DEPTH + low, DEPTH + high, drift_of, emit_first, 3, zero,
        )

    def stage_two(low, high):
        row_sweep(
            lambda row: [first_ref[row, f] for f in range(fields)],
            DEPTH + low, DEPTH + high, drift_of, emit_whole, 4, zero,
        )

    starts = range(-DEPTH, rows - DEPTH, kept)

    def in_window(k, low, high):
        return (lane >= WINDOW * k + low) & (lane < WINDOW * k + high)

    def rows_of(start):
        return range(start, min(start + windows, rows + DEPTH))

    def window_drift(start):
        total = empty[0]
        for k, row in enumerate(rows_of(start)):
            total = jnp.where(in_window(k, 0, WINDOW), drift_of(DEPTH + row), total)
        return total

    def fill_all(first_row, count, edges_ref, first_place):
        for i in range(len(starts)):
            held = [
                (k, row) for k, row in enumerate(rows_of(starts[i]))
                if first_row <= row < first_row + count and row not in late
            ]
            for f in range(fields):
                packed, value = edges_ref[f], windows_ref[i, f]
                for k, row in held:
                    base, from_lane = WINDOW * k, lane_of[first_place + row - first_row]
                    main = moved_ref[f, DEPTH + row]
                    for low, source, turn in (
                        (0, main, base + 4), (4, packed, base + 4 - from_lane), (8, main, base + 8)
                    ):
                        value = jnp.where(
                            in_window(k, low, low + 4), pltpu.roll(source, turn % cols, 1), value
                        )
                if held:
                    windows_ref[i, f] = value

    def fill_late():
        for i in range(len(starts)):
            held = [k for k, row in enumerate(rows_of(starts[i])) if row in late]
            if not held:
                continue
            from_lane = lane_of[starts[i] + held[0]]
            mine = (lane >= WINDOW * held[0]) & (lane < WINDOW * (held[-1] + 1))
            for f in range(fields):
                value = pltpu.roll(own_edges[f], (WINDOW * held[0] - from_lane) % cols, 1)
                windows_ref[i, f] = jnp.where(mine, value, windows_ref[i, f])

    def window_step(values, drift):
        turned = [
            [pltpu.roll(a, (WINDOW * (1 - r)) % cols, 1) for a in values] for r in range(3)
        ]
        drifts = [pltpu.roll(drift, (WINDOW * (1 - r)) % cols, 1) for r in range(3)]
        got = []
        row_sweep(
            lambda r: turned[r], 1, 1, lambda r: drifts[r],
            lambda r, cur, rates: got.extend(a + time_step * b for a, b in zip(cur, rates)),
        )
        return got

    def window_stages(i):
        drift = drifts_ref[i]
        moved = [windows_ref[i, f] for f in range(fields)]
        second = window_step(window_step(moved, drift), drift)
        for f in range(fields):
            windows_ref[i, f] = moved[f] + second[f]

    for i in range(len(starts)):
        drifts_ref[i] = window_drift(starts[i])
        for f in range(fields):
            windows_ref[i, f] = empty[0]
    fill_late()
    for piece in (2, 3):
        wait_back(piece)
    fill_all(0, rows, own_edges, 0)
    inside = [i for i in range(len(starts)) if starts[i] >= 0 and rows_of(starts[i])[-1] < rows]
    for i in inside:
        window_stages(i)
    stage_one(1, late[0] - 2)
    stage_one(late[-1] + 2, rows - 2)

    @pl.when(first_x)
    def _():
        arrived(main_lanes(every, low_row, DEPTH), shear_got)
        fill_all(-DEPTH, DEPTH, own_edges, rows)

    @pl.when(last_x)
    def _():
        arrived(main_lanes(every, high_row, DEPTH), shear_got)
        fill_all(rows, DEPTH, own_edges, rows)

    pl.when(not_first)(rows_up.wait_recv)
    pl.when(not_last)(rows_down.wait_recv)
    stage_one(-1, 0)
    stage_one(rows - 1, rows)

    @pl.when(not_first)
    def _():
        edges_up.wait_recv()
        fill_all(-DEPTH, DEPTH, low_edges, rows - DEPTH)

    @pl.when(not_last)
    def _():
        edges_down.wait_recv()
        fill_all(rows, DEPTH, high_edges, 0)

    for i in range(len(starts)):
        if i not in inside:
            window_stages(i)
    stage_two(0, late[0] - 3)
    stage_two(late[-1] + 3, rows - 1)
    wait_back(4)
    middle = late[len(late) // 2]
    stage_one(late[0] - 1, middle - 2)
    stage_two(late[0] - 2, middle - 3)
    wait_back(5)
    stage_one(middle - 1, late[-1] + 1)
    stage_two(middle - 2, late[-1] + 2)

    away = pl.ds(0, groups - 1)
    left(state_ref.at[away], out_sent)
    left(turned_ref.at[away, pl.ds(0, rows)], back_sent)
    left(edge_ref.at[away], edges_sent)

    @pl.when(first_x | last_x)
    def _():
        left(shear_ref, ends_sent)
        left(turned_ref.at[away, pl.ds(rows, DEPTH)], shear_sent)

    @pl.when(not_first)
    def _():
        rows_down.wait_send()
        edges_down.wait_send()

    @pl.when(not_last)
    def _():
        rows_up.wait_send()
        edges_up.wait_send()


def spread(state, residual, shift_rows, shear_offset):
    fields, vertical, rows, cols = state.shape
    groups, radial = lax.axis_size("gy"), lax.axis_size("gx")
    wide = rows + 2 * DEPTH
    parts = len(range(0, rows, cols // WINDOW - 2 * DEPTH))
    anywhere = pl.BlockSpec(memory_space=pl.ANY)
    vmem = pl.BlockSpec(memory_space=pltpu.VMEM)
    edges = pltpu.VMEM((groups, vertical, cols), jnp.float32)
    out = pl.pallas_call(
        functools.partial(spread_kernel, groups, radial),
        out_shape=pltpu.VMEM(state.shape, jnp.float32),
        in_specs=[anywhere] * 4,
        out_specs=vmem,
        scratch_shapes=[
            pltpu.SMEM(shift_rows.shape, jnp.int32),
            pltpu.SMEM(shear_offset.shape, jnp.int32),
            pltpu.SMEM(residual.shape, jnp.float32),
            *[pltpu.VMEM((groups, vertical, rows // 4, cols), jnp.float32)] * 4,
            pltpu.VMEM((groups, rows + DEPTH, vertical, cols), jnp.float32),
            edges,
            pltpu.VMEM((groups, DEPTH, vertical, cols), jnp.float32),
            pltpu.VMEM((fields, wide, vertical, cols), jnp.float32),
            edges,
            edges,
            edges,
            pltpu.VMEM((wide, fields, vertical, cols), jnp.float32),
            pltpu.VMEM((parts, fields, vertical, cols), jnp.float32),
            pltpu.VMEM((parts, vertical, cols), jnp.float32),
            pltpu.SemaphoreType.DMA((7,)),
            pltpu.SemaphoreType.DMA((17,)),
            pltpu.SemaphoreType.DMA((3,)),
        ],
        compiler_params=pltpu.CompilerParams(collective_id=1, has_side_effects=True),
    )(state, shift_rows, shear_offset, residual)
    return 0.5 * out


def local(state, residual, shift_rows, shear_offset):
    fields, _, rows, cols = state.shape
    paired = lax.axis_size("gy") == fields and lax.axis_size("gx") > 2
    late = len(late_rows(rows))
    if paired and rows % 16 == 0 and WINDOW * late + 4 * (rows + DEPTH - late) <= cols:
        return spread(state, residual, shift_rows, shear_offset)
    return gathered(state, residual, shift_rows, shear_offset)


def solution(mesh):
    return jax.shard_map(
        local,
        mesh=mesh,
        in_specs=(P(None, None, "gx", "gy"), P(), P("gx"), P()),
        out_specs=P(None, None, "gx", "gy"),
        check_vma=False,
    )
```

```python
import functools

import jax
import jax.numpy as jnp
from jax import lax
from jax.experimental import pallas as pl
from jax.experimental.pallas import tpu as pltpu
from jax.sharding import PartitionSpec as P

time_step = 0.2
viscous = 0.1
resist = 0.1
sound_sq = 1.0
rotation = 0.5
shear_rate = 1.5

MESH = pl.DeviceIdType.MESH
DEPTH = 2
WINDOW = 12
EARLY = (1, 0)


def late_rows(rows):
    return range(rows // 4 + EARLY[0], 3 * rows // 4 - EARLY[1])


class Copies:
    def __init__(self, send, recv):
        self.send, self.recv, self.made = send, recv, []

    def start(self, source, target, device):
        k = len(self.made)
        copy = pltpu.make_async_remote_copy(
            src_ref=source,
            dst_ref=target,
            send_sem=self.send.at[k],
            recv_sem=self.recv.at[k],
            device_id=device,
            device_id_type=MESH,
        )
        copy.start()
        self.made.append(copy)
        return copy


def copy_count(chips):
    return 8 + sum(10 if 2 * s < chips else 6 for s in range(1, chips // 2 + 1)) + 8 * (chips // 2 + 1)


def gather(state_ref, grid_ref, copies, local_sem, groups, radial):
    rows = state_ref.shape[0]
    chips = groups // 2
    half = rows // 2
    gx, gy = lax.axis_index("gx"), lax.axis_index("gy")
    chip, core = gy // 2, gy % 2

    def at_chip(offset):
        return lax.rem(chip + offset + chips, chips) * 2 + core

    right, left = (gx, at_chip(1)), (gx, at_chip(-1))
    twin = (gx, chip * 2 + (1 - core))
    x_next = (lax.rem(gx + 1, radial), gy)
    x_prev = (lax.rem(gx + radial - 1, radial), gy)

    barrier = pltpu.get_barrier_semaphore()
    for other in (right, left, twin, x_next, x_prev):
        pl.semaphore_signal(barrier, inc=1, device_id=other, device_id_type=MESH)
    pl.semaphore_wait(barrier, 5)

    def piece(block, part):
        return grid_ref.at[block, pl.ds(DEPTH + part * half, half)]

    def low_rows(block):
        return grid_ref.at[block, pl.ds(0, DEPTH)]

    def high_rows(block):
        return grid_ref.at[block, pl.ds(DEPTH + rows, DEPTH)]

    def send_rows(block, part, source):
        if part == 0:
            edge = source.at[pl.ds(0, DEPTH)]
            return block, 0, copies.start(edge, high_rows(block), x_prev)
        edge = source.at[pl.ds(half - DEPTH, DEPTH)]
        return block, 1, copies.start(edge, low_rows(block), x_next)

    to_twin = []

    def pass_rows(sent):
        for block, part, copy in sent:
            copy.wait_recv()
            strip = high_rows(block) if part == 0 else low_rows(block)
            to_twin.append(copies.start(strip, strip, twin))

    own = [state_ref.at[pl.ds(0, half)], state_ref.at[pl.ds(half, half)]]
    keep = pltpu.make_async_copy(state_ref, grid_ref.at[gy, pl.ds(DEPTH, rows)], local_sem)

    flights = []
    order = [(0, 0), (1, 1), (0, 1), (1, 0)] if chips > 2 else [(0, 0), (1, 1)]
    for way, part in order:
        flights.append(
            (way, part, copies.start(own[part], piece(gy, part), right if way == 0 else left))
        )
    sent = [send_rows(gy, part, own[part]) for part in (0, 1)]
    for part in (0, 1):
        to_twin.append(copies.start(own[part], piece(gy, part), twin))
    keep.start()
    pass_rows(sent)
    for step in range(1, chips // 2 + 1):
        later, sent = [], []
        for way, part, copy in flights:
            block = at_chip(-step if way == 0 else step)
            copy.wait_recv()
            ref = piece(block, part)
            if 2 * (step + 1) < chips or (2 * (step + 1) == chips and part == way):
                later.append((way, part, copies.start(ref, ref, right if way == 0 else left)))
            to_twin.append(copies.start(ref, ref, twin))
            sent.append(send_rows(block, part, ref))
        pass_rows(sent)
        flights = later
    keep.wait()
    for copy in to_twin:
        copy.wait_recv()
    for copy in copies.made:
        copy.wait_send()


def row_sweep(load, first_row, last_row, drift_of, emit, unroll=4, base=0):
    def y_ahead(a):
        return pltpu.roll(a, a.shape[1] - 1, 1)

    def y_behind(a):
        return pltpu.roll(a, 1, 1)

    def z_ahead(a):
        return pltpu.roll(a, a.shape[0] - 1, 0)

    def z_behind(a):
        return pltpu.roll(a, 1, 0)

    def cells(by, bz):
        return by + y_ahead(by), bz + z_ahead(bz)

    def radial_edges(prev, cur, prev_drift, cur_drift):
        sum_x = prev[1] + cur[1]
        sum_w = (prev[2] + prev_drift) + (cur[2] + cur_drift)
        sum_z = prev[3] + cur[3]
        bx, by, bz = cur[5], cur[6], cur[7]
        bx_y, bx_z = y_behind(bx), z_behind(bx)
        emf_z = 0.125 * (
            (sum_w + y_behind(sum_w)) * (bx + bx_y) - (sum_x + y_behind(sum_x)) * (by + prev[6])
        ) + resist * ((by - prev[6]) - (bx - bx_y))
        emf_y = 0.125 * (
            (sum_x + z_behind(sum_x)) * (bz + prev[7]) - (sum_z + z_behind(sum_z)) * (bx + bx_z)
        ) + resist * ((bx - bx_z) - (bz - prev[7]))
        return emf_z, emf_y

    start_prev, start_cur = load(first_row - 1), load(first_row)
    carry = (
        *cells(start_prev[6], start_prev[7]),
        *cells(start_cur[6], start_cur[7]),
        *radial_edges(start_prev, start_cur, drift_of(first_row - 1), drift_of(first_row)),
    )

    def one(row, carry):
        cy_prev, cz_prev, cy, cz, emf_z, emf_y = carry
        prev, cur, nxt = load(row - 1), load(row), load(row + 1)
        drift = drift_of(row)
        log_rho, vx, vy, vz, ent, bx, by, bz = cur
        w = vy + drift
        cy_next, cz_next = cells(nxt[6], nxt[7])
        emf_z_next, emf_y_next = radial_edges(cur, nxt, drift, drift_of(row + 1))

        half_x, half_w, half_z = 0.5 * vx, 0.5 * w, 0.5 * vz
        diffs, advs = [], []
        for f in range(5):
            a = cur[f]
            ya, yb, za, zb = y_ahead(a), y_behind(a), z_ahead(a), z_behind(a)
            dx, dy, dz = nxt[f] - prev[f], ya - yb, za - zb
            lap = ((nxt[f] + prev[f]) + (ya + yb) + (za + zb)) - 6.0 * a
            diffs.append((dx, dy, dz))
            advs.append(viscous * lap - (half_x * dx + half_w * dy + half_z * dz))

        sum_bx = bx + nxt[5]
        cx = sum_bx
        cur_x = (y_ahead(cz) - y_behind(cz)) - (z_ahead(cy) - z_behind(cy))
        cur_y = (z_ahead(cx) - z_behind(cx)) - (cz_next - cz_prev)
        cur_z = (cy_next - cy_prev) - (y_ahead(cx) - y_behind(cx))
        inverse = 0.125 * jnp.exp(-log_rho)
        force_x = inverse * (cur_y * cz - cur_z * cy)
        force_y = inverse * (cur_z * cx - cur_x * cz)
        force_z = inverse * (cur_x * cy - cur_y * cx)

        pairs = [diffs[0][d] + diffs[4][d] for d in range(3)]
        rates = [
            advs[0] - 0.5 * (diffs[1][0] + diffs[2][1] + diffs[3][2]),
            advs[1] - (0.5 * sound_sq) * pairs[0] + force_x + (2.0 * rotation) * vy,
            advs[2] - (0.5 * sound_sq) * pairs[1] + force_y - ((2.0 - shear_rate) * rotation) * vx,
            advs[3] - (0.5 * sound_sq) * pairs[2] + force_z,
            advs[4] + (0.5 * resist) * inverse * (cur_x * cur_x + cur_y * cur_y + cur_z * cur_z),
        ]

        w_y, z_y = w + y_behind(w), vz + y_behind(vz)
        bz_y, by_z = y_behind(bz), z_behind(by)
        emf_x = 0.125 * (
            (z_y + z_behind(z_y)) * (by + by_z) - (w_y + z_behind(w_y)) * (bz + bz_y)
        ) + resist * ((bz - bz_y) - (by - by_z))
        stretch = 0.25 * (sum_bx + y_behind(sum_bx))
        rates.append((z_ahead(emf_y) - emf_y) - (y_ahead(emf_z) - emf_z))
        rates.append(
            (emf_z_next - emf_z) - (z_ahead(emf_x) - emf_x) - (shear_rate * rotation) * stretch
        )
        rates.append((y_ahead(emf_x) - emf_x) - (emf_y_next - emf_y))
        emit(row, cur, rates)
        return cy, cz, cy_next, cz_next, emf_z_next, emf_y_next

    if last_row - first_row < 6:
        for row in range(first_row, last_row + 1):
            carry = one(row + base, carry)
        return
    lax.fori_loop(first_row, last_row + 1, one, carry, unroll=unroll)


def step_kernel(
    groups, radial, state_ref, table_ref, drift_ref, out_ref,
    grid_ref, moved_ref, first_ref, send, recv, local_sem,
):
    rows, fields, _, cols = state_ref.shape
    gather(state_ref, grid_ref, Copies(send, recv), local_sem, groups, radial)

    lane = lax.broadcasted_iota(jnp.int32, state_ref.shape[2:], 1)

    def turn(row, _):
        amount = table_ref[4, row]
        inside = lane < cols - amount
        low_side = lane < cols // 2
        blocks = [table_ref[k, row] for k in range(4)]
        for f in range(fields):
            before, here, after, beyond = [
                pltpu.roll(grid_ref[b, row, f], cols - amount, 1) for b in blocks
            ]
            moved_ref[row, f, :, :cols] = jnp.where(inside, here, after)
            moved_ref[row, f, :, cols:] = jnp.where(
                low_side, jnp.where(inside, after, beyond), jnp.where(inside, before, here)
            )
        return 0

    lax.fori_loop(0, rows + 2 * DEPTH, turn, 0)

    def drift_of(row):
        return drift_ref[row]

    def emit_first(row, cur, rates):
        for f in range(fields):
            first_ref[row, f] = cur[f] + time_step * rates[f]

    def emit_out(row, cur, rates):
        for f in range(fields):
            second = cur[f][:, :cols] + time_step * rates[f][:, :cols]
            out_ref[row - DEPTH, f] = 0.5 * (moved_ref[row, f, :, :cols] + second)

    def load_from(ref):
        return lambda row: [ref[row, f] for f in range(fields)]

    row_sweep(load_from(moved_ref), 1, rows + 2, drift_of, emit_first)
    row_sweep(load_from(first_ref), 2, rows + 1, drift_of, emit_out)


def gathered(state, residual, shift_rows, shear_offset):
    fields, vertical, rows, cols = state.shape
    groups, radial = lax.axis_size("gy"), lax.axis_size("gx")
    gx, gy = lax.axis_index("gx"), lax.axis_index("gy")
    cells_y = cols * groups
    wide = rows + 2 * DEPTH

    up = [(i, (i + 1) % radial) for i in range(radial)]
    down = [(target, source) for source, target in up]
    low = lax.ppermute(shift_rows[-DEPTH:], "gx", up)
    high = lax.ppermute(shift_rows[:DEPTH], "gx", down)
    offset = shear_offset[0]
    low = low - jnp.where(gx == 0, offset, 0)
    high = high + jnp.where(gx == radial - 1, offset, 0)
    amounts = jnp.concatenate([low, shift_rows, high])
    origin = (cols * gy - amounts) % cells_y
    block, part = origin // cols, origin % cols
    table = jnp.stack(
        [(block + groups - 1) % groups, block, (block + 1) % groups, (block + 2) % groups, part]
    )
    padded = jnp.concatenate([residual[-DEPTH:], residual, residual[:DEPTH]])
    drift = lax.dynamic_slice_in_dim(padded, gx * rows, wide)

    count = copy_count(groups // 2)
    out = pl.pallas_call(
        functools.partial(step_kernel, groups, radial),
        out_shape=jax.ShapeDtypeStruct((rows, fields, vertical, cols), jnp.float32),
        in_specs=[
            pl.BlockSpec(memory_space=pltpu.VMEM),
            pl.BlockSpec(memory_space=pltpu.SMEM),
            pl.BlockSpec(memory_space=pltpu.SMEM),
        ],
        out_specs=pl.BlockSpec(memory_space=pltpu.VMEM),
        scratch_shapes=[
            pltpu.VMEM((groups, wide, fields, vertical, cols), jnp.float32),
            pltpu.VMEM((wide, fields, vertical, 2 * cols), jnp.float32),
            pltpu.VMEM((wide, fields, vertical, 2 * cols), jnp.float32),
            pltpu.SemaphoreType.DMA((count,)),
            pltpu.SemaphoreType.DMA((count,)),
            pltpu.SemaphoreType.DMA,
        ],
        compiler_params=pltpu.CompilerParams(collective_id=0, has_side_effects=True),
    )(jnp.transpose(state, (2, 0, 1, 3)), table, drift)
    return jnp.transpose(out, (1, 2, 0, 3))


def spread_kernel(
    groups, radial, state_ref, shift_hbm, offset_hbm, residual_hbm, out_ref,
    shift_ref, offset_ref, residual_ref, taken_0, taken_1, taken_2, taken_3, turned_ref, edge_ref,
    shear_ref, moved_ref, own_edges, low_edges, high_edges, first_ref, windows_ref, drifts_ref, send, recv, local_sems,
):
    fields, vertical, rows, cols = state_ref.shape
    quarter = rows // 4
    taken = (taken_0, taken_1, taken_2, taken_3)
    late = late_rows(rows)
    others_start = WINDOW * len(late)
    short = [row for row in range(rows + DEPTH) if row not in late]
    lane_of = {row: WINDOW * k for k, row in enumerate(late)}
    lane_of.update({row: others_start + 4 * k for k, row in enumerate(short)})
    cells_y = cols * groups
    gx, gy = lax.axis_index("gx"), lax.axis_index("gy")
    x_next = (lax.rem(gx + 1, radial), gy)
    x_prev = (lax.rem(gx + radial - 1, radial), gy)
    others = [(gx, lax.rem(gy + k, groups)) for k in range(1, groups)]
    first_x, last_x = gx == 0, gx == radial - 1
    zero = gx // radial
    not_first, not_last = gx > 0, gx < radial - 1
    out_sent, back_sent, edges_sent, shear_sent, ends_sent, down_sent, up_sent = range(7)
    back_got = (4, 5, 6, 14, 15, 16)
    edges_got, shear_got, ends_got, rows_got, sides_got = 7, 8, 9, (10, 11), (12, 13)

    def remote(source, target, device, sent, got):
        return pltpu.make_async_remote_copy(
            src_ref=source,
            dst_ref=target,
            send_sem=send.at[sent],
            recv_sem=recv.at[got],
            device_id=device,
            device_id_type=MESH,
        )

    def spread_out(source, target, sent, got):
        for other in others:
            remote(source(other[1]), target, other, sent, got).start()
        pltpu.make_async_copy(source(gy), target, recv.at[got]).start()

    def arrived(ref, got):
        pltpu.make_async_copy(ref, ref, recv.at[got]).wait()

    def left(ref, sent):
        pltpu.make_async_copy(ref, ref, send.at[sent]).wait()

    small = [
        pltpu.make_async_copy(source, target, local_sems.at[k])
        for k, (source, target) in enumerate(
            ((shift_hbm, shift_ref), (offset_hbm, offset_ref), (residual_hbm, residual_ref))
        )
    ]
    for copy in small:
        copy.start()
    barrier = pltpu.get_barrier_semaphore()
    for other in (*others, x_prev, x_next):
        pl.semaphore_signal(barrier, inc=1, device_id=other, device_id_type=MESH)
    pl.semaphore_wait(barrier, groups + 1)

    def quarter_rows(q):
        return pl.ds(q * quarter, quarter)

    for pair in ((0, 3), (1, 2)):
        for other in others:
            for q in pair:
                remote(
                    state_ref.at[other[1], :, quarter_rows(q)], taken[q].at[gy], other, out_sent, q
                ).start()
        for q in pair:
            pltpu.make_async_copy(
                state_ref.at[gy, :, quarter_rows(q)], taken[q].at[gy], recv.at[q]
            ).start()

    lane = lax.broadcasted_iota(jnp.int32, (vertical, cols), 1)
    empty = [jnp.zeros((vertical, cols), jnp.float32)] * groups

    def displace(block_of, amount, slot, packed):
        whole, part = amount // cols, amount % cols
        rolled = [
            pltpu.roll(block_of(lax.rem(k - whole + groups, groups)), part, 1)
            for k in range(groups)
        ]
        row = [jnp.where(lane < part, rolled[d - 1], rolled[d]) for d in range(groups)]
        base, long = lane_of[slot], slot in late
        width = WINDOW if long else 4
        mine = (lane >= base) & (lane < base + width)
        result = []
        for d in range(groups):
            turned_ref[d, slot] = row[d]
            before, here, after = row[d - 1], row[d], row[(d + 1) % groups]
            if long:
                after = jnp.where(lane < cols // 2, after, here)
                before = jnp.where(lane < cols // 2, here, before)
            turn = base + 4
            edges = jnp.where(
                lane < base + width // 2,
                pltpu.roll(after, turn % cols if long else base, 1),
                pltpu.roll(before, (base + width - 4 if long else base + 4) % cols, 1),
            )
            result.append(jnp.where(mine, edges, packed[d]))
        return result

    def displace_quarter(q, packed):
        arrived(taken[q], q)
        for place in range(quarter):
            row = q * quarter + place
            packed = displace(
                lambda b: taken[q][b, :, place, :], shift_ref[row], row, packed
            )
        return packed

    def main_lanes(block, first_row, count):
        return moved_ref.at[block, pl.ds(first_row, count)]

    pieces = (
        (0, quarter),
        (3 * quarter, quarter),
        (quarter, EARLY[0]),
        (3 * quarter - EARLY[1], EARLY[1]),
        (late[0], len(late) // 2),
        (late[len(late) // 2], len(late) - len(late) // 2),
    )

    def send_back(piece):
        first, count = pieces[piece]
        if count:
            spread_out(
                lambda d: turned_ref.at[d, pl.ds(first, count)],
                main_lanes(gy, DEPTH + first, count),
                back_sent,
                back_got[piece],
            )

    def wait_back(piece):
        first, count = pieces[piece]
        if count:
            arrived(main_lanes(slice(None), DEPTH + first, count), back_got[piece])

    for copy in small:
        copy.wait()
    packed = displace_quarter(0, empty)
    packed = displace_quarter(3, packed)
    to_last = remote(turned_ref.at[:, pl.ds(0, DEPTH)], shear_ref, x_prev, ends_sent, ends_got)
    to_first = remote(
        turned_ref.at[:, pl.ds(rows - DEPTH, DEPTH)], shear_ref, x_next, ends_sent, ends_got
    )
    pl.when(first_x)(to_last.start)
    pl.when(last_x)(to_first.start)
    for piece in (0, 1):
        send_back(piece)

    low_row, high_row = 0, DEPTH + rows
    offset = offset_ref[0]
    for d in range(groups):
        edge_ref[d] = empty[0]

    def sheared(first_row, amount):
        arrived(shear_ref, ends_got)
        edges = empty
        for place in range(DEPTH):
            edges = displace(
                lambda b: shear_ref[b, place], amount, rows + place, edges
            )
        for d in range(groups):
            edge_ref[d] = edges[d]
        spread_out(
            lambda d: turned_ref.at[d, pl.ds(rows, DEPTH)],
            main_lanes(gy, first_row, DEPTH),
            shear_sent,
            shear_got,
        )

    @pl.when(first_x)
    def _():
        sheared(low_row, lax.rem(cells_y - offset, cells_y))

    @pl.when(last_x)
    def _():
        sheared(high_row, offset)

    packed = displace_quarter(1, packed)
    packed = displace_quarter(2, packed)
    for d in range(groups):
        edge_ref[d] = jnp.where(lane < lane_of[rows], packed[d], edge_ref[d])
    spread_out(lambda d: edge_ref.at[d], own_edges.at[gy], edges_sent, edges_got)
    for piece in (2, 3):
        send_back(piece)

    every = slice(None)
    for piece in (0, 1):
        wait_back(piece)
    rows_down = remote(
        main_lanes(every, DEPTH, DEPTH), main_lanes(every, high_row, DEPTH),
        x_prev, down_sent, rows_got[1],
    )
    rows_up = remote(
        main_lanes(every, rows, DEPTH), main_lanes(every, low_row, DEPTH),
        x_next, up_sent, rows_got[0],
    )
    edges_down = remote(own_edges, high_edges, x_prev, down_sent, sides_got[1])
    edges_up = remote(own_edges, low_edges, x_next, up_sent, sides_got[0])
    pl.when(not_first)(rows_down.start)
    pl.when(not_last)(rows_up.start)
    send_back(4)
    send_back(5)
    arrived(own_edges, edges_got)
    pl.when(not_first)(edges_down.start)
    pl.when(not_last)(edges_up.start)

    start = gx * rows - DEPTH + residual_ref.shape[0]

    def drift_of(row):
        return residual_ref[lax.rem(start + row, residual_ref.shape[0])]

    windows = cols // WINDOW
    kept = windows - 2 * DEPTH

    def emit_first(row, cur, rates):
        for f in range(fields):
            first_ref[row, f] = cur[f] + time_step * rates[f]

    def emit_whole(row, cur, rates):
        i = (row - DEPTH) // kept
        base = WINDOW * (row - i * kept)
        for f in range(fields):
            sides = windows_ref[i, f]
            low = pltpu.roll(sides, cols - base - 8, 1)
            high = pltpu.roll(sides, cols - base - 4, 1)
            total = moved_ref[f, row] + (cur[f] + time_step * rates[f])
            middle = jnp.where(lane >= cols - 2, high, total)
            out_ref[f, :, row - DEPTH, :] = jnp.where(lane < 2, low, middle)

    def stage_one(low, high):
        row_sweep(
            lambda row: [moved_ref[f, row] for f in range(fields)],
            DEPTH + low, DEPTH + high, drift_of, emit_first, 3, zero,
        )

    def stage_two(low, high):
        row_sweep(
            lambda row: [first_ref[row, f] for f in range(fields)],
            DEPTH + low, DEPTH + high, drift_of, emit_whole, 4, zero,
        )

    starts = range(-DEPTH, rows - DEPTH, kept)

    def in_window(k, low, high):
        return (lane >= WINDOW * k + low) & (lane < WINDOW * k + high)

    def rows_of(start):
        return range(start, min(start + windows, rows + DEPTH))

    def window_drift(start):
        total = empty[0]
        for k, row in enumerate(rows_of(start)):
            total = jnp.where(in_window(k, 0, WINDOW), drift_of(DEPTH + row), total)
        return total

    def fill_all(first_row, count, edges_ref, first_place):
        for i in range(len(starts)):
            held = [
                (k, row) for k, row in enumerate(rows_of(starts[i]))
                if first_row <= row < first_row + count and row not in late
            ]
            for f in range(fields):
                packed, value = edges_ref[f], windows_ref[i, f]
                for k, row in held:
                    base, from_lane = WINDOW * k, lane_of[first_place + row - first_row]
                    main = moved_ref[f, DEPTH + row]
                    for low, source, turn in (
                        (0, main, base + 4), (4, packed, base + 4 - from_lane), (8, main, base + 8)
                    ):
                        value = jnp.where(
                            in_window(k, low, low + 4), pltpu.roll(source, turn % cols, 1), value
                        )
                if held:
                    windows_ref[i, f] = value

    def fill_late():
        for i in range(len(starts)):
            held = [k for k, row in enumerate(rows_of(starts[i])) if row in late]
            if not held:
                continue
            from_lane = lane_of[starts[i] + held[0]]
            mine = (lane >= WINDOW * held[0]) & (lane < WINDOW * (held[-1] + 1))
            for f in range(fields):
                value = pltpu.roll(own_edges[f], (WINDOW * held[0] - from_lane) % cols, 1)
                windows_ref[i, f] = jnp.where(mine, value, windows_ref[i, f])

    def window_step(values, drift):
        turned = [
            [pltpu.roll(a, (WINDOW * (1 - r)) % cols, 1) for a in values] for r in range(3)
        ]
        drifts = [pltpu.roll(drift, (WINDOW * (1 - r)) % cols, 1) for r in range(3)]
        got = []
        row_sweep(
            lambda r: turned[r], 1, 1, lambda r: drifts[r],
            lambda r, cur, rates: got.extend(a + time_step * b for a, b in zip(cur, rates)),
        )
        return got

    def window_stages(i):
        drift = drifts_ref[i]
        moved = [windows_ref[i, f] for f in range(fields)]
        second = window_step(window_step(moved, drift), drift)
        for f in range(fields):
            windows_ref[i, f] = moved[f] + second[f]

    for i in range(len(starts)):
        drifts_ref[i] = window_drift(starts[i])
        for f in range(fields):
            windows_ref[i, f] = empty[0]
    fill_late()
    for piece in (2, 3):
        wait_back(piece)
    fill_all(0, rows, own_edges, 0)
    inside = [i for i in range(len(starts)) if starts[i] >= 0 and rows_of(starts[i])[-1] < rows]
    for i in inside:
        window_stages(i)
    stage_one(1, late[0] - 2)
    stage_one(late[-1] + 2, rows - 2)

    @pl.when(first_x)
    def _():
        arrived(main_lanes(every, low_row, DEPTH), shear_got)
        fill_all(-DEPTH, DEPTH, own_edges, rows)

    @pl.when(last_x)
    def _():
        arrived(main_lanes(every, high_row, DEPTH), shear_got)
        fill_all(rows, DEPTH, own_edges, rows)

    pl.when(not_first)(rows_up.wait_recv)
    pl.when(not_last)(rows_down.wait_recv)
    stage_one(-1, 0)
    stage_one(rows - 1, rows)

    @pl.when(not_first)
    def _():
        edges_up.wait_recv()
        fill_all(-DEPTH, DEPTH, low_edges, rows - DEPTH)

    @pl.when(not_last)
    def _():
        edges_down.wait_recv()
        fill_all(rows, DEPTH, high_edges, 0)

    for i in range(len(starts)):
        if i not in inside:
            window_stages(i)
    stage_two(0, late[0] - 3)
    stage_two(late[-1] + 3, rows - 1)
    wait_back(4)
    middle = late[len(late) // 2]
    stage_one(late[0] - 1, middle - 2)
    stage_two(late[0] - 2, middle - 3)
    wait_back(5)
    stage_one(middle - 1, late[-1] + 1)
    stage_two(middle - 2, late[-1] + 2)

    away = pl.ds(0, groups - 1)
    left(state_ref.at[away], out_sent)
    left(turned_ref.at[away, pl.ds(0, rows)], back_sent)
    left(edge_ref.at[away], edges_sent)

    @pl.when(first_x | last_x)
    def _():
        left(shear_ref, ends_sent)
        left(turned_ref.at[away, pl.ds(rows, DEPTH)], shear_sent)

    @pl.when(not_first)
    def _():
        rows_down.wait_send()
        edges_down.wait_send()

    @pl.when(not_last)
    def _():
        rows_up.wait_send()
        edges_up.wait_send()


def spread(state, residual, shift_rows, shear_offset):
    fields, vertical, rows, cols = state.shape
    groups, radial = lax.axis_size("gy"), lax.axis_size("gx")
    wide = rows + 2 * DEPTH
    parts = len(range(0, rows, cols // WINDOW - 2 * DEPTH))
    anywhere = pl.BlockSpec(memory_space=pl.ANY)
    vmem = pl.BlockSpec(memory_space=pltpu.VMEM)
    edges = pltpu.VMEM((groups, vertical, cols), jnp.float32)
    out = pl.pallas_call(
        functools.partial(spread_kernel, groups, radial),
        out_shape=pltpu.VMEM(state.shape, jnp.float32),
        in_specs=[anywhere] * 4,
        out_specs=vmem,
        scratch_shapes=[
            pltpu.SMEM(shift_rows.shape, jnp.int32),
            pltpu.SMEM(shear_offset.shape, jnp.int32),
            pltpu.SMEM(residual.shape, jnp.float32),
            *[pltpu.VMEM((groups, vertical, rows // 4, cols), jnp.float32)] * 4,
            pltpu.VMEM((groups, rows + DEPTH, vertical, cols), jnp.float32),
            edges,
            pltpu.VMEM((groups, DEPTH, vertical, cols), jnp.float32),
            pltpu.VMEM((fields, wide, vertical, cols), jnp.float32),
            edges,
            edges,
            edges,
            pltpu.VMEM((wide, fields, vertical, cols), jnp.float32),
            pltpu.VMEM((parts, fields, vertical, cols), jnp.float32),
            pltpu.VMEM((parts, vertical, cols), jnp.float32),
            pltpu.SemaphoreType.DMA((7,)),
            pltpu.SemaphoreType.DMA((17,)),
            pltpu.SemaphoreType.DMA((3,)),
        ],
        compiler_params=pltpu.CompilerParams(collective_id=1, has_side_effects=True),
    )(state, shift_rows, shear_offset, residual)
    return 0.5 * out


def local(state, residual, shift_rows, shear_offset):
    fields, _, rows, cols = state.shape
    paired = lax.axis_size("gy") == fields and lax.axis_size("gx") > 2
    late = len(late_rows(rows))
    if paired and rows % 16 == 0 and WINDOW * late + 4 * (rows + DEPTH - late) <= cols:
        return spread(state, residual, shift_rows, shear_offset)
    return gathered(state, residual, shift_rows, shear_offset)


def solution(mesh):
    return jax.shard_map(
        local,
        mesh=mesh,
        in_specs=(P(None, None, "gx", "gy"), P(), P("gx"), P()),
        out_specs=P(None, None, "gx", "gy"),
        check_vma=False,
    )
```

```python
import functools

import jax
import jax.numpy as jnp
from jax import lax
from jax.experimental import pallas as pl
from jax.experimental.pallas import tpu as pltpu
from jax.sharding import PartitionSpec as P

time_step = 0.2
viscous = 0.1
resist = 0.1
sound_sq = 1.0
rotation = 0.5
shear_rate = 1.5

MESH = pl.DeviceIdType.MESH
DEPTH = 2
WINDOW = 12
EARLY = (1, 0)


def late_rows(rows):
    return range(rows // 4 + EARLY[0], 3 * rows // 4 - EARLY[1])


class Copies:
    def __init__(self, send, recv):
        self.send, self.recv, self.made = send, recv, []

    def start(self, source, target, device):
        k = len(self.made)
        copy = pltpu.make_async_remote_copy(
            src_ref=source,
            dst_ref=target,
            send_sem=self.send.at[k],
            recv_sem=self.recv.at[k],
            device_id=device,
            device_id_type=MESH,
        )
        copy.start()
        self.made.append(copy)
        return copy


def copy_count(chips):
    return 8 + sum(10 if 2 * s < chips else 6 for s in range(1, chips // 2 + 1)) + 8 * (chips // 2 + 1)


def gather(state_ref, grid_ref, copies, local_sem, groups, radial):
    rows = state_ref.shape[0]
    chips = groups // 2
    half = rows // 2
    gx, gy = lax.axis_index("gx"), lax.axis_index("gy")
    chip, core = gy // 2, gy % 2

    def at_chip(offset):
        return lax.rem(chip + offset + chips, chips) * 2 + core

    right, left = (gx, at_chip(1)), (gx, at_chip(-1))
    twin = (gx, chip * 2 + (1 - core))
    x_next = (lax.rem(gx + 1, radial), gy)
    x_prev = (lax.rem(gx + radial - 1, radial), gy)

    barrier = pltpu.get_barrier_semaphore()
    for other in (right, left, twin, x_next, x_prev):
        pl.semaphore_signal(barrier, inc=1, device_id=other, device_id_type=MESH)
    pl.semaphore_wait(barrier, 5)

    def piece(block, part):
        return grid_ref.at[block, pl.ds(DEPTH + part * half, half)]

    def low_rows(block):
        return grid_ref.at[block, pl.ds(0, DEPTH)]

    def high_rows(block):
        return grid_ref.at[block, pl.ds(DEPTH + rows, DEPTH)]

    def send_rows(block, part, source):
        if part == 0:
            edge = source.at[pl.ds(0, DEPTH)]
            return block, 0, copies.start(edge, high_rows(block), x_prev)
        edge = source.at[pl.ds(half - DEPTH, DEPTH)]
        return block, 1, copies.start(edge, low_rows(block), x_next)

    to_twin = []

    def pass_rows(sent):
        for block, part, copy in sent:
            copy.wait_recv()
            strip = high_rows(block) if part == 0 else low_rows(block)
            to_twin.append(copies.start(strip, strip, twin))

    own = [state_ref.at[pl.ds(0, half)], state_ref.at[pl.ds(half, half)]]
    keep = pltpu.make_async_copy(state_ref, grid_ref.at[gy, pl.ds(DEPTH, rows)], local_sem)

    flights = []
    order = [(0, 0), (1, 1), (0, 1), (1, 0)] if chips > 2 else [(0, 0), (1, 1)]
    for way, part in order:
        flights.append(
            (way, part, copies.start(own[part], piece(gy, part), right if way == 0 else left))
        )
    sent = [send_rows(gy, part, own[part]) for part in (0, 1)]
    for part in (0, 1):
        to_twin.append(copies.start(own[part], piece(gy, part), twin))
    keep.start()
    pass_rows(sent)
    for step in range(1, chips // 2 + 1):
        later, sent = [], []
        for way, part, copy in flights:
            block = at_chip(-step if way == 0 else step)
            copy.wait_recv()
            ref = piece(block, part)
            if 2 * (step + 1) < chips or (2 * (step + 1) == chips and part == way):
                later.append((way, part, copies.start(ref, ref, right if way == 0 else left)))
            to_twin.append(copies.start(ref, ref, twin))
            sent.append(send_rows(block, part, ref))
        pass_rows(sent)
        flights = later
    keep.wait()
    for copy in to_twin:
        copy.wait_recv()
    for copy in copies.made:
        copy.wait_send()


def row_sweep(load, first_row, last_row, drift_of, emit, unroll=4, base=0):
    def y_ahead(a):
        return pltpu.roll(a, a.shape[1] - 1, 1)

    def y_behind(a):
        return pltpu.roll(a, 1, 1)

    def z_ahead(a):
        return pltpu.roll(a, a.shape[0] - 1, 0)

    def z_behind(a):
        return pltpu.roll(a, 1, 0)

    def cells(by, bz):
        return 0.5 * (by + y_ahead(by)), 0.5 * (bz + z_ahead(bz))

    def radial_edges(prev, cur, prev_drift, cur_drift):
        sum_x = prev[1] + cur[1]
        sum_w = (prev[2] + prev_drift) + (cur[2] + cur_drift)
        sum_z = prev[3] + cur[3]
        bx, by, bz = cur[5], cur[6], cur[7]
        bx_y, bx_z = y_behind(bx), z_behind(bx)
        emf_z = 0.125 * (
            (sum_w + y_behind(sum_w)) * (bx + bx_y) - (sum_x + y_behind(sum_x)) * (by + prev[6])
        ) + resist * ((by - prev[6]) - (bx - bx_y))
        emf_y = 0.125 * (
            (sum_x + z_behind(sum_x)) * (bz + prev[7]) - (sum_z + z_behind(sum_z)) * (bx + bx_z)
        ) + resist * ((bx - bx_z) - (bz - prev[7]))
        return emf_z, emf_y

    start_prev, start_cur = load(first_row - 1), load(first_row)
    carry = (
        *cells(start_prev[6], start_prev[7]),
        *cells(start_cur[6], start_cur[7]),
        *radial_edges(start_prev, start_cur, drift_of(first_row - 1), drift_of(first_row)),
    )

    def one(row, carry):
        cy_prev, cz_prev, cy, cz, emf_z, emf_y = carry
        prev, cur, nxt = load(row - 1), load(row), load(row + 1)
        drift = drift_of(row)
        log_rho, vx, vy, vz, ent, bx, by, bz = cur
        w = vy + drift
        cy_next, cz_next = cells(nxt[6], nxt[7])
        emf_z_next, emf_y_next = radial_edges(cur, nxt, drift, drift_of(row + 1))

        half_x, half_w, half_z = 0.5 * vx, 0.5 * w, 0.5 * vz
        diffs, advs = [], []
        for f in range(5):
            a = cur[f]
            ya, yb, za, zb = y_ahead(a), y_behind(a), z_ahead(a), z_behind(a)
            dx, dy, dz = nxt[f] - prev[f], ya - yb, za - zb
            lap = ((nxt[f] + prev[f]) + (ya + yb) + (za + zb)) - 6.0 * a
            diffs.append((dx, dy, dz))
            advs.append(viscous * lap - (half_x * dx + half_w * dy + half_z * dz))

        sum_bx = bx + nxt[5]
        cx = 0.5 * sum_bx
        cur_x = 0.5 * ((y_ahead(cz) - y_behind(cz)) - (z_ahead(cy) - z_behind(cy)))
        cur_y = 0.5 * ((z_ahead(cx) - z_behind(cx)) - (cz_next - cz_prev))
        cur_z = 0.5 * ((cy_next - cy_prev) - (y_ahead(cx) - y_behind(cx)))
        inverse = jnp.exp(-log_rho)
        force_x = inverse * (cur_y * cz - cur_z * cy)
        force_y = inverse * (cur_z * cx - cur_x * cz)
        force_z = inverse * (cur_x * cy - cur_y * cx)

        pairs = [diffs[0][d] + diffs[4][d] for d in range(3)]
        rates = [
            advs[0] - 0.5 * (diffs[1][0] + diffs[2][1] + diffs[3][2]),
            advs[1] - (0.5 * sound_sq) * pairs[0] + force_x + (2.0 * rotation) * vy,
            advs[2] - (0.5 * sound_sq) * pairs[1] + force_y - ((2.0 - shear_rate) * rotation) * vx,
            advs[3] - (0.5 * sound_sq) * pairs[2] + force_z,
            advs[4] + resist * inverse * (cur_x * cur_x + cur_y * cur_y + cur_z * cur_z),
        ]

        w_y, z_y = w + y_behind(w), vz + y_behind(vz)
        bz_y, by_z = y_behind(bz), z_behind(by)
        emf_x = 0.125 * (
            (z_y + z_behind(z_y)) * (by + by_z) - (w_y + z_behind(w_y)) * (bz + bz_y)
        ) + resist * ((bz - bz_y) - (by - by_z))
        stretch = 0.25 * (sum_bx + y_behind(sum_bx))
        rates.append((z_ahead(emf_y) - emf_y) - (y_ahead(emf_z) - emf_z))
        rates.append(
            (emf_z_next - emf_z) - (z_ahead(emf_x) - emf_x) - (shear_rate * rotation) * stretch
        )
        rates.append((y_ahead(emf_x) - emf_x) - (emf_y_next - emf_y))
        emit(row, cur, rates)
        return cy, cz, cy_next, cz_next, emf_z_next, emf_y_next

    if last_row - first_row < 6:
        for row in range(first_row, last_row + 1):
            carry = one(row + base, carry)
        return
    lax.fori_loop(first_row, last_row + 1, one, carry, unroll=unroll)


def step_kernel(
    groups, radial, state_ref, table_ref, drift_ref, out_ref,
    grid_ref, moved_ref, first_ref, send, recv, local_sem,
):
    rows, fields, _, cols = state_ref.shape
    gather(state_ref, grid_ref, Copies(send, recv), local_sem, groups, radial)

    lane = lax.broadcasted_iota(jnp.int32, state_ref.shape[2:], 1)

    def turn(row, _):
        amount = table_ref[4, row]
        inside = lane < cols - amount
        low_side = lane < cols // 2
        blocks = [table_ref[k, row] for k in range(4)]
        for f in range(fields):
            before, here, after, beyond = [
                pltpu.roll(grid_ref[b, row, f], cols - amount, 1) for b in blocks
            ]
            moved_ref[row, f, :, :cols] = jnp.where(inside, here, after)
            moved_ref[row, f, :, cols:] = jnp.where(
                low_side, jnp.where(inside, after, beyond), jnp.where(inside, before, here)
            )
        return 0

    lax.fori_loop(0, rows + 2 * DEPTH, turn, 0)

    def drift_of(row):
        return drift_ref[row]

    def emit_first(row, cur, rates):
        for f in range(fields):
            first_ref[row, f] = cur[f] + time_step * rates[f]

    def emit_out(row, cur, rates):
        for f in range(fields):
            second = cur[f][:, :cols] + time_step * rates[f][:, :cols]
            out_ref[row - DEPTH, f] = 0.5 * (moved_ref[row, f, :, :cols] + second)

    def load_from(ref):
        return lambda row: [ref[row, f] for f in range(fields)]

    row_sweep(load_from(moved_ref), 1, rows + 2, drift_of, emit_first)
    row_sweep(load_from(first_ref), 2, rows + 1, drift_of, emit_out)


def gathered(state, residual, shift_rows, shear_offset):
    fields, vertical, rows, cols = state.shape
    groups, radial = lax.axis_size("gy"), lax.axis_size("gx")
    gx, gy = lax.axis_index("gx"), lax.axis_index("gy")
    cells_y = cols * groups
    wide = rows + 2 * DEPTH

    up = [(i, (i + 1) % radial) for i in range(radial)]
    down = [(target, source) for source, target in up]
    low = lax.ppermute(shift_rows[-DEPTH:], "gx", up)
    high = lax.ppermute(shift_rows[:DEPTH], "gx", down)
    offset = shear_offset[0]
    low = low - jnp.where(gx == 0, offset, 0)
    high = high + jnp.where(gx == radial - 1, offset, 0)
    amounts = jnp.concatenate([low, shift_rows, high])
    origin = (cols * gy - amounts) % cells_y
    block, part = origin // cols, origin % cols
    table = jnp.stack(
        [(block + groups - 1) % groups, block, (block + 1) % groups, (block + 2) % groups, part]
    )
    padded = jnp.concatenate([residual[-DEPTH:], residual, residual[:DEPTH]])
    drift = lax.dynamic_slice_in_dim(padded, gx * rows, wide)

    count = copy_count(groups // 2)
    out = pl.pallas_call(
        functools.partial(step_kernel, groups, radial),
        out_shape=jax.ShapeDtypeStruct((rows, fields, vertical, cols), jnp.float32),
        in_specs=[
            pl.BlockSpec(memory_space=pltpu.VMEM),
            pl.BlockSpec(memory_space=pltpu.SMEM),
            pl.BlockSpec(memory_space=pltpu.SMEM),
        ],
        out_specs=pl.BlockSpec(memory_space=pltpu.VMEM),
        scratch_shapes=[
            pltpu.VMEM((groups, wide, fields, vertical, cols), jnp.float32),
            pltpu.VMEM((wide, fields, vertical, 2 * cols), jnp.float32),
            pltpu.VMEM((wide, fields, vertical, 2 * cols), jnp.float32),
            pltpu.SemaphoreType.DMA((count,)),
            pltpu.SemaphoreType.DMA((count,)),
            pltpu.SemaphoreType.DMA,
        ],
        compiler_params=pltpu.CompilerParams(collective_id=0, has_side_effects=True),
    )(jnp.transpose(state, (2, 0, 1, 3)), table, drift)
    return jnp.transpose(out, (1, 2, 0, 3))


def spread_kernel(
    groups, radial, state_ref, shift_hbm, offset_hbm, residual_hbm, out_ref,
    shift_ref, offset_ref, residual_ref, taken_0, taken_1, taken_2, taken_3, turned_ref, edge_ref,
    shear_ref, moved_ref, own_edges, low_edges, high_edges, first_ref, windows_ref, drifts_ref, send, recv, local_sems,
):
    fields, vertical, rows, cols = state_ref.shape
    quarter = rows // 4
    taken = (taken_0, taken_1, taken_2, taken_3)
    late = late_rows(rows)
    others_start = WINDOW * len(late)
    short = [row for row in range(rows + DEPTH) if row not in late]
    lane_of = {row: WINDOW * k for k, row in enumerate(late)}
    lane_of.update({row: others_start + 4 * k for k, row in enumerate(short)})
    cells_y = cols * groups
    gx, gy = lax.axis_index("gx"), lax.axis_index("gy")
    x_next = (lax.rem(gx + 1, radial), gy)
    x_prev = (lax.rem(gx + radial - 1, radial), gy)
    others = [(gx, lax.rem(gy + k, groups)) for k in range(1, groups)]
    first_x, last_x = gx == 0, gx == radial - 1
    zero = gx // radial
    not_first, not_last = gx > 0, gx < radial - 1
    out_sent, back_sent, edges_sent, shear_sent, ends_sent, down_sent, up_sent = range(7)
    back_got = (4, 5, 6, 14, 15, 16)
    edges_got, shear_got, ends_got, rows_got, sides_got = 7, 8, 9, (10, 11), (12, 13)

    def remote(source, target, device, sent, got):
        return pltpu.make_async_remote_copy(
            src_ref=source,
            dst_ref=target,
            send_sem=send.at[sent],
            recv_sem=recv.at[got],
            device_id=device,
            device_id_type=MESH,
        )

    def spread_out(source, target, sent, got):
        for other in others:
            remote(source(other[1]), target, other, sent, got).start()
        pltpu.make_async_copy(source(gy), target, recv.at[got]).start()

    def arrived(ref, got):
        pltpu.make_async_copy(ref, ref, recv.at[got]).wait()

    def left(ref, sent):
        pltpu.make_async_copy(ref, ref, send.at[sent]).wait()

    small = [
        pltpu.make_async_copy(source, target, local_sems.at[k])
        for k, (source, target) in enumerate(
            ((shift_hbm, shift_ref), (offset_hbm, offset_ref), (residual_hbm, residual_ref))
        )
    ]
    for copy in small:
        copy.start()
    barrier = pltpu.get_barrier_semaphore()
    for other in (*others, x_prev, x_next):
        pl.semaphore_signal(barrier, inc=1, device_id=other, device_id_type=MESH)
    pl.semaphore_wait(barrier, groups + 1)

    def quarter_rows(q):
        return pl.ds(q * quarter, quarter)

    for pair in ((0, 3), (1, 2)):
        for other in [others[k - 1] for k in (2, 3, 4, 5, 6, 7, 1)]:
            for q in pair:
                remote(
                    state_ref.at[other[1], :, quarter_rows(q)], taken[q].at[gy], other, out_sent, q
                ).start()
        for q in pair:
            pltpu.make_async_copy(
                state_ref.at[gy, :, quarter_rows(q)], taken[q].at[gy], recv.at[q]
            ).start()

    lane = lax.broadcasted_iota(jnp.int32, (vertical, cols), 1)
    empty = [jnp.zeros((vertical, cols), jnp.float32)] * groups

    def displace(block_of, amount, slot, packed):
        whole, part = amount // cols, amount % cols
        rolled = [
            pltpu.roll(block_of(lax.rem(k - whole + groups, groups)), part, 1)
            for k in range(groups)
        ]
        row = [jnp.where(lane < part, rolled[d - 1], rolled[d]) for d in range(groups)]
        base, long = lane_of[slot], slot in late
        width = WINDOW if long else 4
        mine = (lane >= base) & (lane < base + width)
        result = []
        for d in range(groups):
            turned_ref[d, slot] = row[d]
            before, here, after = row[d - 1], row[d], row[(d + 1) % groups]
            if long:
                after = jnp.where(lane < cols // 2, after, here)
                before = jnp.where(lane < cols // 2, here, before)
            turn = base + 4
            edges = jnp.where(
                lane < base + width // 2,
                pltpu.roll(after, turn % cols if long else base, 1),
                pltpu.roll(before, (base + width - 4 if long else base + 4) % cols, 1),
            )
            result.append(jnp.where(mine, edges, packed[d]))
        return result

    def displace_quarter(q, packed):
        arrived(taken[q], q)
        for place in range(quarter):
            row = q * quarter + place
            packed = displace(
                lambda b: taken[q][b, :, place, :], shift_ref[row], row, packed
            )
        return packed

    def main_lanes(block, first_row, count):
        return moved_ref.at[block, pl.ds(first_row, count)]

    pieces = (
        (0, quarter),
        (3 * quarter, quarter),
        (quarter, EARLY[0]),
        (3 * quarter - EARLY[1], EARLY[1]),
        (late[0], len(late) // 2),
        (late[len(late) // 2], len(late) - len(late) // 2),
    )

    def send_back(piece):
        first, count = pieces[piece]
        if count:
            spread_out(
                lambda d: turned_ref.at[d, pl.ds(first, count)],
                main_lanes(gy, DEPTH + first, count),
                back_sent,
                back_got[piece],
            )

    def wait_back(piece):
        first, count = pieces[piece]
        if count:
            arrived(main_lanes(slice(None), DEPTH + first, count), back_got[piece])

    for copy in small:
        copy.wait()
    packed = displace_quarter(0, empty)
    packed = displace_quarter(3, packed)
    to_last = remote(turned_ref.at[:, pl.ds(0, DEPTH)], shear_ref, x_prev, ends_sent, ends_got)
    to_first = remote(
        turned_ref.at[:, pl.ds(rows - DEPTH, DEPTH)], shear_ref, x_next, ends_sent, ends_got
    )
    pl.when(first_x)(to_last.start)
    pl.when(last_x)(to_first.start)
    for piece in (0, 1):
        send_back(piece)

    low_row, high_row = 0, DEPTH + rows
    offset = offset_ref[0]
    for d in range(groups):
        edge_ref[d] = empty[0]

    def sheared(first_row, amount):
        arrived(shear_ref, ends_got)
        edges = empty
        for place in range(DEPTH):
            edges = displace(
                lambda b: shear_ref[b, place], amount, rows + place, edges
            )
        for d in range(groups):
            edge_ref[d] = edges[d]
        spread_out(
            lambda d: turned_ref.at[d, pl.ds(rows, DEPTH)],
            main_lanes(gy, first_row, DEPTH),
            shear_sent,
            shear_got,
        )

    @pl.when(first_x)
    def _():
        sheared(low_row, lax.rem(cells_y - offset, cells_y))

    @pl.when(last_x)
    def _():
        sheared(high_row, offset)

    packed = displace_quarter(1, packed)
    packed = displace_quarter(2, packed)
    for d in range(groups):
        edge_ref[d] = jnp.where(lane < lane_of[rows], packed[d], edge_ref[d])
    spread_out(lambda d: edge_ref.at[d], own_edges.at[gy], edges_sent, edges_got)
    for piece in (2, 3):
        send_back(piece)

    every = slice(None)
    for piece in (0, 1):
        wait_back(piece)
    rows_down = remote(
        main_lanes(every, DEPTH, DEPTH), main_lanes(every, high_row, DEPTH),
        x_prev, down_sent, rows_got[1],
    )
    rows_up = remote(
        main_lanes(every, rows, DEPTH), main_lanes(every, low_row, DEPTH),
        x_next, up_sent, rows_got[0],
    )
    edges_down = remote(own_edges, high_edges, x_prev, down_sent, sides_got[1])
    edges_up = remote(own_edges, low_edges, x_next, up_sent, sides_got[0])
    pl.when(not_first)(rows_down.start)
    pl.when(not_last)(rows_up.start)
    send_back(4)
    send_back(5)
    arrived(own_edges, edges_got)
    pl.when(not_first)(edges_down.start)
    pl.when(not_last)(edges_up.start)

    start = gx * rows - DEPTH + residual_ref.shape[0]

    def drift_of(row):
        return residual_ref[lax.rem(start + row, residual_ref.shape[0])]

    windows = cols // WINDOW
    kept = windows - 2 * DEPTH

    def emit_first(row, cur, rates):
        for f in range(fields):
            first_ref[row, f] = cur[f] + time_step * rates[f]

    def emit_whole(row, cur, rates):
        i = (row - DEPTH) // kept
        base = WINDOW * (row - i * kept)
        for f in range(fields):
            sides = windows_ref[i, f]
            low = pltpu.roll(sides, 2 * cols - base - 8, 1)
            high = pltpu.roll(sides, 2 * cols - base - 4, 1)
            total = moved_ref[f, row] + (cur[f] + time_step * rates[f])
            middle = jnp.where(lane >= cols - 2, high, total)
            out_ref[f, :, row - DEPTH, :] = jnp.where(lane < 2, low, middle)

    def stage_one(low, high):
        row_sweep(
            lambda row: [moved_ref[f, row] for f in range(fields)],
            DEPTH + low, DEPTH + high, drift_of, emit_first, 3, zero,
        )

    def stage_two(low, high):
        row_sweep(
            lambda row: [first_ref[row, f] for f in range(fields)],
            DEPTH + low, DEPTH + high, drift_of, emit_whole, 4, zero,
        )

    starts = range(-DEPTH, rows - DEPTH, kept)

    def in_window(k, low, high):
        return (lane >= WINDOW * k + low) & (lane < WINDOW * k + high)

    def rows_of(start):
        return range(start, min(start + windows, rows + DEPTH))

    def window_drift(start):
        total = empty[0]
        for k, row in enumerate(rows_of(start)):
            total = jnp.where(in_window(k, 0, WINDOW), drift_of(DEPTH + row), total)
        return total

    def fill_all(first_row, count, edges_ref, first_place):
        for i in range(len(starts)):
            held = [
                (k, row) for k, row in enumerate(rows_of(starts[i]))
                if first_row <= row < first_row + count and row not in late
            ]
            for f in range(fields):
                packed, value = edges_ref[f], windows_ref[i, f]
                for k, row in held:
                    base, from_lane = WINDOW * k, lane_of[first_place + row - first_row]
                    main = moved_ref[f, DEPTH + row]
                    for low, source, turn in (
                        (0, main, base + 4), (4, packed, base + 4 - from_lane), (8, main, base + 8)
                    ):
                        value = jnp.where(
                            in_window(k, low, low + 4), pltpu.roll(source, turn % cols, 1), value
                        )
                if held:
                    windows_ref[i, f] = value

    def fill_late():
        for i in range(len(starts)):
            held = [k for k, row in enumerate(rows_of(starts[i])) if row in late]
            if not held:
                continue
            from_lane = lane_of[starts[i] + held[0]]
            mine = (lane >= WINDOW * held[0]) & (lane < WINDOW * (held[-1] + 1))
            for f in range(fields):
                value = pltpu.roll(own_edges[f], (WINDOW * held[0] - from_lane) % cols, 1)
                windows_ref[i, f] = jnp.where(mine, value, windows_ref[i, f])

    def window_step(values, drift):
        turned = [
            [pltpu.roll(a, (WINDOW * (1 - r)) % cols, 1) for a in values] for r in range(3)
        ]
        drifts = [pltpu.roll(drift, (WINDOW * (1 - r)) % cols, 1) for r in range(3)]
        got = []
        row_sweep(
            lambda r: turned[r], 1, 1, lambda r: drifts[r],
            lambda r, cur, rates: got.extend(a + time_step * b for a, b in zip(cur, rates)),
        )
        return got

    def window_stages(i):
        drift = drifts_ref[i]
        moved = [windows_ref[i, f] for f in range(fields)]
        second = window_step(window_step(moved, drift), drift)
        for f in range(fields):
            windows_ref[i, f] = moved[f] + second[f]

    for i in range(len(starts)):
        drifts_ref[i] = window_drift(starts[i])
        for f in range(fields):
            windows_ref[i, f] = empty[0]
    fill_late()
    for piece in (2, 3):
        wait_back(piece)
    fill_all(0, rows, own_edges, 0)
    inside = [i for i in range(len(starts)) if starts[i] >= 0 and rows_of(starts[i])[-1] < rows]
    for i in inside:
        window_stages(i)
    stage_one(1, late[0] - 2)
    stage_one(late[-1] + 2, rows - 2)

    @pl.when(first_x)
    def _():
        arrived(main_lanes(every, low_row, DEPTH), shear_got)
        fill_all(-DEPTH, DEPTH, own_edges, rows)

    @pl.when(last_x)
    def _():
        arrived(main_lanes(every, high_row, DEPTH), shear_got)
        fill_all(rows, DEPTH, own_edges, rows)

    pl.when(not_first)(rows_up.wait_recv)
    pl.when(not_last)(rows_down.wait_recv)
    stage_one(-1, 0)
    stage_one(rows - 1, rows)

    @pl.when(not_first)
    def _():
        edges_up.wait_recv()
        fill_all(-DEPTH, DEPTH, low_edges, rows - DEPTH)

    @pl.when(not_last)
    def _():
        edges_down.wait_recv()
        fill_all(rows, DEPTH, high_edges, 0)

    for i in range(len(starts)):
        if i not in inside:
            window_stages(i)
    stage_two(0, late[0] - 3)
    stage_two(late[-1] + 3, rows - 1)
    wait_back(4)
    middle = late[len(late) // 2]
    stage_one(late[0] - 1, middle - 2)
    stage_two(late[0] - 2, middle - 3)
    wait_back(5)
    stage_one(middle - 1, late[-1] + 1)
    stage_two(middle - 2, late[-1] + 2)

    away = pl.ds(0, groups - 1)
    left(state_ref.at[away], out_sent)
    left(turned_ref.at[away, pl.ds(0, rows)], back_sent)
    left(edge_ref.at[away], edges_sent)

    @pl.when(first_x | last_x)
    def _():
        left(shear_ref, ends_sent)
        left(turned_ref.at[away, pl.ds(rows, DEPTH)], shear_sent)

    @pl.when(not_first)
    def _():
        rows_down.wait_send()
        edges_down.wait_send()

    @pl.when(not_last)
    def _():
        rows_up.wait_send()
        edges_up.wait_send()


def spread(state, residual, shift_rows, shear_offset):
    fields, vertical, rows, cols = state.shape
    groups, radial = lax.axis_size("gy"), lax.axis_size("gx")
    wide = rows + 2 * DEPTH
    parts = len(range(0, rows, cols // WINDOW - 2 * DEPTH))
    anywhere = pl.BlockSpec(memory_space=pl.ANY)
    vmem = pl.BlockSpec(memory_space=pltpu.VMEM)
    edges = pltpu.VMEM((groups, vertical, cols), jnp.float32)
    out = pl.pallas_call(
        functools.partial(spread_kernel, groups, radial),
        out_shape=pltpu.VMEM(state.shape, jnp.float32),
        in_specs=[anywhere] * 4,
        out_specs=vmem,
        scratch_shapes=[
            pltpu.SMEM(shift_rows.shape, jnp.int32),
            pltpu.SMEM(shear_offset.shape, jnp.int32),
            pltpu.SMEM(residual.shape, jnp.float32),
            *[pltpu.VMEM((groups, vertical, rows // 4, cols), jnp.float32)] * 4,
            pltpu.VMEM((groups, rows + DEPTH, vertical, cols), jnp.float32),
            edges,
            pltpu.VMEM((groups, DEPTH, vertical, cols), jnp.float32),
            pltpu.VMEM((fields, wide, vertical, cols), jnp.float32),
            edges,
            edges,
            edges,
            pltpu.VMEM((wide, fields, vertical, cols), jnp.float32),
            pltpu.VMEM((parts, fields, vertical, cols), jnp.float32),
            pltpu.VMEM((parts, vertical, cols), jnp.float32),
            pltpu.SemaphoreType.DMA((7,)),
            pltpu.SemaphoreType.DMA((17,)),
            pltpu.SemaphoreType.DMA((3,)),
        ],
        compiler_params=pltpu.CompilerParams(collective_id=1, has_side_effects=True),
    )(state, shift_rows, shear_offset, residual)
    return 0.5 * out


def local(state, residual, shift_rows, shear_offset):
    fields, _, rows, cols = state.shape
    paired = lax.axis_size("gy") == fields and lax.axis_size("gx") > 2
    late = len(late_rows(rows))
    if paired and rows % 16 == 0 and WINDOW * late + 4 * (rows + DEPTH - late) <= cols:
        return spread(state, residual, shift_rows, shear_offset)
    return gathered(state, residual, shift_rows, shear_offset)


def solution(mesh):
    return jax.shard_map(
        local,
        mesh=mesh,
        in_specs=(P(None, None, "gx", "gy"), P(), P("gx"), P()),
        out_specs=P(None, None, "gx", "gy"),
        check_vma=False,
    )
```
